32 devices in a mesh: seq: 8 (over y, x, core), fsdp: 4 (over z).
Axes of the slice: x: 2, y: 2, z: 4, core: 2. Of those that a mesh axis runs over, the one named last changes fastest.
Arguments:
- block_input: float32 [4, 1024, 1024], P('fsdp', 'seq'), may hold values from -6 to 6
- attn_gain: bfloat16 [1024], P('fsdp'), may hold values from 0.099609375 to 1.8984375
- query_weight: bfloat16 [1024, 512], P('fsdp'), may hold values from -0.1875 to 0.1875
- key_weight: bfloat16 [1024, 512], P('fsdp'), may hold values from -0.1875 to 0.1875
- value_weight: bfloat16 [1024, 1024], P('fsdp'), may hold values from -0.1875 to 0.1875
- gate_weight: bfloat16 [1024, 1024], P('fsdp'), may hold values from -0.1875 to 0.1875
- decay_down: bfloat16 [1024, 16], P('fsdp'), may hold values from -0.1875 to 0.1875
- decay_up: bfloat16 [16, 512], P(None, 'fsdp'), may hold values from -1.5 to 1.5
- decay_bias: bfloat16 [512], P('fsdp'), may hold values from -0.5 to 11
- head_gain: bfloat16 [256], P('fsdp'), may hold values from 0.099609375 to 1.8984375
- out_weight: bfloat16 [1024, 1024], P('fsdp'), may hold values from -0.375 to 0.375
- ffn_gain: bfloat16 [1024], P('fsdp'), may hold values from 0.099609375 to 1.8984375
- ffn_gate: bfloat16 [1024, 2816], P('fsdp'), may hold values from -0.1875 to 0.1875
- ffn_up: bfloat16 [1024, 2816], P('fsdp'), may hold values from -0.1875 to 0.1875
- ffn_down: bfloat16 [2816, 1024], P(None, 'fsdp'), may hold values from -0.21875 to 0.21875
- cotangent: float32 [4, 1024, 1024], P('fsdp', 'seq'), may hold values from -6 to 6
Outputs:
- block_output: float32 [4, 1024, 1024], P('fsdp', 'seq')
- input_grad: float32 [4, 1024, 1024], P('fsdp', 'seq')
- grad_attn_gain: float32 [1024], P(('seq', 'fsdp'))
- grad_query: float32 [1024, 512], P(('seq', 'fsdp'))
- grad_key: float32 [1024, 512], P(('seq', 'fsdp'))
- grad_value: float32 [1024, 1024], P(('seq', 'fsdp'))
- grad_gate: float32 [1024, 1024], P(('seq', 'fsdp'))
- grad_decay_down: float32 [1024, 16], P(('seq', 'fsdp'))
- grad_decay_up: float32 [16, 512], P(None, ('seq', 'fsdp'))
- grad_decay_bias: float32 [512], P(('seq', 'fsdp'))
- grad_head_gain: float32 [256], P(('seq', 'fsdp'))
- grad_out: float32 [1024, 1024], P(('seq', 'fsdp'))
- grad_ffn_gain: float32 [1024], P(('seq', 'fsdp'))
- grad_ffn_gate: float32 [1024, 2816], P(('seq', 'fsdp'))
- grad_ffn_up: float32 [1024, 2816], P(('seq', 'fsdp'))
- grad_ffn_down: float32 [2816, 1024], P(None, ('seq', 'fsdp'))
The draws below stay inside these ranges and needn't reach their ends.
All inputs are finite; a program needn't handle non-finite values.
Results may differ from the reference program's by a relative error of at most 0.039.
Values may be sent and summed in bfloat16 or wider, within the bound.
A program may use at most 192 MiB of HBM per device.

```python
import jax
import jax.numpy as jnp
from jax import lax

D = 1024
H = 4
HK = 128
HV = 256
R = 16
FF = 2816
BLOCK = 64
KD = 512
VD = 1024
SEQS = 4
LEN = 1024


def draw_decay_bias(key, part):
    pick_key, slow_key, fast_key, place_key = jax.random.split(jax.random.fold_in(key, 17), 4)
    keep_share = 0.5
    slow_mask = jax.random.bernoulli(pick_key, keep_share, (KD,))
    log_length = jnp.log(jnp.float32(LEN))
    slow_value = log_length + jax.random.uniform(slow_key, (KD,), jnp.float32, -2.5, 0.5)
    fast_value = jax.random.uniform(fast_key, (KD,), jnp.float32, -0.5, 1.5)
    values = jnp.where(slow_mask, slow_value, fast_value)
    order = jax.random.permutation(place_key, KD)
    values = values.at[order[0]].set(11.0)
    values = values.at[order[1]].set(-0.5)
    return values.astype(jnp.bfloat16)


def strengthened(array, stream_key, source, target, shards_of, factor):
    def block_of(axis_at):
        return (jnp.arange(array.shape[axis_at]) // (array.shape[axis_at] // shards_of)).reshape((-1,) + (1,) * (array.ndim - 1 - axis_at))

    one_side = jax.random.permutation(stream_key, shards_of)[block_of(target)]
    far = (block_of(target) + shards_of // 2) % shards_of
    return jnp.where((block_of(source) == one_side) | (block_of(source) == far), factor * array, array)


def level_of(stream_key, shape, cuts, smallest, top_value):
    factor_of, own = 1.0, jax.random.fold_in(stream_key, 6)
    for axis_at, parts in cuts:
        draws = jnp.exp(jax.random.uniform(jax.random.fold_in(own, axis_at), (parts,), jnp.float32, smallest / len(cuts), top_value / len(cuts)))
        factor_of = factor_of * jnp.repeat(draws, shape[axis_at] // parts).reshape([-1 if axis == axis_at else 1 for axis in range(len(shape))])
    return factor_of


def gaussian(key, dims, deviation, most, cuts=(), held_as=jnp.bfloat16):
    loudness = level_of(key, dims, cuts, -0.22, 0.18) if cuts else 1.0
    drawn = jax.random.normal(key, dims, jnp.float32) * deviation * loudness
    return jnp.minimum(jnp.maximum(drawn, -most), most).astype(held_as)


def noise_with(key, shape, width, bound, cuts, heavy, kind=jnp.bfloat16):
    values = width * jax.random.normal(key, shape, jnp.float32)
    if cuts:
        values = values * level_of(key, shape, cuts, -0.22, 0.18)
    return jnp.clip(strengthened(values, jax.random.fold_in(key, 3), *heavy), -bound, bound).astype(kind)


def setup_inputs(seed: int = 0) -> dict:
    key_of = jax.random.split(jax.random.key(seed), 17)
    return {
        "block_input": gaussian(key_of[0], (SEQS, LEN, D), 1.0, 6.0, ((0, 4), (1, 8)), jnp.float32),
        "attn_gain": jnp.clip(1.0 + 0.18 * jax.random.normal(key_of[1], (D,), jnp.float32), 0.099609375, 1.8984375).astype(jnp.bfloat16),
        "query_weight": gaussian(key_of[2], (D, KD), D ** -0.5, 0.1875, ((0, 4),)),
        "key_weight": gaussian(key_of[3], (D, KD), D ** -0.5, 0.1875, ((0, 4),)),
        "value_weight": gaussian(key_of[4], (D, VD), D ** -0.5, 0.1875, ((0, 4),)),
        "gate_weight": gaussian(key_of[5], (D, VD), D ** -0.5, 0.1875, ((0, 4),)),
        "decay_down": gaussian(key_of[6], (D, R), D ** -0.5, 0.1875, ((0, 4),)),
        "decay_up": gaussian(key_of[7], (R, KD), R ** -0.5, 1.5, ((1, 4),)),
        "decay_bias": draw_decay_bias(jax.random.fold_in(key_of[16], 71), 0),
        "head_gain": jnp.clip(1.0 + 0.18 * jax.random.normal(key_of[9], (HV,), jnp.float32), 0.099609375, 1.8984375).astype(jnp.bfloat16),
        "out_weight": gaussian(key_of[10], (VD, D), (VD // 4) ** -0.5, 0.375, ((0, 4),)),
        "ffn_gain": jnp.clip(1.0 + 0.18 * jax.random.normal(key_of[11], (D,), jnp.float32), 0.099609375, 1.8984375).astype(jnp.bfloat16),
        "ffn_gate": gaussian(key_of[12], (D, FF), D ** -0.5, 0.1875, ((0, 4),)),
        "ffn_up": gaussian(key_of[13], (D, FF), D ** -0.5, 0.1875, ((0, 4),)),
        "ffn_down": gaussian(key_of[14], (FF, D), (FF // 4) ** -0.5, 0.21875, ((1, 4),)),
        "cotangent": noise_with(key_of[15], (SEQS, LEN, D), 1.0, 6.0, ((0, 4), (1, 8)), (1, 2, 8, 2.0), jnp.float32),
    }


norm_eps = 1e-06
logit_norm = 16.0
highest_precision = lax.Precision.HIGHEST

def product(left, right):
    return jnp.dot(left, right, preferred_element_type=jnp.float32)

def transposed(left, right):
    return jnp.dot(left.T, right, preferred_element_type=jnp.float32)

def rms_gain(token_rows, gain_row):
    return token_rows * lax.rsqrt(lax.optimization_barrier(jnp.mean(token_rows * token_rows, axis=-1, keepdims=True)) + norm_eps) * gain_row

def gated_norm(attended, gate_pre, head_gain):
    head_rows = attended.reshape(attended.shape[0], H, HV)
    gate_acts = jax.nn.silu(gate_pre.reshape(head_rows.shape))
    return (rms_gain(head_rows, head_gain) * gate_acts).reshape(attended.shape[0], H * HV)

def swiglu(gate_part, up_part):
    return jax.nn.silu(gate_part) * up_part

def block_scan(queries, key_rows, value_rows, log_decay):
    length = queries.shape[0]
    blocks = length // BLOCK
    key_scaling_factor = HK ** (-0.5)
    lower_mask = jnp.arange(BLOCK)[:, None] >= jnp.arange(BLOCK)[None, :]

    def advance(carried_state, pieces):
        query_part, key_part, value_portion, decay_part = pieces
        running = jnp.cumsum(decay_part, axis=0)
        block_count_total = running[-1]
        query_decayed = query_part * jnp.exp(running)
        key_dec = key_part * jnp.exp(-running)
        key_final_decay = key_part * jnp.exp(block_count_total[None] - running)
        scores = jnp.einsum('thk,shk->hts', query_decayed, key_dec, precision=highest_precision)
        scores = jnp.where(lower_mask[None], scores, 0.0)
        output_rows = jnp.einsum('hts,shv->thv', scores, value_portion, precision=highest_precision)
        output_rows = output_rows + jnp.einsum('qse,seg->qsg', query_decayed, carried_state, precision=highest_precision)
        carried_state = jnp.exp(block_count_total)[:, :, None] * carried_state + jnp.einsum('ufn,ufm->fnm', key_final_decay, value_portion, precision=highest_precision)
        return (carried_state, output_rows * key_scaling_factor)
    pieces = (queries.reshape(blocks, BLOCK, H, HK), key_rows.reshape(blocks, BLOCK, H, HK), value_rows.reshape(blocks, BLOCK, H, HV), log_decay.reshape(blocks, BLOCK, H, HK))
    zero_state = jnp.zeros((H, HK, HV), queries.dtype)
    carried_state, output_rows = lax.scan(advance, zero_state, pieces)
    return (output_rows.reshape(length, H * HV), carried_state)

def sequence_pass(token_rows, cot_rows, attn_params, ffn_params):
    attn_gain, query_weight, key_weight, value_weight, gate_weight, decay_down, decay_up, decay_bias, head_gain, out_weight = attn_params
    ffn_gain, ffn_gate, ffn_up, ffn_down = ffn_params
    normed_one, norm_one_back = jax.vjp(rms_gain, token_rows, attn_gain.astype(jnp.float32))
    hidden_one = normed_one.astype(jnp.bfloat16)
    queries = product(hidden_one, query_weight).astype(jnp.bfloat16)
    key_rows = product(hidden_one, key_weight).astype(jnp.bfloat16)
    value_rows = product(hidden_one, value_weight).astype(jnp.bfloat16)
    gate_pre = product(hidden_one, gate_weight)
    low_rank = product(hidden_one, decay_down).astype(jnp.bfloat16)
    logits = product(low_rank, decay_up) + decay_bias.astype(jnp.float32)
    log_decay = jax.nn.log_sigmoid(logits) / logit_norm
    attended, scan_back, final_state = jax.vjp(block_scan, queries.astype(jnp.float32), key_rows.astype(jnp.float32), value_rows.astype(jnp.float32), log_decay, has_aux=True)
    gated, gated_back = jax.vjp(gated_norm, attended, gate_pre, head_gain.astype(jnp.float32))
    gated_low = gated.astype(jnp.bfloat16)
    residual = token_rows + product(gated_low, out_weight)
    normed_two, norm_two_back = jax.vjp(rms_gain, residual, ffn_gain.astype(jnp.float32))
    hidden_two = normed_two.astype(jnp.bfloat16)
    ffn_gate_pre = product(hidden_two, ffn_gate)
    ffn_up_pre = product(hidden_two, ffn_up)
    mixed, mixed_back = jax.vjp(swiglu, ffn_gate_pre, ffn_up_pre)
    mixed_low = mixed.astype(jnp.bfloat16)
    block_output = residual + product(mixed_low, ffn_down)
    cot_low = cot_rows.astype(jnp.bfloat16)
    grad_ffn_down = transposed(mixed_low, cot_low)
    d_gate_part, d_up_part = mixed_back(product(cot_low, ffn_down.T))
    d_gate_low = d_gate_part.astype(jnp.bfloat16)
    d_up_low = d_up_part.astype(jnp.bfloat16)
    grad_ffn_gate = transposed(hidden_two, d_gate_low)
    grad_ffn_up = transposed(hidden_two, d_up_low)
    d_hidden_two = product(d_gate_low, ffn_gate.T) + product(d_up_low, ffn_up.T)
    d_residual_norm, grad_ffn_gain = norm_two_back(d_hidden_two)
    d_residual = cot_rows + d_residual_norm
    d_res_low = d_residual.astype(jnp.bfloat16)
    grad_out = transposed(gated_low, d_res_low)
    d_attended, d_gate_pre, grad_head_gain = gated_back(product(d_res_low, out_weight.T))
    d_queries, d_keys, d_values, d_log_decay = scan_back(d_attended)
    d_logits = d_log_decay * jax.nn.sigmoid(-logits) / logit_norm
    grad_decay_bias = lax.optimization_barrier(jnp.sum(d_logits, axis=0))
    d_logits_low = d_logits.astype(jnp.bfloat16)
    grad_decay_up = transposed(low_rank, d_logits_low)
    d_low_rank = product(d_logits_low, decay_up.T).astype(jnp.bfloat16)
    grad_decay_down = transposed(hidden_one, d_low_rank)
    d_query_low = d_queries.astype(jnp.bfloat16)
    d_key_low = d_keys.astype(jnp.bfloat16)
    d_value_low = d_values.astype(jnp.bfloat16)
    d_gate_one = d_gate_pre.astype(jnp.bfloat16)
    grad_query = transposed(hidden_one, d_query_low)
    grad_key = transposed(hidden_one, d_key_low)
    grad_value = transposed(hidden_one, d_value_low)
    grad_gate = transposed(hidden_one, d_gate_one)
    d_hidden_one = product(d_query_low, query_weight.T) + product(d_key_low, key_weight.T) + product(d_value_low, value_weight.T) + product(d_gate_one, gate_weight.T) + product(d_low_rank, decay_down.T)
    d_input_norm, grad_attn_gain = norm_one_back(d_hidden_one)
    input_grad = d_residual + d_input_norm
    attn_grads = (grad_attn_gain, grad_query, grad_key, grad_value, grad_gate, grad_decay_down, grad_decay_up, grad_decay_bias, grad_head_gain, grad_out)
    ffn_grads = (grad_ffn_gain, grad_ffn_gate, grad_ffn_up, grad_ffn_down)
    return (block_output, input_grad, attn_grads, ffn_grads)

def reference(block_input, attn_gain, query_weight, key_weight, value_weight, gate_weight, decay_down, decay_up, decay_bias, head_gain, out_weight, ffn_gain, ffn_gate, ffn_up, ffn_down, cotangent):
    attn_params = (attn_gain, query_weight, key_weight, value_weight, gate_weight, decay_down, decay_up, decay_bias, head_gain, out_weight)
    ffn_params = (ffn_gain, ffn_gate, ffn_up, ffn_down)
    output_list = []
    input_list = []
    attn_total = None
    ffn_total = None
    for seq_index in range(SEQS):
        block_output, input_grad, attn_grads, ffn_grads = sequence_pass(block_input[seq_index], cotangent[seq_index], attn_params, ffn_params)
        output_list.append(block_output)
        input_list.append(input_grad)
        if attn_total is None:
            attn_total = attn_grads
            ffn_total = ffn_grads
        else:
            attn_total = jax.tree.map(jnp.add, attn_total, attn_grads)
            ffn_total = jax.tree.map(jnp.add, ffn_total, ffn_grads)
    grad_attn_gain, grad_query, grad_key, grad_value, grad_gate, grad_decay_down, grad_decay_up, grad_decay_bias, grad_head_gain, grad_out = attn_total
    grad_ffn_gain, grad_ffn_gate, grad_ffn_up, grad_ffn_down = ffn_total
    return (jnp.stack(output_list), jnp.stack(input_list), grad_attn_gain, grad_query, grad_key, grad_value, grad_gate, grad_decay_down, grad_decay_up, grad_decay_bias, grad_head_gain, grad_out, grad_ffn_gain, grad_ffn_gate, grad_ffn_up, grad_ffn_down)
```

```python
import functools

import jax
import jax.numpy as jnp
from jax import lax
from jax.experimental import pallas as pl
from jax.experimental.pallas import tpu as pltpu
from jax.sharding import PartitionSpec as P

HK = 128
HV = 256
BLOCK = 64


norm_eps = 1e-06
logit_norm = 16.0
exact = lax.Precision.HIGHEST
fine = lax.Precision.HIGH
low = jnp.bfloat16
wide = jnp.float32


def product(left, right):
    return jnp.dot(left, right, preferred_element_type=wide)


def transposed(left, right):
    return lax.dot_general(left, right, (((0,), (0,)), ((), ())), preferred_element_type=wide)


def against(left, right):
    return lax.dot_general(left, right, (((1,), (1,)), ((), ())), preferred_element_type=wide)


def fine_dot(spec, left, right):
    return jnp.einsum(spec, left, right, precision=fine, preferred_element_type=wide)


def rms_gain(token_rows, gain_row):
    return (
        token_rows
        * lax.rsqrt(jnp.mean(token_rows * token_rows, axis=-1, keepdims=True) + norm_eps)
        * gain_row
    )


def gated_norm(attended, gate_pre, head_gain):
    return rms_gain(attended, head_gain) * jax.nn.silu(gate_pre)


def swiglu(gate_part, up_part):
    return jax.nn.silu(gate_part) * up_part


def exchange(pieces):
    return lax.all_to_all(pieces, "fsdp", 0, 0)


def gather_rows(rows):
    return lax.all_gather(rows, "fsdp", axis=0, tiled=True)


def scatter_rows(rows):
    return lax.psum_scatter(rows.astype(low), "fsdp", scatter_dimension=0, tiled=True).astype(wide)


def summed_rows(grads):
    return lax.psum_scatter(grads.astype(low), "seq", scatter_dimension=0, tiled=True)


def owned_columns(section, parts):
    return exchange(section.reshape(parts, section.shape[0] // parts, -1))


def across(pieces):
    rows = pieces.shape[1]
    return pieces.transpose(1, 0, 2).reshape(rows, -1).astype(wide)


def spread(
    block_input,
    attn_gain,
    query_weight,
    key_weight,
    value_weight,
    gate_weight,
    decay_down,
    decay_up,
    decay_bias,
    head_gain,
    out_weight,
    ffn_gain,
    ffn_gate,
    ffn_up,
    ffn_down,
    cotangent,
):
    shards, parts = lax.axis_size("seq"), lax.axis_size("fsdp")
    si = lax.axis_index("seq")
    x = block_input[0]
    cot_rows = cotangent[0]
    length, width = x.shape
    blocks = length // BLOCK
    scale = HK ** (-0.5)

    small = jnp.concatenate([attn_gain, ffn_gain, head_gain, decay_down.reshape(-1)])
    small = exchange(jnp.broadcast_to(small[None], (parts, small.shape[0])))
    own = attn_gain.shape[0]
    own_head = head_gain.shape[0]
    gain_one = small[:, :own].reshape(-1).astype(wide)
    gain_two = small[:, own : 2 * own].reshape(-1).astype(wide)
    gain_head = small[:, 2 * own : 2 * own + own_head].reshape(-1).astype(wide)
    down_full = small[:, 2 * own + own_head :].reshape(width, -1)
    rank = down_full.shape[1]

    normed_one, norm_one_back = jax.vjp(rms_gain, x, gain_one)
    both = gather_rows(jnp.concatenate([normed_one.astype(low), cot_rows.astype(low)], axis=1))
    hidden_one = both[:, :width]
    cot_low = both[:, width:]
    ff = ffn_gate.shape[1] // parts
    rows = own // shards
    down_rows = ff // shards
    cuts = [
        lax.dynamic_slice_in_dim(w, si * rows, rows, 0).reshape(rows, parts, -1).transpose(1, 0, 2)
        for w in (query_weight, key_weight, value_weight, gate_weight, ffn_gate, ffn_up)
    ]
    cuts.append(
        lax.dynamic_slice_in_dim(
            ffn_down.reshape(parts, ff, own), si * down_rows, down_rows, 1
        ).reshape(parts, rows, -1)
    )
    got = lax.all_gather(exchange(jnp.concatenate(cuts, axis=2)), "seq")
    attn_columns = 2 * HK + 2 * HV
    attn_w = got[..., :attn_columns].transpose(1, 0, 2, 3).reshape(width, -1)
    ffn_w = (
        got[..., attn_columns : attn_columns + 2 * ff].transpose(1, 0, 2, 3).reshape(width, -1)
    )
    down_w = (
        got[..., attn_columns + 2 * ff :]
        .reshape(shards, parts, down_rows, own)
        .transpose(0, 2, 1, 3)
        .reshape(ff, width)
    )

    projected = product(hidden_one, attn_w)
    rounded = projected[:, : 2 * HK + HV].astype(low)
    gate_pre = projected[:, 2 * HK + HV :]
    low_rank = product(hidden_one, down_full).astype(low)
    logits = product(low_rank, decay_up) + decay_bias.astype(wide)
    log_decay = jax.nn.log_sigmoid(logits) / logit_norm

    def chunked(rows):
        return rows.reshape(parts * blocks, BLOCK, -1)

    q = chunked(rounded[:, :HK].astype(wide))
    k = chunked(rounded[:, HK : 2 * HK].astype(wide))
    v = chunked(rounded[:, 2 * HK :].astype(wide))
    place = jnp.arange(BLOCK)
    lower = place[:, None] >= place[None, :]
    ones_lower = lower.astype(wide)
    running = jnp.einsum("ts,bsk->btk", ones_lower, chunked(log_decay), precision=exact)
    total = running[:, -1]
    grown = jnp.exp(running)
    shrunk = jnp.exp(-running)
    to_end = jnp.exp(total[:, None] - running)
    qd = q * grown
    kd = k * shrunk
    kf = k * to_end
    scores = jnp.where(lower[None], fine_dot("btk,bsk->bts", qd, kd), 0.0)
    intra = fine_dot("bts,bsv->btv", scores, v)
    added = fine_dot("bsk,bsv->bkv", kf, v)
    added_c = added.reshape(parts, blocks, HK, HV)
    total_c = total.reshape(parts, blocks, HK)
    factor_c = jnp.exp(total_c)[..., None]
    local_state = added_c[:, 0]
    for c in range(1, blocks):
        local_state = factor_c[:, c] * local_state + added_c[:, c]
    totals = lax.all_gather(jnp.sum(total_c, axis=1), "seq")
    states = lax.all_gather(local_state.astype(low), "seq")
    index = jnp.arange(shards)
    upto = jnp.cumsum(totals, axis=0)
    mine_upto = lax.dynamic_index_in_dim(upto, si, 0, False)
    mine_total = lax.dynamic_index_in_dim(totals, si, 0, False)
    before = (index < si)[:, None, None]
    after = (index > si)[:, None, None]
    early = jnp.where(before, jnp.exp(jnp.where(before, mine_upto - mine_total - upto, 0.0)), 0.0)
    late = jnp.where(
        after, jnp.exp(jnp.where(after, upto - totals - mine_upto, 0.0)), 0.0
    )
    incoming = jnp.sum(early[..., None] * states.astype(wide), axis=0)
    entering = [incoming]
    for c in range(blocks):
        entering.append(factor_c[:, c] * entering[-1] + added_c[:, c])
    state_in = jnp.stack(entering[:-1], axis=1).reshape(parts * blocks, HK, HV)
    state_out = jnp.stack(entering[1:], axis=1).reshape(parts * blocks, HK, HV)
    attended = scale * (intra + fine_dot("btk,bkv->btv", qd, state_in))
    attended = attended.reshape(parts * length, HV)

    gated, gated_back = jax.vjp(gated_norm, attended, gate_pre, gain_head)
    gated_low = gated.astype(low)
    residual = x + scatter_rows(product(gated_low, out_weight))
    normed_two, norm_two_back = jax.vjp(rms_gain, residual, gain_two)
    hidden_two = gather_rows(normed_two.astype(low))
    pre = product(hidden_two, ffn_w)
    mixed, mixed_back = jax.vjp(swiglu, pre[:, :ff], pre[:, ff:])
    mixed_low = mixed.astype(low)
    d_gate_part, d_up_part = mixed_back(against(cot_low, down_w))
    d_pre = jnp.concatenate([d_gate_part.astype(low), d_up_part.astype(low)], axis=1)
    both = scatter_rows(
        jnp.concatenate(
            [against(d_pre, ffn_w).astype(low), product(mixed_low, down_w).astype(low)], axis=1
        )
    )
    d_residual_norm, grad_ffn_gain = norm_two_back(both[:, :width])
    d_residual = cot_rows + d_residual_norm
    d_res_low = gather_rows(d_residual.astype(low))
    block_output = residual + both[:, width:]
    ffn_section = summed_rows(
        jnp.concatenate(
            [transposed(hidden_two, d_pre).astype(low), transposed(cot_low, mixed_low).astype(low)],
            axis=1,
        )
    )
    ffn_owned = owned_columns(ffn_section, parts)

    d_attended, d_gate_pre, grad_head_gain = gated_back(against(d_res_low, out_weight))
    d_out = chunked(scale * d_attended)
    pulled = fine_dot("btk,btv->bkv", qd, d_out)
    pulled_c = pulled.reshape(parts, blocks, HK, HV)
    local_pull = pulled_c[:, blocks - 1]
    for c in range(blocks - 2, -1, -1):
        local_pull = factor_c[:, c] * local_pull + pulled_c[:, c]
    pulls = lax.all_gather(local_pull.astype(low), "seq")
    later = jnp.sum(late[..., None] * pulls.astype(wide), axis=0)
    leaving = [later]
    for c in range(blocks - 1, 0, -1):
        leaving.insert(0, factor_c[:, c] * leaving[0] + pulled_c[:, c])
    d_state = jnp.stack(leaving, axis=1).reshape(parts * blocks, HK, HV)
    d_scores = jnp.where(lower[None], fine_dot("btv,bsv->bts", d_out, v), 0.0)
    d_q = grown * (
        fine_dot("bts,bsk->btk", d_scores, kd) + fine_dot("btv,bkv->btk", d_out, state_in)
    )
    d_k = shrunk * fine_dot("bts,btk->bsk", d_scores, qd) + to_end * fine_dot(
        "bsv,bkv->bsk", v, d_state
    )
    d_v = fine_dot("bts,btv->bsv", scores, d_out) + fine_dot("bsk,bkv->bsv", kf, d_state)
    tail_term = jnp.sum(d_state * state_out, axis=2)
    d_log_decay = (
        jnp.einsum("st,bsk->btk", ones_lower, q * d_q - k * d_k, precision=exact)
        + tail_term[:, None]
    )
    d_logits = d_log_decay.reshape(parts * length, HK) * jax.nn.sigmoid(-logits) / logit_norm
    grad_decay_bias = jnp.sum(d_logits, axis=0)
    d_logits_low = d_logits.astype(low)
    grad_decay_up = transposed(low_rank, d_logits_low)
    d_low_rank = against(d_logits_low, decay_up).astype(low)
    grad_decay_down = transposed(hidden_one, d_low_rank)
    d_projected = jnp.concatenate(
        [
            d_q.reshape(parts * length, HK).astype(low),
            d_k.reshape(parts * length, HK).astype(low),
            d_v.reshape(parts * length, HV).astype(low),
            d_gate_pre.astype(low),
        ],
        axis=1,
    )
    d_hidden_one = scatter_rows(against(d_projected, attn_w) + against(d_low_rank, down_full))
    d_input_norm, grad_attn_gain = norm_one_back(d_hidden_one)
    input_grad = d_residual + d_input_norm
    devices = shards * parts
    grad_out = transposed(gated_low, d_res_low).astype(low)
    attn_section = summed_rows(
        jnp.concatenate(
            [transposed(hidden_one, d_projected).astype(low), grad_out.reshape(width, HV)], axis=1
        )
    )
    attn_owned = owned_columns(attn_section[:, :attn_columns], parts)
    turned = [(s * parts + f, f * shards + s) for s in range(shards) for f in range(parts)]
    own_out = lax.ppermute(
        attn_section[:, attn_columns:].reshape(-1, width), ("seq", "fsdp"), turned
    ).astype(wide)
    head_part = jnp.concatenate(
        [
            grad_decay_up.reshape(rank, shards, -1).transpose(1, 0, 2).reshape(shards, -1),
            grad_decay_bias.reshape(shards, -1),
        ],
        axis=1,
    )
    mine = jnp.arange(parts)[:, None, None] == lax.axis_index("fsdp")
    head_part = jnp.where(mine, head_part[None], 0.0).reshape(devices, -1)
    own_bias_size = HK // shards
    summed = jnp.concatenate(
        [
            grad_attn_gain.reshape(devices, -1),
            grad_ffn_gain.reshape(devices, -1),
            grad_head_gain.reshape(devices, -1),
            grad_decay_down.reshape(devices, -1),
            head_part,
        ],
        axis=1,
    )
    summed = jnp.sum(lax.all_to_all(summed, ("seq", "fsdp"), 0, 0), axis=0)
    each = width // devices
    each_head = HV // devices
    own_attn_gain = summed[:each]
    own_ffn_gain = summed[each : 2 * each]
    own_head_gain = summed[2 * each : 2 * each + each_head]
    at_up = 2 * each + each_head + each * rank
    at_bias = at_up + rank * own_bias_size
    own_down = summed[2 * each + each_head : at_up].reshape(each, rank)
    own_up = summed[at_up:at_bias].reshape(rank, own_bias_size)
    own_bias = summed[at_bias:]
    return (
        block_output[None],
        input_grad[None],
        own_attn_gain,
        across(attn_owned[:, :, :HK]),
        across(attn_owned[:, :, HK : 2 * HK]),
        across(attn_owned[:, :, 2 * HK : 2 * HK + HV]),
        across(attn_owned[:, :, 2 * HK + HV :]),
        own_down,
        own_up,
        own_bias,
        own_head_gain,
        own_out,
        own_ffn_gain,
        across(ffn_owned[:, :, :ff]),
        across(ffn_owned[:, :, ff : 2 * ff]),
        across(ffn_owned[:, :, 2 * ff :]).T,
    )


MESH = pl.DeviceIdType.MESH
CHIPS = 4
ROWS = 128
TILE = 256


def nn(left, right):
    return lax.dot_general(left, right, (((1,), (0,)), ((), ())), preferred_element_type=wide)


def nt(left, right):
    return lax.dot_general(left, right, (((1,), (1,)), ((), ())), preferred_element_type=wide)


def tn(left, right):
    return lax.dot_general(left, right, (((0,), (0,)), ((), ())), preferred_element_type=wide)


def halves(values):
    top = values.astype(low)
    return top, (values - top.astype(wide)).astype(low)


def fine_both(op, left, right):
    lh, ll = halves(left)
    rh, rl = halves(right)
    return op(lh, rh) + (op(lh, rl) + op(ll, rh))


def fine_left(op, left, right):
    lh, ll = halves(left)
    return op(lh, right) + op(ll, right)


def fine_right(op, left, right):
    rh, rl = halves(right)
    return op(left, rh) + op(left, rl)


def summed_by(ones, values):
    top, rest = halves(values)
    mid = (values - top.astype(wide)).astype(low)
    last = (values - top.astype(wide) - mid.astype(wide)).astype(low)
    return nn(ones, top) + (nn(ones, mid) + nn(ones, last))


def at(start, size, unit):
    return pl.ds(pl.multiple_of(start, unit), size)


def scratch_of(width, ffw, rank_pad):
    tokens = CHIPS * ROWS
    attn_cols = 2 * HK + 2 * HV
    ext = attn_cols + rank_pad
    tiles = width // TILE
    steps = ffw // TILE
    return {
        "SM": ((CHIPS, 48, TILE), low),
        "WA": ((width, attn_cols), low),
        "WO": ((4 * CHIPS, 2, 32, width), low),
        "WG": ((width, ffw), low),
        "WU": ((width, ffw), low),
        "WD": ((ffw, width), low),
        "DN": ((rank_pad, width), low),
        "UP": ((rank_pad, HK), low),
        "H1": ((tokens, width), low),
        "CT": ((tokens, width), low),
        "H2": ((tokens, width), low),
        "DR": ((tokens, width), low),
        "PJ": ((3, tokens, TILE), wide),
        "LG": ((tokens, HK), wide),
        "LR": ((tokens, rank_pad), low),
        "RU": ((tokens, HK), wide),
        "SC": ((tokens, ROWS), wide),
        "ADD": ((2, CHIPS, HV, HK), wide),
        "PUL": ((2, CHIPS, HV, HK), wide),
        "TOT": ((2, CHIPS, 8, HK), wide),
        "SS": ((2 * CHIPS + 1, HV, HK), wide),
        "DS": ((2 * CHIPS, HV, HK), wide),
        "ATT": ((tokens, HV), wide),
        "GS": ((tokens, HV), low),
        "GR": ((ROWS, width), low),
        "RES": ((ROWS, width), wide),
        "MX": ((tokens, ffw), low),
        "DGU": ((tokens, 2 * ffw), low),
        "SB": ((3, tiles, tokens, TILE), low),
        "RB": ((3, 3, tiles, ROWS, TILE), low),
        "DGS": ((CHIPS, ROWS, HV), low),
        "DGR": ((tokens, HV), low),
        "DO": ((tokens, HV), wide),
        "DQ": ((tokens, HK), wide),
        "DK": ((tokens, HK), wide),
        "DV": ((tokens, HV), wide),
        "DL": ((tokens, HK), low),
        "DP": ((tokens, ext), low),
        "H2T": ((width, tokens), low),
        "CTT": ((width, tokens), low),
        "GF": ((steps, tiles, 2, ROWS, 3 * TILE), low),
        "GFC": ((steps, tiles, ROWS, 3 * TILE), low),
        "GFZ": ((steps, 3, tiles, 32, 3 * TILE), low),
        "GFL": ((steps, tiles, 32, 3 * TILE), low),
        "GFS": ((steps, tiles, 32, 3 * TILE), low),
        "GFR": ((CHIPS, steps, 32, 3 * TILE), low),
        "GA": ((2, tiles // 2, 2, ROWS, ext), low),
        "GAC": ((2, tiles // 2, ROWS, ext), low),
        "GAZ": ((2, 3, tiles // 2, 32, ext), low),
        "GAL": ((2, tiles // 2, 32, ext), low),
        "GAS": ((tiles, 32, ext), low),
        "GAR": ((CHIPS, 32, ext), low),
        "GO": ((2, ROWS, width), low),
        "GOC": ((ROWS, width), low),
        "GOZ": ((3, 32, width), low),
        "GOL": ((32, width), low),
        "GP": ((8, width), wide),
        "GPC": ((8, width), wide),
        "GPX": ((3, 8, width), wide),
        "GPZ": ((3, 8, width), wide),
        "GPS": ((8, width), wide),
        "UB": ((24, HK), wide),
        "UBC": ((24, HK), wide),
        "UBZ": ((3, 24, HK), wide),
    }


COPIES = 320
LOCALS = 24


def plane_kernel(names, *refs):
    (factor_ref, up_in_ref, gain_one_ref, gain_two_ref, head_gain_ref, bias_ref) = refs[:6]
    (x_ref, cot_ref, q_hbm, k_hbm, v_hbm, g_hbm, o_hbm, fg_hbm, fu_hbm, fd_hbm) = refs[6:16]
    (out_ref, in_ref, go_ref, gf_ref, ga_ref, gains_ref, ub_ref) = refs[16:23]
    b = dict(zip(names, refs[23 : 23 + len(names)]))
    send_sems, recv_sems, local_sems = refs[23 + len(names) :]
    SM, WA, WO, WG, WU, WD, DN, UP = (b[n] for n in ("SM", "WA", "WO", "WG", "WU", "WD", "DN", "UP"))
    H1, CT, H2, DR, PJ, LG, LR, RU, SC = (
        b[n] for n in ("H1", "CT", "H2", "DR", "PJ", "LG", "LR", "RU", "SC")
    )
    ADD, PUL, TOT, SS, DS, ATT, GS, GR, RES = (
        b[n] for n in ("ADD", "PUL", "TOT", "SS", "DS", "ATT", "GS", "GR", "RES")
    )
    MX, DGU, SB, RB, DGS, DGR, DO, DQ, DK, DV, DL, DP = (
        b[n] for n in ("MX", "DGU", "SB", "RB", "DGS", "DGR", "DO", "DQ", "DK", "DV", "DL", "DP")
    )
    GP, GPC, GPX, GPZ, GPS, UB, UBC, UBZ = (
        b[n] for n in ("GP", "GPC", "GPX", "GPZ", "GPS", "UB", "UBC", "UBZ")
    )
    GO, GOC, GOZ, GOL = (b[n] for n in ("GO", "GOC", "GOZ", "GOL"))
    H2T, CTT = b["H2T"], b["CTT"]
    GF, GFC, GFZ, GFL, GFS, GFR = (b[n] for n in ("GF", "GFC", "GFZ", "GFL", "GFS", "GFR"))
    GA, GAC, GAZ, GAL, GAS, GAR = (b[n] for n in ("GA", "GAC", "GAZ", "GAL", "GAS", "GAR"))
    width = x_ref.shape[1]
    tokens = H1.shape[0]
    tiles = width // TILE
    ffw = WG.shape[1]
    steps = ffw // TILE
    last_ff = fg_hbm.shape[1] - (CHIPS - 1) * ffw
    rest_ff = ffw - last_ff
    ext = DP.shape[1]
    cols = 2 * HK + 2 * HV
    own = width // 4
    half = own // 2
    scale = HK ** (-0.5)

    s = lax.axis_index("seq")
    f = lax.axis_index("fsdp")
    p = s // 2
    c = s % 2
    chip = (None, p + 1 - 2 * (p % 2), (p + 2) % 4, 3 - p)
    plane = (None, f + 1 - 2 * (f % 2), (f + 2) % 4, 3 - f)
    near = (s + 1 - 2 * c, f)
    full = p < CHIPS - 1
    inner = (f > 0) & (f < 3)
    outer = jnp.logical_not(inner)

    used = [0, 0]
    pending = []

    def take(count=1):
        first = used[0]
        used[0] += count
        return first

    def remote(src, dst, dev, index, landed=None):
        return pltpu.make_async_remote_copy(
            src_ref=src,
            dst_ref=dst,
            send_sem=send_sems.at[index],
            recv_sem=recv_sems.at[index if landed is None else landed],
            device_id=dev,
            device_id_type=MESH,
        )

    def chip_dev(j):
        return (2 * chip[j] + c, f)

    def plane_dev(j):
        return (s, plane[j])

    def push(src, dst, dev):
        copy = remote(src, dst, dev, take())
        copy.start()
        pending.append(copy)
        return copy

    def local(src, dst):
        copy = pltpu.make_async_copy(src, dst, local_sems.at[used[1]])
        used[1] += 1
        copy.start()
        return copy

    def got(copies):
        for copy in copies:
            copy.wait_recv()

    ends = []

    def when(conds, action):
        conds = [cond for cond in conds if cond is not None]

        def run():
            action()

        if not conds:
            run()
            return
        both = conds[0]
        for cond in conds[1:]:
            both = both & cond
        pl.when(both)(run)

    class Gather:
        def __init__(self, parts, cond=None):
            self.parts, self.cond, self.count = parts, cond, len(parts)
            self.first, self.passed = take(3 * len(parts)), take(len(parts))
            ends.append(self.end)

        def copies(self, j, source=None):
            made = []
            for i, (src, view) in enumerate(self.parts):
                index = self.first + (j - 1) * self.count + i
                if source is None:
                    made.append(remote(src, view(f), plane_dev(j), index))
                else:
                    made.append(remote(view(source), view(source), plane_dev(j), index))
            return made

        def handed(self):
            return [
                remote(
                    view(plane[2]),
                    view(plane[2]),
                    plane_dev(1),
                    self.passed + i,
                    self.first + 2 * self.count + i,
                )
                for i, (_, view) in enumerate(self.parts)
            ]

        def start(self):
            when([self.cond], lambda: [copy.start() for j in (2, 1) for copy in self.copies(j)])
            when([self.cond, inner], lambda: [copy.start() for copy in self.copies(3)])

        def landed(self, j):
            for copy in self.copies(j, plane[j]):
                copy.wait_recv()

        def forward(self):
            def action():
                self.landed(2)
                for copy in self.handed():
                    copy.start()

            when([self.cond, inner], action)

        def arrived(self):
            when([self.cond], lambda: self.landed(1))
            when([self.cond, outer], lambda: self.landed(2))
            when([self.cond], lambda: self.landed(3))

        def end(self):
            when([self.cond], lambda: [copy.wait_send() for j in (1, 2) for copy in self.copies(j)])
            when(
                [self.cond, inner],
                lambda: [copy.wait_send() for copy in self.copies(3) + self.handed()],
            )

    class Scatter:
        def __init__(self, block, landing, relay):
            self.block, self.landing, self.relay = block, landing, relay
            self.first, self.extra = take(3), take(1)
            ends.append(self.end)

        def copy(self, j):
            return remote(self.block(plane[j]), self.landing.at[j - 1], plane_dev(j), self.first + j - 1)

        def aside(self):
            return remote(self.block(plane[3]), self.relay, plane_dev(1), self.extra)

        def start(self):
            when([outer], lambda: [self.aside().start(), self.copy(2).start()])
            self.copy(1).start()
            when([inner], lambda: self.copy(3).start())

        def forward(self):
            def action():
                self.aside().wait_recv()
                mine_too = self.block(plane[2])
                mine_too[...] = (mine_too[...].astype(wide) + self.relay[...].astype(wide)).astype(low)
                self.copy(2).start()

            when([inner], action)

        def arrived(self):
            self.copy(1).wait_recv()
            self.copy(2).wait_recv()
            when([inner], lambda: self.copy(3).wait_recv())

        def total(self):
            kept = self.block(f)[...].astype(wide)
            return kept + (
                self.landing[0].astype(wide) + self.landing[1].astype(wide) + self.landing[2].astype(wide)
            )

        def end(self):
            self.copy(1).wait_send()
            self.copy(2).wait_send()
            when([inner], lambda: self.copy(3).wait_send())
            when([outer], lambda: self.aside().wait_send())

    own_rows = at(f * own, own, own)
    at_qk = at(p * HK, HK, HK)
    at_v = at(p * HV, HV, HV)
    at_ff = at(p * ffw, last_ff, TILE)
    at_ff_rest = at(p * ffw + last_ff, rest_ff, TILE)
    loads_a = [
        local(q_hbm.at[:, at_qk], WA.at[own_rows, 0:HK]),
        local(k_hbm.at[:, at_qk], WA.at[own_rows, HK : 2 * HK]),
        local(v_hbm.at[:, at_v], WA.at[own_rows, 2 * HK : 2 * HK + HV]),
        local(g_hbm.at[:, at_v], WA.at[own_rows, 2 * HK + HV : cols]),
    ]
    loads_o = [
        local(
            o_hbm.at[pl.ds(pl.multiple_of(64 * i + 32 * h, 32), 32), :],
            WO.at[4 * f + i, h],
        )
        for i in range(CHIPS)
        for h in range(2)
    ]
    loads_f = [
        local(fg_hbm.at[:, at_ff], WG.at[own_rows, 0:last_ff]),
        local(fu_hbm.at[:, at_ff], WU.at[own_rows, 0:last_ff]),
        local(fd_hbm.at[at_ff, :], WD.at[0:last_ff, own_rows]),
    ]
    rest_at = used[1]
    used[1] += 3

    def loads_rest():
        pairs = (
            (fg_hbm.at[:, at_ff_rest], WG.at[own_rows, last_ff:ffw]),
            (fu_hbm.at[:, at_ff_rest], WU.at[own_rows, last_ff:ffw]),
            (fd_hbm.at[at_ff_rest, :], WD.at[last_ff:ffw, own_rows]),
        )
        return [
            pltpu.make_async_copy(src, dst, local_sems.at[rest_at + i])
            for i, (src, dst) in enumerate(pairs)
        ]

    @pl.when(full)
    def _():
        for copy in loads_rest():
            copy.start()

    @pl.when(jnp.logical_not(full))
    def _():
        WG[:, last_ff:ffw] = jnp.zeros((width, rest_ff), low)
        WU[:, last_ff:ffw] = jnp.zeros((width, rest_ff), low)
        WD[last_ff:ffw, :] = jnp.zeros((rest_ff, width), low)

    @pl.when(outer)
    def _():
        GFZ[:, 2] = jnp.zeros((steps, tiles, 32, 3 * TILE), low)
        GAZ[:, 2] = jnp.zeros((2, tiles // 2, 32, ext), low)
        GOZ[2] = jnp.zeros((32, width), low)

    DN[...] = jnp.zeros(DN.shape, low)
    UP[...] = jnp.zeros(UP.shape, low)
    GP[...] = jnp.zeros(GP.shape, wide)
    UB[...] = jnp.zeros(UB.shape, wide)
    SM[f, 0:16, :] = factor_ref[...]
    SM[f, 16:32, 0:HK] = up_in_ref[...]

    def as_row(ref, count):
        row = ref[...].astype(wide).reshape(1, count)
        return row if count == TILE else jnp.concatenate([row, jnp.zeros((1, TILE - count), wide)], axis=1)

    SM[f, 32:48, :] = jnp.concatenate(
        [
            as_row(gain_one_ref, TILE),
            as_row(gain_two_ref, TILE),
            as_row(head_gain_ref, HV // CHIPS),
            as_row(bias_ref, HK),
            jnp.zeros((12, TILE), wide),
        ],
        axis=0,
    ).astype(low)

    barrier = pltpu.get_barrier_semaphore()
    peers = [near] + [chip_dev(j) for j in (1, 2, 3)] + [plane_dev(j) for j in (1, 2, 3)]
    for dev in peers:
        pl.semaphore_signal(barrier, inc=1, device_id=dev, device_id_type=MESH)
    pl.semaphore_wait(barrier, len(peers))

    smalls = [push(SM.at[f], SM.at[f], plane_dev(j)) for j in (1, 2, 3)]
    half_rows = at(c * half, half, half)

    def half_at(fi):
        return at(fi * own + c * half, half, half)

    def columns(ref, first, count, start=0):
        return lambda fi: ref.at[half_at(fi), start : start + count]

    weights_a = Gather(
        [
            (q_hbm.at[half_rows, at_qk], columns(WA, 0, HK)),
            (k_hbm.at[half_rows, at_qk], columns(WA, 0, HK, HK)),
            (v_hbm.at[half_rows, at_v], columns(WA, 0, HV, 2 * HK)),
            (g_hbm.at[half_rows, at_v], columns(WA, 0, HV, 2 * HK + HV)),
        ]
    )
    o_rows = at(64 * p + 32 * c, 32, 32)
    weights_o = Gather([(o_hbm.at[o_rows, :], lambda fi: WO.at[4 * fi + p, c])])
    weights_f = []
    for n in range(steps):
        here = at(p * ffw + n * TILE, TILE, TILE)
        down_here = at(p * ffw + n * TILE + c * ROWS, ROWS, ROWS)
        down_there = at(n * TILE + c * ROWS, ROWS, ROWS)
        weights_f.append(
            Gather(
                [
                    (fg_hbm.at[half_rows, here], columns(WG, 0, TILE, n * TILE)),
                    (fu_hbm.at[half_rows, here], columns(WU, 0, TILE, n * TILE)),
                    (
                        fd_hbm.at[down_here, :],
                        lambda fi, down_there=down_there: WD.at[down_there, at(fi * own, own, own)],
                    ),
                ],
                None if n * TILE < last_ff else full,
            )
        )

    def swap_f(n):
        made = []
        for j in (1, 2, 3):
            for _, view in weights_f[n].parts:
                made.append(push(view(plane[j]), view(plane[j]), near))
        return made

    weights_a.start()

    x = x_ref[...]
    inv_one = lax.rsqrt(jnp.mean(x * x, axis=1, keepdims=True) + norm_eps)
    got(smalls)

    def full_row(row):
        return jnp.concatenate([SM[i, 32:48, :].astype(wide)[row : row + 1] for i in range(CHIPS)], axis=1)

    gain_one = full_row(0)
    gain_two = full_row(1)
    head_gain = jnp.concatenate(
        [SM[i, 32:48, :].astype(wide)[2:3, 0 : HV // CHIPS] for i in range(CHIPS)], axis=1
    )
    bias = SM[p, 32:48, 0:HK][3:4].astype(wide)
    for i in range(CHIPS):
        DN[0:16, i * TILE : (i + 1) * TILE] = SM[i, 0:16, :]
    UP[0:16, :] = SM[p, 16:32, 0:HK]

    mine = at(p * ROWS, ROWS, ROWS)
    H1[mine, :] = (x * inv_one * gain_one).astype(low)
    CT[mine, :] = cot_ref[...].astype(low)
    sends_h1 = [push(H1.at[mine, :], H1.at[mine, :], chip_dev(j)) for j in (1, 2, 3)]

    sends_ct = [push(CT.at[mine, :], CT.at[mine, :], chip_dev(j)) for j in (1, 2, 3)]
    weights_a.forward()
    weights_o.start()
    weights_f[0].start()
    weights_a.arrived()
    swaps_a = []
    for j in (1, 2, 3):
        swaps_a.append(push(WA.at[half_at(plane[j]), :], WA.at[half_at(plane[j]), :], near))
    for copy in loads_a:
        copy.wait()
    got(sends_h1)
    weights_o.forward()
    weights_f[1].start()
    got(swaps_a)

    def project(n, carry):
        PJ[n] = nn(H1[...], WA[:, at(n * TILE, TILE, TILE)])
        return carry

    lax.fori_loop(0, cols // TILE, project, 0)
    LR[...] = nt(H1[...], DN[...]).astype(low)
    LG[...] = nn(LR[...], UP[...]) + bias

    share_o = []
    weights_o.arrived()
    for j in (1, 2, 3):
        share_o += [
            push(WO.at[4 * plane[j] + p, c], WO.at[4 * plane[j] + p, c], chip_dev(t)) for t in (1, 2, 3)
        ]

    place_t = lax.broadcasted_iota(jnp.int32, (ROWS, ROWS), 0)
    place_s = lax.broadcasted_iota(jnp.int32, (ROWS, ROWS), 1)
    lower = place_t >= place_s
    ones_lower = lower.astype(wide).astype(low)
    ones_upper = (place_t <= place_s).astype(wide).astype(low)

    def block_rows(j):
        return at(j * ROWS, ROWS, ROWS)

    def block_q(rows):
        return PJ[0, rows, 0:HK].astype(low).astype(wide)

    def block_k(rows):
        return PJ[0, rows, HK : 2 * HK].astype(low).astype(wide)

    def block_v(rows):
        return PJ[1, rows, :].astype(low)

    mid = ROWS // 2

    def states(j, carry):
        rows = block_rows(j)
        running = summed_by(ones_lower, jax.nn.log_sigmoid(LG[rows, :]) / logit_norm)
        RU[rows, :] = running
        total = running[ROWS - 1 : ROWS]
        TOT[c, j] = jnp.broadcast_to(total, (8, HK))
        ADD[c, j] = fine_right(tn, block_v(rows), block_k(rows) * jnp.exp(total - running))
        return carry

    lax.fori_loop(0, CHIPS, states, 0)
    sends_state = [push(ADD.at[c], ADD.at[c], near), push(TOT.at[c], TOT.at[c], near)]

    def inside(j, carry):
        rows = block_rows(j)
        running = RU[rows, :]
        middle = running[mid - 1 : mid]
        qd = block_q(rows) * jnp.exp(running - middle)
        kd = block_k(rows) * jnp.exp(middle - running)
        scores = jnp.where(lower, fine_both(nt, qd, kd), 0.0)
        SC[rows, :] = scores
        ATT[rows, :] = fine_left(nn, scores, block_v(rows))
        return carry

    lax.fori_loop(0, CHIPS, inside, 0)

    got(sends_state)
    state = jnp.zeros((HV, HK), wide)
    for blk in range(2 * CHIPS):
        SS[blk] = state
        state = jnp.exp(TOT[blk % 2, blk // 2, 0:1, :]) * state + ADD[blk % 2, blk // 2]
    SS[2 * CHIPS] = state

    def attend(j, carry):
        rows = block_rows(j)
        qs = block_q(rows) * jnp.exp(RU[rows, :])
        att = scale * (ATT[rows, :] + fine_both(nt, qs, SS[2 * j + c]))
        ATT[rows, :] = att
        inv = lax.rsqrt(jnp.mean(att * att, axis=1, keepdims=True) + norm_eps)
        GS[rows, :] = (att * inv * head_gain * jax.nn.silu(PJ[2, rows, :])).astype(low)
        return carry

    lax.fori_loop(0, CHIPS, attend, 0)
    at_head = at(p * HV, HV, HV)
    sends_gated = [
        push(GS.at[at(chip[j] * ROWS, ROWS, ROWS), :], GR.at[:, at_head], chip_dev(j)) for j in (1, 2, 3)
    ]
    GR[:, at_head] = GS[mine, :]

    weights_f[0].forward()
    weights_f[2].start()

    got(share_o)
    swaps_o = []
    for j in (1, 2, 3):
        part = pl.ds(pl.multiple_of(4 * plane[j], 4), 4)
        swaps_o.append(push(WO.at[part, c], WO.at[part, c], near))

    got(sends_gated)
    for copy in loads_o:
        copy.wait()
    got(swaps_o)

    def out_tile(n, carry):
        here = at(n * TILE, TILE, TILE)
        RES[:, here] = x_ref[:, here] + nn(GR[...], WO[:, :, :, here].reshape(width, TILE))
        return carry

    lax.fori_loop(0, tiles, out_tile, 0)
    residual = RES[...]
    inv_two = lax.rsqrt(jnp.mean(residual * residual, axis=1, keepdims=True) + norm_eps)
    H2[mine, :] = (residual * inv_two * gain_two).astype(low)
    sends_h2 = [push(H2.at[mine, :], H2.at[mine, :], chip_dev(j)) for j in (1, 2, 3)]

    def turn(src, dst):
        def tile(n, carry):
            here = at(n * TILE, TILE, TILE)
            dst[here, :] = src[:, here].T
            return carry

        lax.fori_loop(0, tiles, tile, 0)

    got(sends_ct)
    turn(CT, CTT)
    weights_f[0].arrived()
    swaps_f = [swap_f(0)]
    for copy in loads_f:
        copy.wait()

    @pl.when(full)
    def _():
        for copy in loads_rest():
            copy.wait()

    got(sends_h2)

    def feed(n):
        here = slice(n * TILE, (n + 1) * TILE)
        rows_h2 = H2[...]
        pre_g = nn(rows_h2, WG[:, here])
        pre_u = nn(rows_h2, WU[:, here])
        d_mixed = nt(CT[...], WD[here, :])
        sig = jax.nn.sigmoid(pre_g)
        act = pre_g * sig
        MX[:, here] = (act * pre_u).astype(low)
        DGU[:, here] = (d_mixed * pre_u * (sig * (1.0 + pre_g * (1.0 - sig)))).astype(low)
        DGU[:, ffw + n * TILE : ffw + (n + 1) * TILE] = (d_mixed * act).astype(low)

    def ffn_grads(n):
        here = slice(n * TILE, (n + 1) * TILE)
        there = slice(ffw + n * TILE, ffw + (n + 1) * TILE)

        def tile(m, carry):
            rows = at(m * TILE, TILE, TILE)
            left = H2T[rows, :]
            GF[n, m, :, :, 0:TILE] = nn(left, DGU[:, here]).reshape(2, ROWS, TILE).astype(low)
            GF[n, m, :, :, TILE : 2 * TILE] = nn(left, DGU[:, there]).reshape(2, ROWS, TILE).astype(low)
            GF[n, m, :, :, 2 * TILE :] = nn(CTT[rows, :], MX[:, here]).reshape(2, ROWS, TILE).astype(low)
            return carry

        lax.fori_loop(0, tiles, tile, 0)
        return push(GF.at[n, :, 1 - c], GFC.at[n], near)

    z_ffn = [
        Scatter(
            lambda fi, n=n: GF.at[n, :, c, at(fi * 32, 32, 32), :],
            GFZ.at[n],
            GFL.at[n],
        )
        for n in range(steps)
    ]

    def ffn_out(n, swap):
        swap.wait_recv()

        def tile(m, carry):
            GF[n, m, c] = (GF[n, m, c].astype(wide) + GFC[n, m].astype(wide)).astype(low)
            return carry

        lax.fori_loop(0, tiles, tile, 0)
        z_ffn[n].start()

    weights_f[1].forward()
    got(swaps_f[0])
    feed(0)
    turn(H2, H2T)
    weights_f[1].arrived()
    swaps_f.append(swap_f(1))
    swap_g = [ffn_grads(0)]
    for n in range(1, steps):
        if n + 1 < steps:
            weights_f[n + 1].forward()
        got(swaps_f[n])
        feed(n)
        ffn_out(n - 1, swap_g[n - 1])
        if n + 1 < steps:
            swap_g.append(ffn_grads(n))
            weights_f[n + 1].arrived()
            swaps_f.append(swap_f(n + 1))

    sums_at = [take(3 * tiles) for _ in range(3)]

    def part_copy(kind, n, j):
        return remote(
            SB.at[kind, n, at(chip[j] * ROWS, ROWS, ROWS), :],
            RB.at[kind, j - 1, n],
            chip_dev(j),
            sums_at[kind] + 3 * n + (j - 1),
        )

    def send_parts(kind, n):
        for j in (1, 2, 3):
            part_copy(kind, n, j).start()

    def part_sum(kind, n):
        for j in (1, 2, 3):
            part_copy(kind, n, j).wait_recv()
        return (
            SB[kind, n, mine, :].astype(wide)
            + RB[kind, 0, n].astype(wide)
            + RB[kind, 1, n].astype(wide)
            + RB[kind, 2, n].astype(wide)
        )

    def d_hidden_tile(n, carry):
        rows = at(n * TILE, TILE, TILE)
        SB[0, n] = (nt(DGU[:, 0:ffw], WG[rows, :]) + nt(DGU[:, ffw : 2 * ffw], WU[rows, :])).astype(low)
        send_parts(0, n)
        return carry

    lax.fori_loop(0, tiles, d_hidden_tile, 0)

    swap_g.append(ffn_grads(steps - 1))

    def y_tile(n, carry):
        SB[1, n] = nn(MX[...], WD[:, at(n * TILE, TILE, TILE)]).astype(low)
        return carry

    lax.fori_loop(0, tiles, y_tile, 0)

    z_ffn[0].forward()
    ffn_out(steps - 1, swap_g[steps - 1])

    d_h2 = jnp.concatenate([part_sum(0, n) for n in range(tiles)], axis=1)
    residual = RES[...]
    inv_two = lax.rsqrt(jnp.mean(residual * residual, axis=1, keepdims=True) + norm_eps)
    unit = residual * inv_two
    pulled = d_h2 * gain_two
    GP[1:2, :] = jnp.sum(d_h2 * unit, axis=0, keepdims=True)
    d_res = cot_ref[...] + inv_two * (pulled - unit * jnp.mean(pulled * unit, axis=1, keepdims=True))
    in_ref[...] = d_res
    d_res_low = d_res.astype(low)
    DR[mine, :] = d_res_low

    def d_gated_tile(n, carry):
        w = WO[pl.ds(pl.multiple_of(4 * n, 4), 4)].reshape(own, width)
        DGS[n] = nt(DR[mine, :], w).astype(low)
        return carry

    lax.fori_loop(0, CHIPS, d_gated_tile, 0)
    sends_dg = [push(DGS.at[chip[j]], DGR.at[mine, :], chip_dev(j)) for j in (1, 2, 3)]
    DGR[mine, :] = DGS[p]

    got(sends_dg)
    z_ffn[1].forward()
    sends_dr = [push(DR.at[mine, :], DR.at[mine, :], chip_dev(j)) for j in (1, 2, 3)]

    def through_gate(j, head_sum):
        rows = block_rows(j)
        att = ATT[rows, :]
        inv = lax.rsqrt(jnp.mean(att * att, axis=1, keepdims=True) + norm_eps)
        unit_att = att * inv
        pre = PJ[2, rows, :]
        sig = jax.nn.sigmoid(pre)
        act = pre * sig
        d_gated = DGR[rows, :].astype(wide)
        through = d_gated * unit_att
        DP[rows, 2 * HK + HV : cols] = (through * head_gain * (sig * (1.0 + pre * (1.0 - sig)))).astype(low)
        d_unit = d_gated * head_gain * act
        d_out = scale * inv * (d_unit - unit_att * jnp.mean(d_unit * unit_att, axis=1, keepdims=True))
        DO[rows, :] = d_out
        PUL[c, j] = fine_both(tn, d_out, block_q(rows) * jnp.exp(RU[rows, :]))
        return head_sum + jnp.sum(through * act, axis=0, keepdims=True)

    head_sum = lax.fori_loop(0, CHIPS, through_gate, jnp.zeros((1, HV), wide))
    GP[2:3, 0:HV] = head_sum
    send_pull = push(PUL.at[c], PUL.at[c], near)

    def inside_back(j, carry):
        rows = block_rows(j)
        running = RU[rows, :]
        middle = running[mid - 1 : mid]
        up = jnp.exp(running - middle)
        down = jnp.exp(middle - running)
        qd = block_q(rows) * up
        kd = block_k(rows) * down
        d_out = DO[rows, :]
        d_scores = jnp.where(lower, fine_left(nt, d_out, block_v(rows)), 0.0)
        DQ[rows, :] = up * fine_both(nn, d_scores, kd) + jnp.exp(running) * fine_both(nn, d_out, SS[2 * j + c])
        DK[rows, :] = down * fine_both(tn, d_scores, qd)
        DV[rows, :] = fine_both(tn, SC[rows, :], d_out)
        return carry

    lax.fori_loop(0, CHIPS, inside_back, 0)
    send_pull.wait_recv()
    d_state = jnp.zeros((HV, HK), wide)
    for blk in range(2 * CHIPS - 1, -1, -1):
        DS[blk] = d_state
        d_state = jnp.exp(TOT[blk % 2, blk // 2, 0:1, :]) * d_state + PUL[blk % 2, blk // 2]

    def across_back(j, bias_sum):
        rows = block_rows(j)
        running = RU[rows, :]
        to_end = jnp.exp(running[ROWS - 1 : ROWS] - running)
        d_after = DS[2 * j + c]
        k_rows = block_k(rows)
        d_k = DK[rows, :] + to_end * fine_right(nn, block_v(rows), d_after)
        d_v = DV[rows, :] + fine_both(nt, k_rows * to_end, d_after)
        d_q = DQ[rows, :]
        tail = jnp.sum(d_after * SS[2 * j + c + 1], axis=0, keepdims=True)
        d_decay = summed_by(ones_upper, block_q(rows) * d_q - k_rows * d_k) + tail
        d_logits = d_decay * jax.nn.sigmoid(-LG[rows, :]) / logit_norm
        d_logits_low = d_logits.astype(low)
        DL[rows, :] = d_logits_low
        DP[rows, 0:HK] = d_q.astype(low)
        DP[rows, HK : 2 * HK] = d_k.astype(low)
        DP[rows, 2 * HK : 2 * HK + HV] = d_v.astype(low)
        DP[rows, cols:ext] = nt(d_logits_low, UP[...]).astype(low)
        return bias_sum + jnp.sum(d_logits, axis=0, keepdims=True)

    bias_sum = lax.fori_loop(0, CHIPS, across_back, jnp.zeros((1, HK), wide))
    UB[0:16, :] = tn(LR[...], DL[...])[0:16]
    UB[16:17, :] = bias_sum
    send_ub = push(UB, UBC, near)

    z_attn = [
        Scatter(
            lambda fi, i=i: GA.at[i, :, c, at(fi * 32, 32, 32), :],
            GAZ.at[i],
            GAL.at[i],
        )
        for i in range(2)
    ]

    def attn_grads(i):
        for m in range(tiles // 2):
            col = (i * (tiles // 2) + m) * TILE
            GA[i, m] = nn(H1[:, col : col + TILE].T, DP[...]).reshape(2, ROWS, ext).astype(low)
        return push(GA.at[i, :, 1 - c], GAC.at[i], near)

    def attn_out(i, swap):
        swap.wait_recv()
        for m in range(tiles // 2):
            GA[i, m, c] = (GA[i, m, c].astype(wide) + GAC[i, m].astype(wide)).astype(low)
        z_attn[i].start()

    swap_a = [attn_grads(0), attn_grads(1)]
    z_ffn[2].forward()
    attn_out(0, swap_a[0])
    attn_out(1, swap_a[1])

    got(sends_dr)

    def out_grad(n, carry):
        here = at(n * TILE, TILE, TILE)
        GO[:, :, here] = tn(GS[...], DR[:, here]).reshape(2, ROWS, TILE).astype(low)
        return carry

    lax.fori_loop(0, tiles, out_grad, 0)
    swap_out = push(GO.at[1 - c], GOC, near)

    def d_input_tile(n, carry):
        rows = at(n * TILE, TILE, TILE)
        SB[2, n] = (nt(DP[:, 0:cols], WA[rows, :]) + nn(DP[:, cols:ext], DN[:, rows])).astype(low)
        send_parts(2, n)
        return carry

    lax.fori_loop(0, tiles, d_input_tile, 0)

    swap_out.wait_recv()
    GO[c] = (GO[c].astype(wide) + GOC[...].astype(wide)).astype(low)
    z_out = Scatter(lambda fi: GO.at[c, at(fi * 32, 32, 32), :], GOZ, GOL)
    z_out.start()
    z_attn[0].forward()
    send_ub.wait_recv()
    UBC[...] = UB[...] + UBC[...]
    z_ub = [push(UBC, UBZ.at[j - 1], plane_dev(j)) for j in (1, 2, 3)]

    for n in range(tiles):
        send_parts(1, n)

    d_h1 = jnp.concatenate([part_sum(2, n) for n in range(tiles)], axis=1)
    x = x_ref[...]
    inv_one = lax.rsqrt(jnp.mean(x * x, axis=1, keepdims=True) + norm_eps)
    unit_one = x * inv_one
    pulled_one = d_h1 * gain_one
    GP[0:1, :] = jnp.sum(d_h1 * unit_one, axis=0, keepdims=True)
    send_gp = push(GP, GPC, near)
    in_ref[...] += inv_one * (
        pulled_one - unit_one * jnp.mean(pulled_one * unit_one, axis=1, keepdims=True)
    )
    send_gp.wait_recv()
    GPC[...] = GP[...] + GPC[...]
    x_gp = [push(GPC, GPX.at[j - 1], chip_dev(j)) for j in (1, 2, 3)]

    z_attn[1].forward()
    z_out.forward()

    def ffn_done(n):
        z_ffn[n].arrived()
        GFS[n] = z_ffn[n].total().astype(low)
        GFR[p, n] = GFS[n, p]
        return [push(GFS.at[n, chip[j]], GFR.at[p, n], chip_dev(j)) for j in (1, 2, 3)]

    a_ffn = [ffn_done(n) for n in range(steps)]
    got(x_gp)
    GPS[...] = GPC[...] + GPX[0] + GPX[1] + GPX[2]
    z_gp = [push(GPS, GPZ.at[j - 1], plane_dev(j)) for j in (1, 2, 3)]

    for n in range(tiles):
        here = slice(n * TILE, (n + 1) * TILE)
        out_ref[:, here] = RES[:, here] + part_sum(1, n)

    a_attn = []
    for i in range(2):
        z_attn[i].arrived()
        GAS[i * (tiles // 2) : (i + 1) * (tiles // 2)] = z_attn[i].total().astype(low)
    for j in (1, 2, 3):
        a_attn.append(push(GAS.at[chip[j]], GAR.at[p], chip_dev(j)))
    GAR[p] = GAS[p]
    for copies in a_ffn:
        got(copies)
    gf_ref[...] = GFR[...]
    z_out.arrived()
    go_ref[...] = z_out.total()
    got(z_ub)
    ub_ref[...] = UBC[...] + UBZ[0] + UBZ[1] + UBZ[2]
    got(z_gp)
    gains_ref[...] = GPS[...] + GPZ[0] + GPZ[1] + GPZ[2]
    got(a_attn)
    ga_ref[...] = GAR[...]

    for copy in pending:
        copy.wait_send()
    for end in ends:
        end()
    for kind in range(3):
        for n in range(tiles):
            for j in (1, 2, 3):
                part_copy(kind, n, j).wait_send()


def finish_kernel(out_in, in_in, go_in, gf, ga, gains, ub, *refs):
    (
        out_ref,
        in_ref,
        attn_gain_ref,
        gq_ref,
        gk_ref,
        gv_ref,
        gg_ref,
        down_ref,
        up_ref,
        bias_ref,
        head_ref,
        go_ref,
        ffn_gain_ref,
        gfg_ref,
        gfu_ref,
        gfd_ref,
    ) = refs
    out_ref[...] = out_in[...]
    in_ref[...] = in_in[...]
    go_ref[...] = go_in[...]
    device = lax.axis_index("seq") * CHIPS + lax.axis_index("fsdp")
    steps = gf.shape[1]
    cols = 2 * HK + 2 * HV
    down_total = jnp.zeros((32, ga.shape[2] - cols), wide)
    for i in range(CHIPS):
        piece = ga[i].astype(wide)
        gq_ref[:, i * HK : (i + 1) * HK] = piece[:, 0:HK]
        gk_ref[:, i * HK : (i + 1) * HK] = piece[:, HK : 2 * HK]
        gv_ref[:, i * HV : (i + 1) * HV] = piece[:, 2 * HK : 2 * HK + HV]
        gg_ref[:, i * HV : (i + 1) * HV] = piece[:, 2 * HK + HV : cols]
        down_total = down_total + piece[:, cols:]
        for n in range(steps):
            first = (i * steps + n) * TILE
            if first < gfg_ref.shape[1]:
                piece_f = gf[i, n].astype(wide)
                gfg_ref[:, first : first + TILE] = piece_f[:, 0:TILE]
                gfu_ref[:, first : first + TILE] = piece_f[:, TILE : 2 * TILE]
                gfd_ref[:, first : first + TILE] = piece_f[:, 2 * TILE :]
    down_ref[...] = down_total.T[0 : down_ref.shape[0], :]

    def lanes(ref, first, count):
        around = ref[:, pl.ds(pl.multiple_of(first // 128 * 128, 128), 128)]
        return pltpu.roll(around, (128 - first % 128) % 128, 1)[:, 0:count]

    gain_part = lanes(gains, device * attn_gain_ref.shape[1], attn_gain_ref.shape[1])
    attn_gain_ref[...] = gain_part[0:1]
    ffn_gain_ref[...] = gain_part[1:2]
    head_ref[...] = lanes(gains, device * head_ref.shape[1], head_ref.shape[1])[2:3]
    up_part = lanes(ub, (device % 8) * up_ref.shape[1], up_ref.shape[1])
    up_ref[...] = up_part[0:16]
    bias_ref[...] = up_part[16:17]


def in_plane(
    block_input,
    attn_gain,
    query_weight,
    key_weight,
    value_weight,
    gate_weight,
    decay_down,
    decay_up,
    decay_bias,
    head_gain,
    out_weight,
    ffn_gain,
    ffn_gate,
    ffn_up,
    ffn_down,
    cotangent,
):
    width = block_input.shape[2]
    ff_full = ffn_gate.shape[1]
    ffw = -(-ff_full // (CHIPS * TILE)) * TILE
    rank = decay_down.shape[1]

    scratch = scratch_of(width, ffw, 128)
    f32 = jax.ShapeDtypeStruct
    outs = pl.pallas_call(
        functools.partial(plane_kernel, tuple(scratch)),
        out_shape=[
            f32((ROWS, width), wide),
            f32((ROWS, width), wide),
            f32((32, width), wide),
            f32(*scratch["GFR"]),
            f32(*scratch["GAR"]),
            f32((8, width), wide),
            f32((24, HK), wide),
        ],
        in_specs=[pl.BlockSpec(memory_space=pltpu.VMEM)] * 8 + [pl.BlockSpec(memory_space=pl.ANY)] * 8,
        out_specs=[pl.BlockSpec(memory_space=pltpu.VMEM)] * 7,
        scratch_shapes=[pltpu.VMEM(shape, kind) for shape, kind in scratch.values()]
        + [
            pltpu.SemaphoreType.DMA((COPIES,)),
            pltpu.SemaphoreType.DMA((COPIES,)),
            pltpu.SemaphoreType.DMA((LOCALS,)),
        ],
        compiler_params=pltpu.CompilerParams(
            collective_id=0, has_side_effects=True, vmem_limit_bytes=62 * 1024 * 1024
        ),
        name="layer_step",
    )(
        decay_down.T,
        decay_up,
        attn_gain,
        ffn_gain,
        head_gain,
        decay_bias,
        block_input[0],
        cotangent[0],
        query_weight,
        key_weight,
        value_weight,
        gate_weight,
        out_weight,
        ffn_gate,
        ffn_up,
        ffn_down,
    )
    each = width // 32
    done = pl.pallas_call(
        finish_kernel,
        out_shape=[
            f32((ROWS, width), wide),
            f32((ROWS, width), wide),
            f32((1, each), wide),
            f32((32, CHIPS * HK), wide),
            f32((32, CHIPS * HK), wide),
            f32((32, CHIPS * HV), wide),
            f32((32, CHIPS * HV), wide),
            f32((rank, 32), wide),
            f32((rank, CHIPS * HK // 32), wide),
            f32((1, CHIPS * HK // 32), wide),
            f32((1, HV // 32), wide),
            f32((32, width), wide),
            f32((1, each), wide),
            f32((32, ff_full), wide),
            f32((32, ff_full), wide),
            f32((32, ff_full), wide),
        ],
        in_specs=[pl.BlockSpec(memory_space=pltpu.VMEM)] * 7,
        out_specs=[pl.BlockSpec(memory_space=pltpu.VMEM)] * 16,
        compiler_params=pltpu.CompilerParams(vmem_limit_bytes=62 * 1024 * 1024),
        name="results",
    )(*outs)
    shapes = {0: (1, ROWS, width), 1: (1, ROWS, width), 2: (-1,), 9: (-1,), 10: (-1,), 12: (-1,)}
    done = [v.reshape(shapes[i]) if i in shapes else v for i, v in enumerate(done)]
    done[7], done[15] = done[7].T, done[15].T
    return tuple(done)


def solution(mesh):
    one_plane = mesh.shape["seq"] == 2 * CHIPS and mesh.shape["fsdp"] == CHIPS
    return jax.shard_map(
        in_plane if one_plane else spread,
        mesh=mesh,
        in_specs=(
            P("fsdp", "seq", None),
            P("fsdp"),
            P("fsdp", None),
            P("fsdp", None),
            P("fsdp", None),
            P("fsdp", None),
            P("fsdp", None),
            P(None, "fsdp"),
            P("fsdp"),
            P("fsdp"),
            P("fsdp", None),
            P("fsdp"),
            P("fsdp", None),
            P("fsdp", None),
            P(None, "fsdp"),
            P("fsdp", "seq", None),
        ),
        out_specs=(
            P("fsdp", "seq", None),
            P("fsdp", "seq", None),
            P(("seq", "fsdp")),
            P(("seq", "fsdp"), None),
            P(("seq", "fsdp"), None),
            P(("seq", "fsdp"), None),
            P(("seq", "fsdp"), None),
            P(("seq", "fsdp"), None),
            P(None, ("seq", "fsdp")),
            P(("seq", "fsdp")),
            P(("seq", "fsdp")),
            P(("seq", "fsdp"), None),
            P(("seq", "fsdp")),
            P(("seq", "fsdp"), None),
            P(("seq", "fsdp"), None),
            P(None, ("seq", "fsdp")),
        ),
        check_vma=False,
    )
```

```python
import functools

import jax
import jax.numpy as jnp
from jax import lax
from jax.experimental import pallas as pl
from jax.experimental.pallas import tpu as pltpu
from jax.sharding import PartitionSpec as P

HK = 128
HV = 256
BLOCK = 64


norm_eps = 1e-06
logit_norm = 16.0
exact = lax.Precision.HIGHEST
fine = lax.Precision.HIGH
low = jnp.bfloat16
wide = jnp.float32


def product(left, right):
    return jnp.dot(left, right, preferred_element_type=wide)


def transposed(left, right):
    return lax.dot_general(left, right, (((0,), (0,)), ((), ())), preferred_element_type=wide)


def against(left, right):
    return lax.dot_general(left, right, (((1,), (1,)), ((), ())), preferred_element_type=wide)


def fine_dot(spec, left, right):
    return jnp.einsum(spec, left, right, precision=fine, preferred_element_type=wide)


def rms_gain(token_rows, gain_row):
    return (
        token_rows
        * lax.rsqrt(jnp.mean(token_rows * token_rows, axis=-1, keepdims=True) + norm_eps)
        * gain_row
    )


def gated_norm(attended, gate_pre, head_gain):
    return rms_gain(attended, head_gain) * jax.nn.silu(gate_pre)


def swiglu(gate_part, up_part):
    return jax.nn.silu(gate_part) * up_part


def exchange(pieces):
    return lax.all_to_all(pieces, "fsdp", 0, 0)


def gather_rows(rows):
    return lax.all_gather(rows, "fsdp", axis=0, tiled=True)


def scatter_rows(rows):
    return lax.psum_scatter(rows.astype(low), "fsdp", scatter_dimension=0, tiled=True).astype(wide)


def summed_rows(grads):
    return lax.psum_scatter(grads.astype(low), "seq", scatter_dimension=0, tiled=True)


def owned_columns(section, parts):
    return exchange(section.reshape(parts, section.shape[0] // parts, -1))


def across(pieces):
    rows = pieces.shape[1]
    return pieces.transpose(1, 0, 2).reshape(rows, -1).astype(wide)


def spread(
    block_input,
    attn_gain,
    query_weight,
    key_weight,
    value_weight,
    gate_weight,
    decay_down,
    decay_up,
    decay_bias,
    head_gain,
    out_weight,
    ffn_gain,
    ffn_gate,
    ffn_up,
    ffn_down,
    cotangent,
):
    shards, parts = lax.axis_size("seq"), lax.axis_size("fsdp")
    si = lax.axis_index("seq")
    x = block_input[0]
    cot_rows = cotangent[0]
    length, width = x.shape
    blocks = length // BLOCK
    scale = HK ** (-0.5)

    small = jnp.concatenate([attn_gain, ffn_gain, head_gain, decay_down.reshape(-1)])
    small = exchange(jnp.broadcast_to(small[None], (parts, small.shape[0])))
    own = attn_gain.shape[0]
    own_head = head_gain.shape[0]
    gain_one = small[:, :own].reshape(-1).astype(wide)
    gain_two = small[:, own : 2 * own].reshape(-1).astype(wide)
    gain_head = small[:, 2 * own : 2 * own + own_head].reshape(-1).astype(wide)
    down_full = small[:, 2 * own + own_head :].reshape(width, -1)
    rank = down_full.shape[1]

    normed_one, norm_one_back = jax.vjp(rms_gain, x, gain_one)
    both = gather_rows(jnp.concatenate([normed_one.astype(low), cot_rows.astype(low)], axis=1))
    hidden_one = both[:, :width]
    cot_low = both[:, width:]
    ff = ffn_gate.shape[1] // parts
    rows = own // shards
    down_rows = ff // shards
    cuts = [
        lax.dynamic_slice_in_dim(w, si * rows, rows, 0).reshape(rows, parts, -1).transpose(1, 0, 2)
        for w in (query_weight, key_weight, value_weight, gate_weight, ffn_gate, ffn_up)
    ]
    cuts.append(
        lax.dynamic_slice_in_dim(
            ffn_down.reshape(parts, ff, own), si * down_rows, down_rows, 1
        ).reshape(parts, rows, -1)
    )
    got = lax.all_gather(exchange(jnp.concatenate(cuts, axis=2)), "seq")
    attn_columns = 2 * HK + 2 * HV
    attn_w = got[..., :attn_columns].transpose(1, 0, 2, 3).reshape(width, -1)
    ffn_w = (
        got[..., attn_columns : attn_columns + 2 * ff].transpose(1, 0, 2, 3).reshape(width, -1)
    )
    down_w = (
        got[..., attn_columns + 2 * ff :]
        .reshape(shards, parts, down_rows, own)
        .transpose(0, 2, 1, 3)
        .reshape(ff, width)
    )

    projected = product(hidden_one, attn_w)
    rounded = projected[:, : 2 * HK + HV].astype(low)
    gate_pre = projected[:, 2 * HK + HV :]
    low_rank = product(hidden_one, down_full).astype(low)
    logits = product(low_rank, decay_up) + decay_bias.astype(wide)
    log_decay = jax.nn.log_sigmoid(logits) / logit_norm

    def chunked(rows):
        return rows.reshape(parts * blocks, BLOCK, -1)

    q = chunked(rounded[:, :HK].astype(wide))
    k = chunked(rounded[:, HK : 2 * HK].astype(wide))
    v = chunked(rounded[:, 2 * HK :].astype(wide))
    place = jnp.arange(BLOCK)
    lower = place[:, None] >= place[None, :]
    ones_lower = lower.astype(wide)
    running = jnp.einsum("ts,bsk->btk", ones_lower, chunked(log_decay), precision=exact)
    total = running[:, -1]
    grown = jnp.exp(running)
    shrunk = jnp.exp(-running)
    to_end = jnp.exp(total[:, None] - running)
    qd = q * grown
    kd = k * shrunk
    kf = k * to_end
    scores = jnp.where(lower[None], fine_dot("btk,bsk->bts", qd, kd), 0.0)
    intra = fine_dot("bts,bsv->btv", scores, v)
    added = fine_dot("bsk,bsv->bkv", kf, v)
    added_c = added.reshape(parts, blocks, HK, HV)
    total_c = total.reshape(parts, blocks, HK)
    factor_c = jnp.exp(total_c)[..., None]
    local_state = added_c[:, 0]
    for c in range(1, blocks):
        local_state = factor_c[:, c] * local_state + added_c[:, c]
    totals = lax.all_gather(jnp.sum(total_c, axis=1), "seq")
    states = lax.all_gather(local_state.astype(low), "seq")
    index = jnp.arange(shards)
    upto = jnp.cumsum(totals, axis=0)
    mine_upto = lax.dynamic_index_in_dim(upto, si, 0, False)
    mine_total = lax.dynamic_index_in_dim(totals, si, 0, False)
    before = (index < si)[:, None, None]
    after = (index > si)[:, None, None]
    early = jnp.where(before, jnp.exp(jnp.where(before, mine_upto - mine_total - upto, 0.0)), 0.0)
    late = jnp.where(
        after, jnp.exp(jnp.where(after, upto - totals - mine_upto, 0.0)), 0.0
    )
    incoming = jnp.sum(early[..., None] * states.astype(wide), axis=0)
    entering = [incoming]
    for c in range(blocks):
        entering.append(factor_c[:, c] * entering[-1] + added_c[:, c])
    state_in = jnp.stack(entering[:-1], axis=1).reshape(parts * blocks, HK, HV)
    state_out = jnp.stack(entering[1:], axis=1).reshape(parts * blocks, HK, HV)
    attended = scale * (intra + fine_dot("btk,bkv->btv", qd, state_in))
    attended = attended.reshape(parts * length, HV)

    gated, gated_back = jax.vjp(gated_norm, attended, gate_pre, gain_head)
    gated_low = gated.astype(low)
    residual = x + scatter_rows(product(gated_low, out_weight))
    normed_two, norm_two_back = jax.vjp(rms_gain, residual, gain_two)
    hidden_two = gather_rows(normed_two.astype(low))
    pre = product(hidden_two, ffn_w)
    mixed, mixed_back = jax.vjp(swiglu, pre[:, :ff], pre[:, ff:])
    mixed_low = mixed.astype(low)
    d_gate_part, d_up_part = mixed_back(against(cot_low, down_w))
    d_pre = jnp.concatenate([d_gate_part.astype(low), d_up_part.astype(low)], axis=1)
    both = scatter_rows(
        jnp.concatenate(
            [against(d_pre, ffn_w).astype(low), product(mixed_low, down_w).astype(low)], axis=1
        )
    )
    d_residual_norm, grad_ffn_gain = norm_two_back(both[:, :width])
    d_residual = cot_rows + d_residual_norm
    d_res_low = gather_rows(d_residual.astype(low))
    block_output = residual + both[:, width:]
    ffn_section = summed_rows(
        jnp.concatenate(
            [transposed(hidden_two, d_pre).astype(low), transposed(cot_low, mixed_low).astype(low)],
            axis=1,
        )
    )
    ffn_owned = owned_columns(ffn_section, parts)

    d_attended, d_gate_pre, grad_head_gain = gated_back(against(d_res_low, out_weight))
    d_out = chunked(scale * d_attended)
    pulled = fine_dot("btk,btv->bkv", qd, d_out)
    pulled_c = pulled.reshape(parts, blocks, HK, HV)
    local_pull = pulled_c[:, blocks - 1]
    for c in range(blocks - 2, -1, -1):
        local_pull = factor_c[:, c] * local_pull + pulled_c[:, c]
    pulls = lax.all_gather(local_pull.astype(low), "seq")
    later = jnp.sum(late[..., None] * pulls.astype(wide), axis=0)
    leaving = [later]
    for c in range(blocks - 1, 0, -1):
        leaving.insert(0, factor_c[:, c] * leaving[0] + pulled_c[:, c])
    d_state = jnp.stack(leaving, axis=1).reshape(parts * blocks, HK, HV)
    d_scores = jnp.where(lower[None], fine_dot("btv,bsv->bts", d_out, v), 0.0)
    d_q = grown * (
        fine_dot("bts,bsk->btk", d_scores, kd) + fine_dot("btv,bkv->btk", d_out, state_in)
    )
    d_k = shrunk * fine_dot("bts,btk->bsk", d_scores, qd) + to_end * fine_dot(
        "bsv,bkv->bsk", v, d_state
    )
    d_v = fine_dot("bts,btv->bsv", scores, d_out) + fine_dot("bsk,bkv->bsv", kf, d_state)
    tail_term = jnp.sum(d_state * state_out, axis=2)
    d_log_decay = (
        jnp.einsum("st,bsk->btk", ones_lower, q * d_q - k * d_k, precision=exact)
        + tail_term[:, None]
    )
    d_logits = d_log_decay.reshape(parts * length, HK) * jax.nn.sigmoid(-logits) / logit_norm
    grad_decay_bias = jnp.sum(d_logits, axis=0)
    d_logits_low = d_logits.astype(low)
    grad_decay_up = transposed(low_rank, d_logits_low)
    d_low_rank = against(d_logits_low, decay_up).astype(low)
    grad_decay_down = transposed(hidden_one, d_low_rank)
    d_projected = jnp.concatenate(
        [
            d_q.reshape(parts * length, HK).astype(low),
            d_k.reshape(parts * length, HK).astype(low),
            d_v.reshape(parts * length, HV).astype(low),
            d_gate_pre.astype(low),
        ],
        axis=1,
    )
    d_hidden_one = scatter_rows(against(d_projected, attn_w) + against(d_low_rank, down_full))
    d_input_norm, grad_attn_gain = norm_one_back(d_hidden_one)
    input_grad = d_residual + d_input_norm
    devices = shards * parts
    grad_out = transposed(gated_low, d_res_low).astype(low)
    attn_section = summed_rows(
        jnp.concatenate(
            [transposed(hidden_one, d_projected).astype(low), grad_out.reshape(width, HV)], axis=1
        )
    )
    attn_owned = owned_columns(attn_section[:, :attn_columns], parts)
    turned = [(s * parts + f, f * shards + s) for s in range(shards) for f in range(parts)]
    own_out = lax.ppermute(
        attn_section[:, attn_columns:].reshape(-1, width), ("seq", "fsdp"), turned
    ).astype(wide)
    head_part = jnp.concatenate(
        [
            grad_decay_up.reshape(rank, shards, -1).transpose(1, 0, 2).reshape(shards, -1),
            grad_decay_bias.reshape(shards, -1),
        ],
        axis=1,
    )
    mine = jnp.arange(parts)[:, None, None] == lax.axis_index("fsdp")
    head_part = jnp.where(mine, head_part[None], 0.0).reshape(devices, -1)
    own_bias_size = HK // shards
    summed = jnp.concatenate(
        [
            grad_attn_gain.reshape(devices, -1),
            grad_ffn_gain.reshape(devices, -1),
            grad_head_gain.reshape(devices, -1),
            grad_decay_down.reshape(devices, -1),
            head_part,
        ],
        axis=1,
    )
    summed = jnp.sum(lax.all_to_all(summed, ("seq", "fsdp"), 0, 0), axis=0)
    each = width // devices
    each_head = HV // devices
    own_attn_gain = summed[:each]
    own_ffn_gain = summed[each : 2 * each]
    own_head_gain = summed[2 * each : 2 * each + each_head]
    at_up = 2 * each + each_head + each * rank
    at_bias = at_up + rank * own_bias_size
    own_down = summed[2 * each + each_head : at_up].reshape(each, rank)
    own_up = summed[at_up:at_bias].reshape(rank, own_bias_size)
    own_bias = summed[at_bias:]
    return (
        block_output[None],
        input_grad[None],
        own_attn_gain,
        across(attn_owned[:, :, :HK]),
        across(attn_owned[:, :, HK : 2 * HK]),
        across(attn_owned[:, :, 2 * HK : 2 * HK + HV]),
        across(attn_owned[:, :, 2 * HK + HV :]),
        own_down,
        own_up,
        own_bias,
        own_head_gain,
        own_out,
        own_ffn_gain,
        across(ffn_owned[:, :, :ff]),
        across(ffn_owned[:, :, ff : 2 * ff]),
        across(ffn_owned[:, :, 2 * ff :]).T,
    )


MESH = pl.DeviceIdType.MESH
CHIPS = 4
ROWS = 128
TILE = 256


def nn(left, right):
    return lax.dot_general(left, right, (((1,), (0,)), ((), ())), preferred_element_type=wide)


def nt(left, right):
    return lax.dot_general(left, right, (((1,), (1,)), ((), ())), preferred_element_type=wide)


def tn(left, right):
    return lax.dot_general(left, right, (((0,), (0,)), ((), ())), preferred_element_type=wide)


def halves(values):
    top = values.astype(low)
    return top, (values - top.astype(wide)).astype(low)


def fine_both(op, left, right):
    lh, ll = halves(left)
    rh, rl = halves(right)
    return op(lh, rh) + (op(lh, rl) + op(ll, rh))


def fine_left(op, left, right):
    lh, ll = halves(left)
    return op(lh, right) + op(ll, right)


def fine_right(op, left, right):
    rh, rl = halves(right)
    return op(left, rh) + op(left, rl)


def summed_by(ones, values):
    top, rest = halves(values)
    mid = (values - top.astype(wide)).astype(low)
    last = (values - top.astype(wide) - mid.astype(wide)).astype(low)
    return nn(ones, top) + (nn(ones, mid) + nn(ones, last))


def at(start, size, unit):
    return pl.ds(pl.multiple_of(start, unit), size)


def scratch_of(width, ffw, rank_pad):
    tokens = CHIPS * ROWS
    attn_cols = 2 * HK + 2 * HV
    ext = attn_cols + rank_pad
    tiles = width // TILE
    steps = ffw // TILE
    return {
        "SM": ((CHIPS, 48, TILE), low),
        "WA": ((width, attn_cols), low),
        "WO": ((4 * CHIPS, 2, 32, width), low),
        "WG": ((width, ffw), low),
        "WU": ((width, ffw), low),
        "WD": ((ffw, width), low),
        "DN": ((rank_pad, width), low),
        "UP": ((rank_pad, HK), low),
        "H1": ((tokens, width), low),
        "CT": ((tokens, width), low),
        "H2": ((tokens, width), low),
        "DR": ((tokens, width), low),
        "PJ": ((3, tokens, TILE), wide),
        "LG": ((tokens, HK), wide),
        "LR": ((tokens, rank_pad), low),
        "RU": ((tokens, HK), wide),
        "SC": ((tokens, ROWS), wide),
        "ADD": ((2, CHIPS, HV, HK), wide),
        "PUL": ((2, CHIPS, HV, HK), wide),
        "TOT": ((2, CHIPS, 8, HK), wide),
        "SS": ((2 * CHIPS + 1, HV, HK), wide),
        "DS": ((2 * CHIPS, HV, HK), wide),
        "ATT": ((tokens, HV), wide),
        "GS": ((tokens, HV), low),
        "GR": ((ROWS, width), low),
        "RES": ((ROWS, width), wide),
        "MX": ((tokens, ffw), low),
        "DGU": ((tokens, 2 * ffw), low),
        "SB": ((3, tiles, tokens, TILE), low),
        "RB": ((3, 2, tiles, ROWS, TILE), low),
        "RL": ((3, 2, tiles, ROWS // 2, TILE), low),
        "DGS": ((CHIPS, ROWS, HV), low),
        "DGR": ((tokens, HV), low),
        "DO": ((tokens, HV), wide),
        "DQ": ((tokens, HK), wide),
        "DK": ((tokens, HK), wide),
        "DV": ((tokens, HV), wide),
        "DL": ((tokens, HK), low),
        "DP": ((tokens, ext), low),
        "H2T": ((width, tokens), low),
        "CTT": ((width, tokens), low),
        "GF": ((steps, tiles, 2, ROWS, 3 * TILE), low),
        "GFC": ((steps, tiles, ROWS, 3 * TILE), low),
        "GFZ": ((steps, 3, tiles, 32, 3 * TILE), low),
        "GFL": ((steps, tiles, 32, 3 * TILE), low),
        "GFS": ((steps, tiles, 32, 3 * TILE), low),
        "GFR": ((CHIPS, steps, 32, 3 * TILE), low),
        "GA": ((2, tiles // 2, 2, ROWS, ext), low),
        "GAC": ((2, tiles // 2, ROWS, ext), low),
        "GAZ": ((2, 3, tiles // 2, 32, ext), low),
        "GAL": ((2, tiles // 2, 32, ext), low),
        "GAS": ((tiles, 32, ext), low),
        "GAR": ((CHIPS, 32, ext), low),
        "GO": ((2, ROWS, width), low),
        "GOC": ((ROWS, width), low),
        "GOZ": ((3, 32, width), low),
        "GOL": ((32, width), low),
        "GP": ((8, width), wide),
        "GPC": ((8, width), wide),
        "GPX": ((3, 8, width), wide),
        "GPZ": ((3, 8, width), wide),
        "GPS": ((8, width), wide),
        "UB": ((24, HK), wide),
        "UBC": ((24, HK), wide),
        "UBZ": ((3, 24, HK), wide),
    }


COPIES = 320
LOCALS = 24


def plane_kernel(names, *refs):
    (factor_ref, up_in_ref, gain_one_ref, gain_two_ref, head_gain_ref, bias_ref) = refs[:6]
    (x_ref, cot_ref, q_hbm, k_hbm, v_hbm, g_hbm, o_hbm, fg_hbm, fu_hbm, fd_hbm) = refs[6:16]
    (out_ref, in_ref, go_ref, gf_ref, ga_ref, gains_ref, ub_ref) = refs[16:23]
    b = dict(zip(names, refs[23 : 23 + len(names)]))
    send_sems, recv_sems, local_sems = refs[23 + len(names) :]
    SM, WA, WO, WG, WU, WD, DN, UP = (b[n] for n in ("SM", "WA", "WO", "WG", "WU", "WD", "DN", "UP"))
    H1, CT, H2, DR, PJ, LG, LR, RU, SC = (
        b[n] for n in ("H1", "CT", "H2", "DR", "PJ", "LG", "LR", "RU", "SC")
    )
    ADD, PUL, TOT, SS, DS, ATT, GS, GR, RES = (
        b[n] for n in ("ADD", "PUL", "TOT", "SS", "DS", "ATT", "GS", "GR", "RES")
    )
    MX, DGU, SB, RB, DGS, DGR, DO, DQ, DK, DV, DL, DP = (
        b[n] for n in ("MX", "DGU", "SB", "RB", "DGS", "DGR", "DO", "DQ", "DK", "DV", "DL", "DP")
    )
    GP, GPC, GPX, GPZ, GPS, UB, UBC, UBZ = (
        b[n] for n in ("GP", "GPC", "GPX", "GPZ", "GPS", "UB", "UBC", "UBZ")
    )
    GO, GOC, GOZ, GOL = (b[n] for n in ("GO", "GOC", "GOZ", "GOL"))
    H2T, CTT, RL = b["H2T"], b["CTT"], b["RL"]
    GF, GFC, GFZ, GFL, GFS, GFR = (b[n] for n in ("GF", "GFC", "GFZ", "GFL", "GFS", "GFR"))
    GA, GAC, GAZ, GAL, GAS, GAR = (b[n] for n in ("GA", "GAC", "GAZ", "GAL", "GAS", "GAR"))
    width = x_ref.shape[1]
    tokens = H1.shape[0]
    tiles = width // TILE
    ffw = WG.shape[1]
    steps = ffw // TILE
    last_ff = fg_hbm.shape[1] - (CHIPS - 1) * ffw
    rest_ff = ffw - last_ff
    ext = DP.shape[1]
    cols = 2 * HK + 2 * HV
    own = width // 4
    half = own // 2
    scale = HK ** (-0.5)

    s = lax.axis_index("seq")
    f = lax.axis_index("fsdp")
    p = s // 2
    c = s % 2
    chip = (None, p + 1 - 2 * (p % 2), (p + 2) % 4, 3 - p)
    plane = (None, f + 1 - 2 * (f % 2), (f + 2) % 4, 3 - f)
    near = (s + 1 - 2 * c, f)
    full = p < CHIPS - 1
    inner = (f > 0) & (f < 3)
    outer = jnp.logical_not(inner)

    used = [0, 0]
    pending = []

    def take(count=1):
        first = used[0]
        used[0] += count
        return first

    def remote(src, dst, dev, index, landed=None):
        return pltpu.make_async_remote_copy(
            src_ref=src,
            dst_ref=dst,
            send_sem=send_sems.at[index],
            recv_sem=recv_sems.at[index if landed is None else landed],
            device_id=dev,
            device_id_type=MESH,
        )

    def chip_dev(j):
        return (2 * chip[j] + c, f)

    def plane_dev(j):
        return (s, plane[j])

    def push(src, dst, dev):
        copy = remote(src, dst, dev, take())
        copy.start()
        pending.append(copy)
        return copy

    def local(src, dst):
        copy = pltpu.make_async_copy(src, dst, local_sems.at[used[1]])
        used[1] += 1
        copy.start()
        return copy

    def got(copies):
        for copy in copies:
            copy.wait_recv()

    ends = []

    def when(conds, action):
        conds = [cond for cond in conds if cond is not None]

        def run():
            action()

        if not conds:
            run()
            return
        both = conds[0]
        for cond in conds[1:]:
            both = both & cond
        pl.when(both)(run)

    class Gather:
        def __init__(self, parts, cond=None):
            self.parts, self.cond, self.count = parts, cond, len(parts)
            self.first, self.passed = take(3 * len(parts)), take(len(parts))
            ends.append(self.end)

        def copies(self, j, source=None):
            made = []
            for i, (src, view) in enumerate(self.parts):
                index = self.first + (j - 1) * self.count + i
                if source is None:
                    made.append(remote(src, view(f), plane_dev(j), index))
                else:
                    made.append(remote(view(source), view(source), plane_dev(j), index))
            return made

        def handed(self):
            return [
                remote(
                    view(plane[2]),
                    view(plane[2]),
                    plane_dev(1),
                    self.passed + i,
                    self.first + 2 * self.count + i,
                )
                for i, (_, view) in enumerate(self.parts)
            ]

        def start(self):
            when([self.cond], lambda: [copy.start() for j in (2, 1) for copy in self.copies(j)])
            when([self.cond, inner], lambda: [copy.start() for copy in self.copies(3)])

        def landed(self, j):
            for copy in self.copies(j, plane[j]):
                copy.wait_recv()

        def forward(self):
            def action():
                self.landed(2)
                for copy in self.handed():
                    copy.start()

            when([self.cond, inner], action)

        def arrived(self):
            when([self.cond], lambda: self.landed(1))
            when([self.cond, outer], lambda: self.landed(2))
            when([self.cond], lambda: self.landed(3))

        def end(self):
            when([self.cond], lambda: [copy.wait_send() for j in (1, 2) for copy in self.copies(j)])
            when(
                [self.cond, inner],
                lambda: [copy.wait_send() for copy in self.copies(3) + self.handed()],
            )

    class Scatter:
        def __init__(self, block, landing, relay):
            self.block, self.landing, self.relay = block, landing, relay
            self.first, self.extra = take(3), take(1)
            ends.append(self.end)

        def copy(self, j):
            return remote(self.block(plane[j]), self.landing.at[j - 1], plane_dev(j), self.first + j - 1)

        def aside(self):
            return remote(self.block(plane[3]), self.relay, plane_dev(1), self.extra)

        def start(self):
            when([outer], lambda: [self.aside().start(), self.copy(2).start()])
            self.copy(1).start()
            when([inner], lambda: self.copy(3).start())

        def forward(self):
            def action():
                self.aside().wait_recv()
                mine_too = self.block(plane[2])
                mine_too[...] = (mine_too[...].astype(wide) + self.relay[...].astype(wide)).astype(low)
                self.copy(2).start()

            when([inner], action)

        def arrived(self):
            self.copy(1).wait_recv()
            self.copy(2).wait_recv()
            when([inner], lambda: self.copy(3).wait_recv())

        def total(self):
            kept = self.block(f)[...].astype(wide)
            return kept + (
                self.landing[0].astype(wide) + self.landing[1].astype(wide) + self.landing[2].astype(wide)
            )

        def end(self):
            self.copy(1).wait_send()
            self.copy(2).wait_send()
            when([inner], lambda: self.copy(3).wait_send())
            when([outer], lambda: self.aside().wait_send())

    def token_rows(chip_at, part=None):
        if part is None:
            return at(chip_at * ROWS, ROWS, ROWS)
        return at(chip_at * ROWS + part * (ROWS // 2), ROWS // 2, ROWS // 2)

    class Spread:
        def __init__(self, buf):
            self.buf, self.first = buf, take(4)
            ends.append(self.end)

        def sent(self, j, chip_at, part=None, index=0):
            here = self.buf.at[token_rows(chip_at, part), :]
            return remote(here, here, chip_dev(j), self.first + index)

        def start(self):
            self.sent(1, p, None, 0).start()
            self.sent(2, p, None, 1).start()

        def forward(self):
            self.sent(1, chip[1], None, 0).wait_recv()
            self.sent(2, chip[1], 0, 2).start()
            self.sent(2, chip[2], None, 1).wait_recv()
            self.sent(1, chip[2], 1, 3).start()

        def arrived(self):
            self.sent(2, chip[3], 0, 2).wait_recv()
            self.sent(1, chip[3], 1, 3).wait_recv()

        def end(self):
            self.sent(1, p, None, 0).wait_send()
            self.sent(2, p, None, 1).wait_send()
            self.sent(2, chip[1], 0, 2).wait_send()
            self.sent(1, chip[2], 1, 3).wait_send()

    own_rows = at(f * own, own, own)
    at_qk = at(p * HK, HK, HK)
    at_v = at(p * HV, HV, HV)
    at_ff = at(p * ffw, last_ff, TILE)
    at_ff_rest = at(p * ffw + last_ff, rest_ff, TILE)
    loads_a = [
        local(q_hbm.at[:, at_qk], WA.at[own_rows, 0:HK]),
        local(k_hbm.at[:, at_qk], WA.at[own_rows, HK : 2 * HK]),
        local(v_hbm.at[:, at_v], WA.at[own_rows, 2 * HK : 2 * HK + HV]),
        local(g_hbm.at[:, at_v], WA.at[own_rows, 2 * HK + HV : cols]),
    ]
    loads_o = [
        local(
            o_hbm.at[pl.ds(pl.multiple_of(64 * i + 32 * h, 32), 32), :],
            WO.at[4 * f + i, h],
        )
        for i in range(CHIPS)
        for h in range(2)
    ]
    loads_f = [
        local(fg_hbm.at[:, at_ff], WG.at[own_rows, 0:last_ff]),
        local(fu_hbm.at[:, at_ff], WU.at[own_rows, 0:last_ff]),
        local(fd_hbm.at[at_ff, :], WD.at[0:last_ff, own_rows]),
    ]
    rest_at = used[1]
    used[1] += 3

    def loads_rest():
        pairs = (
            (fg_hbm.at[:, at_ff_rest], WG.at[own_rows, last_ff:ffw]),
            (fu_hbm.at[:, at_ff_rest], WU.at[own_rows, last_ff:ffw]),
            (fd_hbm.at[at_ff_rest, :], WD.at[last_ff:ffw, own_rows]),
        )
        return [
            pltpu.make_async_copy(src, dst, local_sems.at[rest_at + i])
            for i, (src, dst) in enumerate(pairs)
        ]

    @pl.when(full)
    def _():
        for copy in loads_rest():
            copy.start()

    @pl.when(jnp.logical_not(full))
    def _():
        WG[:, last_ff:ffw] = jnp.zeros((width, rest_ff), low)
        WU[:, last_ff:ffw] = jnp.zeros((width, rest_ff), low)
        WD[last_ff:ffw, :] = jnp.zeros((rest_ff, width), low)

    @pl.when(outer)
    def _():
        GFZ[:, 2] = jnp.zeros((steps, tiles, 32, 3 * TILE), low)
        GAZ[:, 2] = jnp.zeros((2, tiles // 2, 32, ext), low)
        GOZ[2] = jnp.zeros((32, width), low)

    DN[...] = jnp.zeros(DN.shape, low)
    UP[...] = jnp.zeros(UP.shape, low)
    GP[...] = jnp.zeros(GP.shape, wide)
    UB[...] = jnp.zeros(UB.shape, wide)
    SM[f, 0:16, :] = factor_ref[...]
    SM[f, 16:32, 0:HK] = up_in_ref[...]

    def as_row(ref, count):
        row = ref[...].astype(wide).reshape(1, count)
        return row if count == TILE else jnp.concatenate([row, jnp.zeros((1, TILE - count), wide)], axis=1)

    SM[f, 32:48, :] = jnp.concatenate(
        [
            as_row(gain_one_ref, TILE),
            as_row(gain_two_ref, TILE),
            as_row(head_gain_ref, HV // CHIPS),
            as_row(bias_ref, HK),
            jnp.zeros((12, TILE), wide),
        ],
        axis=0,
    ).astype(low)

    barrier = pltpu.get_barrier_semaphore()
    peers = [near] + [chip_dev(j) for j in (1, 2, 3)] + [plane_dev(j) for j in (1, 2, 3)]
    for dev in peers:
        pl.semaphore_signal(barrier, inc=1, device_id=dev, device_id_type=MESH)
    pl.semaphore_wait(barrier, len(peers))

    smalls = [push(SM.at[f], SM.at[f], plane_dev(j)) for j in (1, 2, 3)]
    half_rows = at(c * half, half, half)

    def half_at(fi):
        return at(fi * own + c * half, half, half)

    def columns(ref, first, count, start=0):
        return lambda fi: ref.at[half_at(fi), start : start + count]

    weights_a = Gather(
        [
            (q_hbm.at[half_rows, at_qk], columns(WA, 0, HK)),
            (k_hbm.at[half_rows, at_qk], columns(WA, 0, HK, HK)),
            (v_hbm.at[half_rows, at_v], columns(WA, 0, HV, 2 * HK)),
        ]
    )
    weights_g = Gather([(g_hbm.at[half_rows, at_v], columns(WA, 0, HV, 2 * HK + HV))])
    o_rows = at(64 * p + 32 * c, 32, 32)
    weights_o = Gather([(o_hbm.at[o_rows, :], lambda fi: WO.at[4 * fi + p, c])])
    weights_f = []
    for n in range(steps):
        here = at(p * ffw + n * TILE, TILE, TILE)
        down_here = at(p * ffw + n * TILE + c * ROWS, ROWS, ROWS)
        down_there = at(n * TILE + c * ROWS, ROWS, ROWS)
        weights_f.append(
            Gather(
                [
                    (fg_hbm.at[half_rows, here], columns(WG, 0, TILE, n * TILE)),
                    (fu_hbm.at[half_rows, here], columns(WU, 0, TILE, n * TILE)),
                    (
                        fd_hbm.at[down_here, :],
                        lambda fi, down_there=down_there: WD.at[down_there, at(fi * own, own, own)],
                    ),
                ],
                None if n * TILE < last_ff else full,
            )
        )

    def swap_f(n):
        made = []
        for j in (1, 2, 3):
            for _, view in weights_f[n].parts:
                made.append(push(view(plane[j]), view(plane[j]), near))
        return made

    weights_a.start()
    weights_o.start()

    x = x_ref[...]
    inv_one = lax.rsqrt(jnp.mean(x * x, axis=1, keepdims=True) + norm_eps)
    got(smalls)

    def full_row(row):
        return jnp.concatenate([SM[i, 32:48, :].astype(wide)[row : row + 1] for i in range(CHIPS)], axis=1)

    gain_one = full_row(0)
    gain_two = full_row(1)
    head_gain = jnp.concatenate(
        [SM[i, 32:48, :].astype(wide)[2:3, 0 : HV // CHIPS] for i in range(CHIPS)], axis=1
    )
    bias = SM[p, 32:48, 0:HK][3:4].astype(wide)
    for i in range(CHIPS):
        DN[0:16, i * TILE : (i + 1) * TILE] = SM[i, 0:16, :]
    UP[0:16, :] = SM[p, 16:32, 0:HK]

    mine = at(p * ROWS, ROWS, ROWS)
    H1[mine, :] = (x * inv_one * gain_one).astype(low)
    CT[mine, :] = cot_ref[...].astype(low)
    spread_h1, spread_ct, spread_h2, spread_dr = (Spread(buf) for buf in (H1, CT, H2, DR))
    spread_h1.start()
    spread_h1.forward()
    spread_ct.start()
    weights_a.forward()
    weights_g.start()
    weights_o.forward()
    weights_f[0].start()

    def swap_cols(first, last):
        made = []
        for j in (1, 2, 3):
            here = WA.at[half_at(plane[j]), first:last]
            made.append(push(here, here, near))
        return made

    weights_a.arrived()
    swaps_a = swap_cols(0, 2 * HK + HV)
    for copy in loads_a:
        copy.wait()
    spread_ct.forward()
    spread_h1.arrived()
    weights_g.forward()
    weights_f[1].start()
    got(swaps_a)

    def project(n, carry):
        PJ[n] = nn(H1[...], WA[:, at(n * TILE, TILE, TILE)])
        return carry

    lax.fori_loop(0, (2 * HK + HV) // TILE, project, 0)
    LR[...] = nt(H1[...], DN[...]).astype(low)
    LG[...] = nn(LR[...], UP[...]) + bias

    share_o = []
    weights_o.arrived()
    for j in (1, 2, 3):
        share_o += [
            push(WO.at[4 * plane[j] + p, c], WO.at[4 * plane[j] + p, c], chip_dev(t)) for t in (1, 2, 3)
        ]

    place_t = lax.broadcasted_iota(jnp.int32, (ROWS, ROWS), 0)
    place_s = lax.broadcasted_iota(jnp.int32, (ROWS, ROWS), 1)
    lower = place_t >= place_s
    ones_lower = lower.astype(wide).astype(low)
    ones_upper = (place_t <= place_s).astype(wide).astype(low)

    def block_rows(j):
        return at(j * ROWS, ROWS, ROWS)

    def block_q(rows):
        return PJ[0, rows, 0:HK].astype(low).astype(wide)

    def block_k(rows):
        return PJ[0, rows, HK : 2 * HK].astype(low).astype(wide)

    def block_v(rows):
        return PJ[1, rows, :].astype(low)

    mid = ROWS // 2

    def states(j, carry):
        rows = block_rows(j)
        running = summed_by(ones_lower, jax.nn.log_sigmoid(LG[rows, :]) / logit_norm)
        RU[rows, :] = running
        total = running[ROWS - 1 : ROWS]
        TOT[c, j] = jnp.broadcast_to(total, (8, HK))
        ADD[c, j] = fine_right(tn, block_v(rows), block_k(rows) * jnp.exp(total - running))
        return carry

    lax.fori_loop(0, CHIPS, states, 0)
    sends_state = [push(ADD.at[c], ADD.at[c], near), push(TOT.at[c], TOT.at[c], near)]

    def inside(j, carry):
        rows = block_rows(j)
        running = RU[rows, :]
        middle = running[mid - 1 : mid]
        qd = block_q(rows) * jnp.exp(running - middle)
        kd = block_k(rows) * jnp.exp(middle - running)
        scores = jnp.where(lower, fine_both(nt, qd, kd), 0.0)
        SC[rows, :] = scores
        ATT[rows, :] = fine_left(nn, scores, block_v(rows))
        return carry

    lax.fori_loop(0, CHIPS, inside, 0)

    weights_g.arrived()
    swaps_g = swap_cols(2 * HK + HV, cols)
    got(sends_state)
    state = jnp.zeros((HV, HK), wide)
    for blk in range(2 * CHIPS):
        SS[blk] = state
        state = jnp.exp(TOT[blk % 2, blk // 2, 0:1, :]) * state + ADD[blk % 2, blk // 2]
    SS[2 * CHIPS] = state

    got(swaps_g)
    lax.fori_loop((2 * HK + HV) // TILE, cols // TILE, project, 0)

    def attend(j, carry):
        rows = block_rows(j)
        qs = block_q(rows) * jnp.exp(RU[rows, :])
        att = scale * (ATT[rows, :] + fine_both(nt, qs, SS[2 * j + c]))
        ATT[rows, :] = att
        inv = lax.rsqrt(jnp.mean(att * att, axis=1, keepdims=True) + norm_eps)
        GS[rows, :] = (att * inv * head_gain * jax.nn.silu(PJ[2, rows, :])).astype(low)
        return carry

    lax.fori_loop(0, CHIPS, attend, 0)
    at_head = at(p * HV, HV, HV)
    sends_gated = [
        push(GS.at[at(chip[j] * ROWS, ROWS, ROWS), :], GR.at[:, at_head], chip_dev(j)) for j in (1, 2, 3)
    ]
    GR[:, at_head] = GS[mine, :]

    weights_f[0].forward()
    weights_f[2].start()

    got(share_o)
    swaps_o = []
    for j in (1, 2, 3):
        part = pl.ds(pl.multiple_of(4 * plane[j], 4), 4)
        swaps_o.append(push(WO.at[part, c], WO.at[part, c], near))

    got(sends_gated)
    for copy in loads_o:
        copy.wait()
    got(swaps_o)

    def out_tile(n, carry):
        here = at(n * TILE, TILE, TILE)
        RES[:, here] = x_ref[:, here] + nn(GR[...], WO[:, :, :, here].reshape(width, TILE))
        return carry

    lax.fori_loop(0, tiles, out_tile, 0)
    residual = RES[...]
    inv_two = lax.rsqrt(jnp.mean(residual * residual, axis=1, keepdims=True) + norm_eps)
    H2[mine, :] = (residual * inv_two * gain_two).astype(low)
    spread_h2.start()

    def turn(src, dst):
        def tile(n, carry):
            here = at(n * TILE, TILE, TILE)
            dst[here, :] = src[:, here].T
            return carry

        lax.fori_loop(0, tiles, tile, 0)

    spread_ct.arrived()
    turn(CT, CTT)
    weights_f[0].arrived()
    swaps_f = [swap_f(0)]
    for copy in loads_f:
        copy.wait()

    @pl.when(full)
    def _():
        for copy in loads_rest():
            copy.wait()

    spread_h2.forward()
    spread_h2.arrived()

    def feed(n):
        here = slice(n * TILE, (n + 1) * TILE)
        rows_h2 = H2[...]
        pre_g = nn(rows_h2, WG[:, here])
        pre_u = nn(rows_h2, WU[:, here])
        d_mixed = nt(CT[...], WD[here, :])
        sig = jax.nn.sigmoid(pre_g)
        act = pre_g * sig
        MX[:, here] = (act * pre_u).astype(low)
        DGU[:, here] = (d_mixed * pre_u * (sig * (1.0 + pre_g * (1.0 - sig)))).astype(low)
        DGU[:, ffw + n * TILE : ffw + (n + 1) * TILE] = (d_mixed * act).astype(low)

    def ffn_grads(n):
        here = slice(n * TILE, (n + 1) * TILE)
        there = slice(ffw + n * TILE, ffw + (n + 1) * TILE)

        def tile(m, carry):
            rows = at(m * TILE, TILE, TILE)
            left = H2T[rows, :]
            GF[n, m, :, :, 0:TILE] = nn(left, DGU[:, here]).reshape(2, ROWS, TILE).astype(low)
            GF[n, m, :, :, TILE : 2 * TILE] = nn(left, DGU[:, there]).reshape(2, ROWS, TILE).astype(low)
            GF[n, m, :, :, 2 * TILE :] = nn(CTT[rows, :], MX[:, here]).reshape(2, ROWS, TILE).astype(low)
            return carry

        lax.fori_loop(0, tiles, tile, 0)
        return push(GF.at[n, :, 1 - c], GFC.at[n], near)

    z_ffn = [
        Scatter(
            lambda fi, n=n: GF.at[n, :, c, at(fi * 32, 32, 32), :],
            GFZ.at[n],
            GFL.at[n],
        )
        for n in range(steps)
    ]

    def ffn_out(n, swap):
        swap.wait_recv()

        def tile(m, carry):
            GF[n, m, c] = (GF[n, m, c].astype(wide) + GFC[n, m].astype(wide)).astype(low)
            return carry

        lax.fori_loop(0, tiles, tile, 0)
        z_ffn[n].start()

    weights_f[1].forward()
    got(swaps_f[0])
    feed(0)
    turn(H2, H2T)
    weights_f[1].arrived()
    swaps_f.append(swap_f(1))
    swap_g = [ffn_grads(0)]
    for n in range(1, steps):
        if n + 1 < steps:
            weights_f[n + 1].forward()
        got(swaps_f[n])
        feed(n)
        ffn_out(n - 1, swap_g[n - 1])
        if n + 1 < steps:
            swap_g.append(ffn_grads(n))
            weights_f[n + 1].arrived()
            swaps_f.append(swap_f(n + 1))

    sums_at = [take(6 * tiles) for _ in range(3)]
    low_half, high_half = pl.ds(0, ROWS // 2), pl.ds(ROWS // 2, ROWS // 2)

    def part_copies(kind, n):
        index = sums_at[kind] + 6 * n

        def made(chip_at, part, dst, j, i):
            return remote(SB.at[kind, n, token_rows(chip_at, part), :], dst, chip_dev(j), index + i)

        return [
            made(chip[3], 0, RL.at[kind, 0, n], 1, 0),
            made(chip[3], 1, RL.at[kind, 1, n], 2, 1),
            made(chip[1], 0, RB.at[kind, 0, n, low_half], 1, 2),
            made(chip[2], 1, RB.at[kind, 1, n, high_half], 2, 3),
            made(chip[1], 1, RB.at[kind, 0, n, high_half], 1, 4),
            made(chip[2], 0, RB.at[kind, 1, n, low_half], 2, 5),
        ]

    def send_parts(kind, n):
        for copy in part_copies(kind, n)[:4]:
            copy.start()

    def pass_parts(kind):
        def tile(n, carry):
            copies = part_copies(kind, n)
            for side, rows in ((0, token_rows(chip[2], 0)), (1, token_rows(chip[1], 1))):
                copies[side].wait_recv()
                SB[kind, n, rows, :] = (
                    SB[kind, n, rows, :].astype(wide) + RL[kind, side, n].astype(wide)
                ).astype(low)
                copies[5 - side].start()
            return carry

        lax.fori_loop(0, tiles, tile, 0)

    def part_sum(kind, n):
        for copy in part_copies(kind, n)[2:]:
            copy.wait_recv()
        return (
            SB[kind, n, mine, :].astype(wide)
            + RB[kind, 0, n].astype(wide)
            + RB[kind, 1, n].astype(wide)
        )

    def d_hidden_tile(n, carry):
        rows = at(n * TILE, TILE, TILE)
        SB[0, n] = (nt(DGU[:, 0:ffw], WG[rows, :]) + nt(DGU[:, ffw : 2 * ffw], WU[rows, :])).astype(low)
        send_parts(0, n)
        return carry

    lax.fori_loop(0, tiles, d_hidden_tile, 0)

    swap_g.append(ffn_grads(steps - 1))
    pass_parts(0)

    def y_tile(n, carry):
        SB[1, n] = nn(MX[...], WD[:, at(n * TILE, TILE, TILE)]).astype(low)
        return carry

    lax.fori_loop(0, tiles, y_tile, 0)

    z_ffn[0].forward()
    ffn_out(steps - 1, swap_g[steps - 1])

    d_h2 = jnp.concatenate([part_sum(0, n) for n in range(tiles)], axis=1)
    residual = RES[...]
    inv_two = lax.rsqrt(jnp.mean(residual * residual, axis=1, keepdims=True) + norm_eps)
    unit = residual * inv_two
    pulled = d_h2 * gain_two
    GP[1:2, :] = jnp.sum(d_h2 * unit, axis=0, keepdims=True)
    d_res = cot_ref[...] + inv_two * (pulled - unit * jnp.mean(pulled * unit, axis=1, keepdims=True))
    in_ref[...] = d_res
    d_res_low = d_res.astype(low)
    DR[mine, :] = d_res_low

    def d_gated_tile(n, carry):
        w = WO[pl.ds(pl.multiple_of(4 * n, 4), 4)].reshape(own, width)
        DGS[n] = nt(DR[mine, :], w).astype(low)
        return carry

    lax.fori_loop(0, CHIPS, d_gated_tile, 0)
    sends_dg = [push(DGS.at[chip[j]], DGR.at[mine, :], chip_dev(j)) for j in (1, 2, 3)]
    DGR[mine, :] = DGS[p]

    got(sends_dg)
    z_ffn[1].forward()
    spread_dr.start()

    def through_gate(j, head_sum):
        rows = block_rows(j)
        att = ATT[rows, :]
        inv = lax.rsqrt(jnp.mean(att * att, axis=1, keepdims=True) + norm_eps)
        unit_att = att * inv
        pre = PJ[2, rows, :]
        sig = jax.nn.sigmoid(pre)
        act = pre * sig
        d_gated = DGR[rows, :].astype(wide)
        through = d_gated * unit_att
        DP[rows, 2 * HK + HV : cols] = (through * head_gain * (sig * (1.0 + pre * (1.0 - sig)))).astype(low)
        d_unit = d_gated * head_gain * act
        d_out = scale * inv * (d_unit - unit_att * jnp.mean(d_unit * unit_att, axis=1, keepdims=True))
        DO[rows, :] = d_out
        PUL[c, j] = fine_both(tn, d_out, block_q(rows) * jnp.exp(RU[rows, :]))
        return head_sum + jnp.sum(through * act, axis=0, keepdims=True)

    head_sum = lax.fori_loop(0, CHIPS, through_gate, jnp.zeros((1, HV), wide))
    GP[2:3, 0:HV] = head_sum
    send_pull = push(PUL.at[c], PUL.at[c], near)

    def inside_back(j, carry):
        rows = block_rows(j)
        running = RU[rows, :]
        middle = running[mid - 1 : mid]
        up = jnp.exp(running - middle)
        down = jnp.exp(middle - running)
        qd = block_q(rows) * up
        kd = block_k(rows) * down
        d_out = DO[rows, :]
        d_scores = jnp.where(lower, fine_left(nt, d_out, block_v(rows)), 0.0)
        DQ[rows, :] = up * fine_both(nn, d_scores, kd) + jnp.exp(running) * fine_both(nn, d_out, SS[2 * j + c])
        DK[rows, :] = down * fine_both(tn, d_scores, qd)
        DV[rows, :] = fine_both(tn, SC[rows, :], d_out)
        return carry

    lax.fori_loop(0, CHIPS, inside_back, 0)
    spread_dr.forward()
    send_pull.wait_recv()
    d_state = jnp.zeros((HV, HK), wide)
    for blk in range(2 * CHIPS - 1, -1, -1):
        DS[blk] = d_state
        d_state = jnp.exp(TOT[blk % 2, blk // 2, 0:1, :]) * d_state + PUL[blk % 2, blk // 2]

    def across_back(j, bias_sum):
        rows = block_rows(j)
        running = RU[rows, :]
        to_end = jnp.exp(running[ROWS - 1 : ROWS] - running)
        d_after = DS[2 * j + c]
        k_rows = block_k(rows)
        d_k = DK[rows, :] + to_end * fine_right(nn, block_v(rows), d_after)
        d_v = DV[rows, :] + fine_both(nt, k_rows * to_end, d_after)
        d_q = DQ[rows, :]
        tail = jnp.sum(d_after * SS[2 * j + c + 1], axis=0, keepdims=True)
        d_decay = summed_by(ones_upper, block_q(rows) * d_q - k_rows * d_k) + tail
        d_logits = d_decay * jax.nn.sigmoid(-LG[rows, :]) / logit_norm
        d_logits_low = d_logits.astype(low)
        DL[rows, :] = d_logits_low
        DP[rows, 0:HK] = d_q.astype(low)
        DP[rows, HK : 2 * HK] = d_k.astype(low)
        DP[rows, 2 * HK : 2 * HK + HV] = d_v.astype(low)
        DP[rows, cols:ext] = nt(d_logits_low, UP[...]).astype(low)
        return bias_sum + jnp.sum(d_logits, axis=0, keepdims=True)

    bias_sum = lax.fori_loop(0, CHIPS, across_back, jnp.zeros((1, HK), wide))
    UB[0:16, :] = tn(LR[...], DL[...])[0:16]
    UB[16:17, :] = bias_sum
    send_ub = push(UB, UBC, near)

    z_attn = [
        Scatter(
            lambda fi, i=i: GA.at[i, :, c, at(fi * 32, 32, 32), :],
            GAZ.at[i],
            GAL.at[i],
        )
        for i in range(2)
    ]

    def attn_grads(i):
        for m in range(tiles // 2):
            col = (i * (tiles // 2) + m) * TILE
            GA[i, m] = nn(H1[:, col : col + TILE].T, DP[...]).reshape(2, ROWS, ext).astype(low)
        return push(GA.at[i, :, 1 - c], GAC.at[i], near)

    def attn_out(i, swap):
        swap.wait_recv()
        for m in range(tiles // 2):
            GA[i, m, c] = (GA[i, m, c].astype(wide) + GAC[i, m].astype(wide)).astype(low)
        z_attn[i].start()

    swap_a = [attn_grads(0), attn_grads(1)]
    z_ffn[2].forward()
    attn_out(0, swap_a[0])
    attn_out(1, swap_a[1])

    spread_dr.arrived()

    def out_grad(n, carry):
        here = at(n * TILE, TILE, TILE)
        GO[:, :, here] = tn(GS[...], DR[:, here]).reshape(2, ROWS, TILE).astype(low)
        return carry

    lax.fori_loop(0, tiles, out_grad, 0)
    swap_out = push(GO.at[1 - c], GOC, near)

    def d_input_tile(n, carry):
        rows = at(n * TILE, TILE, TILE)
        SB[2, n] = (nt(DP[:, 0:cols], WA[rows, :]) + nn(DP[:, cols:ext], DN[:, rows])).astype(low)
        send_parts(2, n)
        return carry

    lax.fori_loop(0, tiles, d_input_tile, 0)

    swap_out.wait_recv()
    GO[c] = (GO[c].astype(wide) + GOC[...].astype(wide)).astype(low)
    z_out = Scatter(lambda fi: GO.at[c, at(fi * 32, 32, 32), :], GOZ, GOL)
    z_out.start()
    z_attn[0].forward()
    send_ub.wait_recv()
    UBC[...] = UB[...] + UBC[...]
    z_ub = [push(UBC, UBZ.at[j - 1], plane_dev(j)) for j in (1, 2, 3)]

    pass_parts(2)

    for n in range(tiles):
        send_parts(1, n)

    d_h1 = jnp.concatenate([part_sum(2, n) for n in range(tiles)], axis=1)
    x = x_ref[...]
    inv_one = lax.rsqrt(jnp.mean(x * x, axis=1, keepdims=True) + norm_eps)
    unit_one = x * inv_one
    pulled_one = d_h1 * gain_one
    GP[0:1, :] = jnp.sum(d_h1 * unit_one, axis=0, keepdims=True)
    send_gp = push(GP, GPC, near)
    in_ref[...] += inv_one * (
        pulled_one - unit_one * jnp.mean(pulled_one * unit_one, axis=1, keepdims=True)
    )
    send_gp.wait_recv()
    GPC[...] = GP[...] + GPC[...]
    x_gp = [push(GPC, GPX.at[j - 1], chip_dev(j)) for j in (1, 2, 3)]

    z_attn[1].forward()
    z_out.forward()

    def ffn_done(n):
        z_ffn[n].arrived()
        GFS[n] = z_ffn[n].total().astype(low)
        GFR[p, n] = GFS[n, p]
        return [push(GFS.at[n, chip[j]], GFR.at[p, n], chip_dev(j)) for j in (1, 2, 3)]

    a_ffn = [ffn_done(0)]
    pass_parts(1)
    a_ffn += [ffn_done(n) for n in range(1, steps)]
    got(x_gp)
    GPS[...] = GPC[...] + GPX[0] + GPX[1] + GPX[2]
    z_gp = [push(GPS, GPZ.at[j - 1], plane_dev(j)) for j in (1, 2, 3)]

    for n in range(tiles):
        here = slice(n * TILE, (n + 1) * TILE)
        out_ref[:, here] = RES[:, here] + part_sum(1, n)

    a_attn = []
    for i in range(2):
        z_attn[i].arrived()
        GAS[i * (tiles // 2) : (i + 1) * (tiles // 2)] = z_attn[i].total().astype(low)
    for j in (1, 2, 3):
        a_attn.append(push(GAS.at[chip[j]], GAR.at[p], chip_dev(j)))
    GAR[p] = GAS[p]
    for copies in a_ffn:
        got(copies)
    gf_ref[...] = GFR[...]
    z_out.arrived()
    go_ref[...] = z_out.total()
    got(z_ub)
    ub_ref[...] = UBC[...] + UBZ[0] + UBZ[1] + UBZ[2]
    got(z_gp)
    gains_ref[...] = GPS[...] + GPZ[0] + GPZ[1] + GPZ[2]
    got(a_attn)
    ga_ref[...] = GAR[...]

    for copy in pending:
        copy.wait_send()
    for end in ends:
        end()
    for kind in range(3):
        for n in range(tiles):
            for copy in part_copies(kind, n):
                copy.wait_send()


def finish_kernel(out_in, in_in, go_in, gf, ga, gains, ub, *refs):
    (
        out_ref,
        in_ref,
        attn_gain_ref,
        gq_ref,
        gk_ref,
        gv_ref,
        gg_ref,
        down_ref,
        up_ref,
        bias_ref,
        head_ref,
        go_ref,
        ffn_gain_ref,
        gfg_ref,
        gfu_ref,
        gfd_ref,
    ) = refs
    out_ref[...] = out_in[...]
    in_ref[...] = in_in[...]
    go_ref[...] = go_in[...]
    device = lax.axis_index("seq") * CHIPS + lax.axis_index("fsdp")
    steps = gf.shape[1]
    cols = 2 * HK + 2 * HV
    down_total = jnp.zeros((32, ga.shape[2] - cols), wide)
    for i in range(CHIPS):
        piece = ga[i].astype(wide)
        gq_ref[:, i * HK : (i + 1) * HK] = piece[:, 0:HK]
        gk_ref[:, i * HK : (i + 1) * HK] = piece[:, HK : 2 * HK]
        gv_ref[:, i * HV : (i + 1) * HV] = piece[:, 2 * HK : 2 * HK + HV]
        gg_ref[:, i * HV : (i + 1) * HV] = piece[:, 2 * HK + HV : cols]
        down_total = down_total + piece[:, cols:]
        for n in range(steps):
            first = (i * steps + n) * TILE
            if first < gfg_ref.shape[1]:
                piece_f = gf[i, n].astype(wide)
                gfg_ref[:, first : first + TILE] = piece_f[:, 0:TILE]
                gfu_ref[:, first : first + TILE] = piece_f[:, TILE : 2 * TILE]
                gfd_ref[:, first : first + TILE] = piece_f[:, 2 * TILE :]
    down_ref[...] = down_total.T[0 : down_ref.shape[0], :]

    def lanes(ref, first, count):
        around = ref[:, pl.ds(pl.multiple_of(first // 128 * 128, 128), 128)]
        return pltpu.roll(around, (128 - first % 128) % 128, 1)[:, 0:count]

    gain_part = lanes(gains, device * attn_gain_ref.shape[1], attn_gain_ref.shape[1])
    attn_gain_ref[...] = gain_part[0:1]
    ffn_gain_ref[...] = gain_part[1:2]
    head_ref[...] = lanes(gains, device * head_ref.shape[1], head_ref.shape[1])[2:3]
    up_part = lanes(ub, (device % 8) * up_ref.shape[1], up_ref.shape[1])
    up_ref[...] = up_part[0:16]
    bias_ref[...] = up_part[16:17]


def in_plane(
    block_input,
    attn_gain,
    query_weight,
    key_weight,
    value_weight,
    gate_weight,
    decay_down,
    decay_up,
    decay_bias,
    head_gain,
    out_weight,
    ffn_gain,
    ffn_gate,
    ffn_up,
    ffn_down,
    cotangent,
):
    width = block_input.shape[2]
    ff_full = ffn_gate.shape[1]
    ffw = -(-ff_full // (CHIPS * TILE)) * TILE
    rank = decay_down.shape[1]

    scratch = scratch_of(width, ffw, 128)
    f32 = jax.ShapeDtypeStruct
    outs = pl.pallas_call(
        functools.partial(plane_kernel, tuple(scratch)),
        out_shape=[
            f32((ROWS, width), wide),
            f32((ROWS, width), wide),
            f32((32, width), wide),
            f32(*scratch["GFR"]),
            f32(*scratch["GAR"]),
            f32((8, width), wide),
            f32((24, HK), wide),
        ],
        in_specs=[pl.BlockSpec(memory_space=pltpu.VMEM)] * 8 + [pl.BlockSpec(memory_space=pl.ANY)] * 8,
        out_specs=[pl.BlockSpec(memory_space=pltpu.VMEM)] * 7,
        scratch_shapes=[pltpu.VMEM(shape, kind) for shape, kind in scratch.values()]
        + [
            pltpu.SemaphoreType.DMA((COPIES,)),
            pltpu.SemaphoreType.DMA((COPIES,)),
            pltpu.SemaphoreType.DMA((LOCALS,)),
        ],
        compiler_params=pltpu.CompilerParams(
            collective_id=0, has_side_effects=True, vmem_limit_bytes=62 * 1024 * 1024
        ),
        name="layer_step",
    )(
        decay_down.T,
        decay_up,
        attn_gain,
        ffn_gain,
        head_gain,
        decay_bias,
        block_input[0],
        cotangent[0],
        query_weight,
        key_weight,
        value_weight,
        gate_weight,
        out_weight,
        ffn_gate,
        ffn_up,
        ffn_down,
    )
    each = width // 32
    done = pl.pallas_call(
        finish_kernel,
        out_shape=[
            f32((ROWS, width), wide),
            f32((ROWS, width), wide),
            f32((1, each), wide),
            f32((32, CHIPS * HK), wide),
            f32((32, CHIPS * HK), wide),
            f32((32, CHIPS * HV), wide),
            f32((32, CHIPS * HV), wide),
            f32((rank, 32), wide),
            f32((rank, CHIPS * HK // 32), wide),
            f32((1, CHIPS * HK // 32), wide),
            f32((1, HV // 32), wide),
            f32((32, width), wide),
            f32((1, each), wide),
            f32((32, ff_full), wide),
            f32((32, ff_full), wide),
            f32((32, ff_full), wide),
        ],
        in_specs=[pl.BlockSpec(memory_space=pltpu.VMEM)] * 7,
        out_specs=[pl.BlockSpec(memory_space=pltpu.VMEM)] * 16,
        compiler_params=pltpu.CompilerParams(vmem_limit_bytes=62 * 1024 * 1024),
        name="results",
    )(*outs)
    shapes = {0: (1, ROWS, width), 1: (1, ROWS, width), 2: (-1,), 9: (-1,), 10: (-1,), 12: (-1,)}
    done = [v.reshape(shapes[i]) if i in shapes else v for i, v in enumerate(done)]
    done[7], done[15] = done[7].T, done[15].T
    return tuple(done)


def solution(mesh):
    one_plane = mesh.shape["seq"] == 2 * CHIPS and mesh.shape["fsdp"] == CHIPS
    return jax.shard_map(
        in_plane if one_plane else spread,
        mesh=mesh,
        in_specs=(
            P("fsdp", "seq", None),
            P("fsdp"),
            P("fsdp", None),
            P("fsdp", None),
            P("fsdp", None),
            P("fsdp", None),
            P("fsdp", None),
            P(None, "fsdp"),
            P("fsdp"),
            P("fsdp"),
            P("fsdp", None),
            P("fsdp"),
            P("fsdp", None),
            P("fsdp", None),
            P(None, "fsdp"),
            P("fsdp", "seq", None),
        ),
        out_specs=(
            P("fsdp", "seq", None),
            P("fsdp", "seq", None),
            P(("seq", "fsdp")),
            P(("seq", "fsdp"), None),
            P(("seq", "fsdp"), None),
            P(("seq", "fsdp"), None),
            P(("seq", "fsdp"), None),
            P(("seq", "fsdp"), None),
            P(None, ("seq", "fsdp")),
            P(("seq", "fsdp")),
            P(("seq", "fsdp")),
            P(("seq", "fsdp"), None),
            P(("seq", "fsdp")),
            P(("seq", "fsdp"), None),
            P(("seq", "fsdp"), None),
            P(None, ("seq", "fsdp")),
        ),
        check_vma=False,
    )
```

```python
import functools

import jax
import jax.numpy as jnp
from jax import lax
from jax.experimental import pallas as pl
from jax.experimental.pallas import tpu as pltpu
from jax.sharding import PartitionSpec as P

HK = 128
HV = 256
BLOCK = 64


norm_eps = 1e-06
logit_norm = 16.0
exact = lax.Precision.HIGHEST
fine = lax.Precision.HIGH
low = jnp.bfloat16
wide = jnp.float32


def product(left, right):
    return jnp.dot(left, right, preferred_element_type=wide)


def transposed(left, right):
    return lax.dot_general(left, right, (((0,), (0,)), ((), ())), preferred_element_type=wide)


def against(left, right):
    return lax.dot_general(left, right, (((1,), (1,)), ((), ())), preferred_element_type=wide)


def fine_dot(spec, left, right):
    return jnp.einsum(spec, left, right, precision=fine, preferred_element_type=wide)


def rms_gain(token_rows, gain_row):
    return (
        token_rows
        * lax.rsqrt(jnp.mean(token_rows * token_rows, axis=-1, keepdims=True) + norm_eps)
        * gain_row
    )


def gated_norm(attended, gate_pre, head_gain):
    return rms_gain(attended, head_gain) * jax.nn.silu(gate_pre)


def swiglu(gate_part, up_part):
    return jax.nn.silu(gate_part) * up_part


def exchange(pieces):
    return lax.all_to_all(pieces, "fsdp", 0, 0)


def gather_rows(rows):
    return lax.all_gather(rows, "fsdp", axis=0, tiled=True)


def scatter_rows(rows):
    return lax.psum_scatter(rows.astype(low), "fsdp", scatter_dimension=0, tiled=True).astype(wide)


def summed_rows(grads):
    return lax.psum_scatter(grads.astype(low), "seq", scatter_dimension=0, tiled=True)


def owned_columns(section, parts):
    return exchange(section.reshape(parts, section.shape[0] // parts, -1))


def across(pieces):
    rows = pieces.shape[1]
    return pieces.transpose(1, 0, 2).reshape(rows, -1).astype(wide)


def spread(
    block_input,
    attn_gain,
    query_weight,
    key_weight,
    value_weight,
    gate_weight,
    decay_down,
    decay_up,
    decay_bias,
    head_gain,
    out_weight,
    ffn_gain,
    ffn_gate,
    ffn_up,
    ffn_down,
    cotangent,
):
    shards, parts = lax.axis_size("seq"), lax.axis_size("fsdp")
    si = lax.axis_index("seq")
    x = block_input[0]
    cot_rows = cotangent[0]
    length, width = x.shape
    blocks = length // BLOCK
    scale = HK ** (-0.5)

    small = jnp.concatenate([attn_gain, ffn_gain, head_gain, decay_down.reshape(-1)])
    small = exchange(jnp.broadcast_to(small[None], (parts, small.shape[0])))
    own = attn_gain.shape[0]
    own_head = head_gain.shape[0]
    gain_one = small[:, :own].reshape(-1).astype(wide)
    gain_two = small[:, own : 2 * own].reshape(-1).astype(wide)
    gain_head = small[:, 2 * own : 2 * own + own_head].reshape(-1).astype(wide)
    down_full = small[:, 2 * own + own_head :].reshape(width, -1)
    rank = down_full.shape[1]

    normed_one, norm_one_back = jax.vjp(rms_gain, x, gain_one)
    both = gather_rows(jnp.concatenate([normed_one.astype(low), cot_rows.astype(low)], axis=1))
    hidden_one = both[:, :width]
    cot_low = both[:, width:]
    ff = ffn_gate.shape[1] // parts
    rows = own // shards
    down_rows = ff // shards
    cuts = [
        lax.dynamic_slice_in_dim(w, si * rows, rows, 0).reshape(rows, parts, -1).transpose(1, 0, 2)
        for w in (query_weight, key_weight, value_weight, gate_weight, ffn_gate, ffn_up)
    ]
    cuts.append(
        lax.dynamic_slice_in_dim(
            ffn_down.reshape(parts, ff, own), si * down_rows, down_rows, 1
        ).reshape(parts, rows, -1)
    )
    got = lax.all_gather(exchange(jnp.concatenate(cuts, axis=2)), "seq")
    attn_columns = 2 * HK + 2 * HV
    attn_w = got[..., :attn_columns].transpose(1, 0, 2, 3).reshape(width, -1)
    ffn_w = (
        got[..., attn_columns : attn_columns + 2 * ff].transpose(1, 0, 2, 3).reshape(width, -1)
    )
    down_w = (
        got[..., attn_columns + 2 * ff :]
        .reshape(shards, parts, down_rows, own)
        .transpose(0, 2, 1, 3)
        .reshape(ff, width)
    )

    projected = product(hidden_one, attn_w)
    rounded = projected[:, : 2 * HK + HV].astype(low)
    gate_pre = projected[:, 2 * HK + HV :]
    low_rank = product(hidden_one, down_full).astype(low)
    logits = product(low_rank, decay_up) + decay_bias.astype(wide)
    log_decay = jax.nn.log_sigmoid(logits) / logit_norm

    def chunked(rows):
        return rows.reshape(parts * blocks, BLOCK, -1)

    q = chunked(rounded[:, :HK].astype(wide))
    k = chunked(rounded[:, HK : 2 * HK].astype(wide))
    v = chunked(rounded[:, 2 * HK :].astype(wide))
    place = jnp.arange(BLOCK)
    lower = place[:, None] >= place[None, :]
    ones_lower = lower.astype(wide)
    running = jnp.einsum("ts,bsk->btk", ones_lower, chunked(log_decay), precision=exact)
    total = running[:, -1]
    grown = jnp.exp(running)
    shrunk = jnp.exp(-running)
    to_end = jnp.exp(total[:, None] - running)
    qd = q * grown
    kd = k * shrunk
    kf = k * to_end
    scores = jnp.where(lower[None], fine_dot("btk,bsk->bts", qd, kd), 0.0)
    intra = fine_dot("bts,bsv->btv", scores, v)
    added = fine_dot("bsk,bsv->bkv", kf, v)
    added_c = added.reshape(parts, blocks, HK, HV)
    total_c = total.reshape(parts, blocks, HK)
    factor_c = jnp.exp(total_c)[..., None]
    local_state = added_c[:, 0]
    for c in range(1, blocks):
        local_state = factor_c[:, c] * local_state + added_c[:, c]
    totals = lax.all_gather(jnp.sum(total_c, axis=1), "seq")
    states = lax.all_gather(local_state.astype(low), "seq")
    index = jnp.arange(shards)
    upto = jnp.cumsum(totals, axis=0)
    mine_upto = lax.dynamic_index_in_dim(upto, si, 0, False)
    mine_total = lax.dynamic_index_in_dim(totals, si, 0, False)
    before = (index < si)[:, None, None]
    after = (index > si)[:, None, None]
    early = jnp.where(before, jnp.exp(jnp.where(before, mine_upto - mine_total - upto, 0.0)), 0.0)
    late = jnp.where(
        after, jnp.exp(jnp.where(after, upto - totals - mine_upto, 0.0)), 0.0
    )
    incoming = jnp.sum(early[..., None] * states.astype(wide), axis=0)
    entering = [incoming]
    for c in range(blocks):
        entering.append(factor_c[:, c] * entering[-1] + added_c[:, c])
    state_in = jnp.stack(entering[:-1], axis=1).reshape(parts * blocks, HK, HV)
    state_out = jnp.stack(entering[1:], axis=1).reshape(parts * blocks, HK, HV)
    attended = scale * (intra + fine_dot("btk,bkv->btv", qd, state_in))
    attended = attended.reshape(parts * length, HV)

    gated, gated_back = jax.vjp(gated_norm, attended, gate_pre, gain_head)
    gated_low = gated.astype(low)
    residual = x + scatter_rows(product(gated_low, out_weight))
    normed_two, norm_two_back = jax.vjp(rms_gain, residual, gain_two)
    hidden_two = gather_rows(normed_two.astype(low))
    pre = product(hidden_two, ffn_w)
    mixed, mixed_back = jax.vjp(swiglu, pre[:, :ff], pre[:, ff:])
    mixed_low = mixed.astype(low)
    d_gate_part, d_up_part = mixed_back(against(cot_low, down_w))
    d_pre = jnp.concatenate([d_gate_part.astype(low), d_up_part.astype(low)], axis=1)
    both = scatter_rows(
        jnp.concatenate(
            [against(d_pre, ffn_w).astype(low), product(mixed_low, down_w).astype(low)], axis=1
        )
    )
    d_residual_norm, grad_ffn_gain = norm_two_back(both[:, :width])
    d_residual = cot_rows + d_residual_norm
    d_res_low = gather_rows(d_residual.astype(low))
    block_output = residual + both[:, width:]
    ffn_section = summed_rows(
        jnp.concatenate(
            [transposed(hidden_two, d_pre).astype(low), transposed(cot_low, mixed_low).astype(low)],
            axis=1,
        )
    )
    ffn_owned = owned_columns(ffn_section, parts)

    d_attended, d_gate_pre, grad_head_gain = gated_back(against(d_res_low, out_weight))
    d_out = chunked(scale * d_attended)
    pulled = fine_dot("btk,btv->bkv", qd, d_out)
    pulled_c = pulled.reshape(parts, blocks, HK, HV)
    local_pull = pulled_c[:, blocks - 1]
    for c in range(blocks - 2, -1, -1):
        local_pull = factor_c[:, c] * local_pull + pulled_c[:, c]
    pulls = lax.all_gather(local_pull.astype(low), "seq")
    later = jnp.sum(late[..., None] * pulls.astype(wide), axis=0)
    leaving = [later]
    for c in range(blocks - 1, 0, -1):
        leaving.insert(0, factor_c[:, c] * leaving[0] + pulled_c[:, c])
    d_state = jnp.stack(leaving, axis=1).reshape(parts * blocks, HK, HV)
    d_scores = jnp.where(lower[None], fine_dot("btv,bsv->bts", d_out, v), 0.0)
    d_q = grown * (
        fine_dot("bts,bsk->btk", d_scores, kd) + fine_dot("btv,bkv->btk", d_out, state_in)
    )
    d_k = shrunk * fine_dot("bts,btk->bsk", d_scores, qd) + to_end * fine_dot(
        "bsv,bkv->bsk", v, d_state
    )
    d_v = fine_dot("bts,btv->bsv", scores, d_out) + fine_dot("bsk,bkv->bsv", kf, d_state)
    tail_term = jnp.sum(d_state * state_out, axis=2)
    d_log_decay = (
        jnp.einsum("st,bsk->btk", ones_lower, q * d_q - k * d_k, precision=exact)
        + tail_term[:, None]
    )
    d_logits = d_log_decay.reshape(parts * length, HK) * jax.nn.sigmoid(-logits) / logit_norm
    grad_decay_bias = jnp.sum(d_logits, axis=0)
    d_logits_low = d_logits.astype(low)
    grad_decay_up = transposed(low_rank, d_logits_low)
    d_low_rank = against(d_logits_low, decay_up).astype(low)
    grad_decay_down = transposed(hidden_one, d_low_rank)
    d_projected = jnp.concatenate(
        [
            d_q.reshape(parts * length, HK).astype(low),
            d_k.reshape(parts * length, HK).astype(low),
            d_v.reshape(parts * length, HV).astype(low),
            d_gate_pre.astype(low),
        ],
        axis=1,
    )
    d_hidden_one = scatter_rows(against(d_projected, attn_w) + against(d_low_rank, down_full))
    d_input_norm, grad_attn_gain = norm_one_back(d_hidden_one)
    input_grad = d_residual + d_input_norm
    devices = shards * parts
    grad_out = transposed(gated_low, d_res_low).astype(low)
    attn_section = summed_rows(
        jnp.concatenate(
            [transposed(hidden_one, d_projected).astype(low), grad_out.reshape(width, HV)], axis=1
        )
    )
    attn_owned = owned_columns(attn_section[:, :attn_columns], parts)
    turned = [(s * parts + f, f * shards + s) for s in range(shards) for f in range(parts)]
    own_out = lax.ppermute(
        attn_section[:, attn_columns:].reshape(-1, width), ("seq", "fsdp"), turned
    ).astype(wide)
    head_part = jnp.concatenate(
        [
            grad_decay_up.reshape(rank, shards, -1).transpose(1, 0, 2).reshape(shards, -1),
            grad_decay_bias.reshape(shards, -1),
        ],
        axis=1,
    )
    mine = jnp.arange(parts)[:, None, None] == lax.axis_index("fsdp")
    head_part = jnp.where(mine, head_part[None], 0.0).reshape(devices, -1)
    own_bias_size = HK // shards
    summed = jnp.concatenate(
        [
            grad_attn_gain.reshape(devices, -1),
            grad_ffn_gain.reshape(devices, -1),
            grad_head_gain.reshape(devices, -1),
            grad_decay_down.reshape(devices, -1),
            head_part,
        ],
        axis=1,
    )
    summed = jnp.sum(lax.all_to_all(summed, ("seq", "fsdp"), 0, 0), axis=0)
    each = width // devices
    each_head = HV // devices
    own_attn_gain = summed[:each]
    own_ffn_gain = summed[each : 2 * each]
    own_head_gain = summed[2 * each : 2 * each + each_head]
    at_up = 2 * each + each_head + each * rank
    at_bias = at_up + rank * own_bias_size
    own_down = summed[2 * each + each_head : at_up].reshape(each, rank)
    own_up = summed[at_up:at_bias].reshape(rank, own_bias_size)
    own_bias = summed[at_bias:]
    return (
        block_output[None],
        input_grad[None],
        own_attn_gain,
        across(attn_owned[:, :, :HK]),
        across(attn_owned[:, :, HK : 2 * HK]),
        across(attn_owned[:, :, 2 * HK : 2 * HK + HV]),
        across(attn_owned[:, :, 2 * HK + HV :]),
        own_down,
        own_up,
        own_bias,
        own_head_gain,
        own_out,
        own_ffn_gain,
        across(ffn_owned[:, :, :ff]),
        across(ffn_owned[:, :, ff : 2 * ff]),
        across(ffn_owned[:, :, 2 * ff :]).T,
    )


MESH = pl.DeviceIdType.MESH
CHIPS = 4
ROWS = 128
TILE = 256


def nn(left, right):
    return lax.dot_general(left, right, (((1,), (0,)), ((), ())), preferred_element_type=wide)


def nt(left, right):
    return lax.dot_general(left, right, (((1,), (1,)), ((), ())), preferred_element_type=wide)


def tn(left, right):
    return lax.dot_general(left, right, (((0,), (0,)), ((), ())), preferred_element_type=wide)


def halves(values):
    top = values.astype(low)
    return top, (values - top.astype(wide)).astype(low)


def fine_both(op, left, right):
    lh, ll = halves(left)
    rh, rl = halves(right)
    return op(lh, rh) + (op(lh, rl) + op(ll, rh))


def fine_left(op, left, right):
    lh, ll = halves(left)
    return op(lh, right) + op(ll, right)


def fine_right(op, left, right):
    rh, rl = halves(right)
    return op(left, rh) + op(left, rl)


def summed_by(ones, values):
    top, rest = halves(values)
    mid = (values - top.astype(wide)).astype(low)
    last = (values - top.astype(wide) - mid.astype(wide)).astype(low)
    return nn(ones, top) + (nn(ones, mid) + nn(ones, last))


def at(start, size, unit):
    return pl.ds(pl.multiple_of(start, unit), size)


def scratch_of(width, ffw, rank_pad):
    tokens = CHIPS * ROWS
    attn_cols = 2 * HK + 2 * HV
    ext = attn_cols + rank_pad
    tiles = width // TILE
    steps = ffw // TILE
    return {
        "SM": ((CHIPS, 48, TILE), low),
        "WA": ((width, attn_cols), low),
        "WO": ((4 * CHIPS, 2, 32, width), low),
        "WG": ((width, ffw), low),
        "WU": ((width, ffw), low),
        "WD": ((ffw, width), low),
        "DN": ((rank_pad, width), low),
        "UP": ((rank_pad, HK), low),
        "H1": ((tokens, width), low),
        "CT": ((tokens, width), low),
        "H2": ((tokens, width), low),
        "DR": ((tokens, width), low),
        "PJ": ((3, tokens, TILE), wide),
        "LG": ((tokens, HK), wide),
        "LR": ((tokens, rank_pad), low),
        "RU": ((tokens, HK), wide),
        "SC": ((tokens, ROWS), wide),
        "ADD": ((2, CHIPS, HV, HK), wide),
        "PUL": ((2, CHIPS, HV, HK), wide),
        "TOT": ((2, CHIPS, 8, HK), wide),
        "SS": ((2 * CHIPS + 1, HV, HK), wide),
        "DS": ((2 * CHIPS, HV, HK), wide),
        "ATT": ((tokens, HV), wide),
        "GS": ((tokens, HV), low),
        "GR": ((ROWS, width), low),
        "RES": ((ROWS, width), wide),
        "MX": ((tokens, ffw), low),
        "DGU": ((tokens, 2 * ffw), low),
        "SB": ((3, tiles, tokens, TILE), low),
        "RB": ((3, 2, tiles, ROWS, TILE), low),
        "RL": ((3, 2, tiles, ROWS // 2, TILE), low),
        "DGS": ((CHIPS, ROWS, HV), low),
        "DGR": ((tokens, HV), low),
        "DO": ((tokens, HV), wide),
        "DQ": ((tokens, HK), wide),
        "DK": ((tokens, HK), wide),
        "DV": ((tokens, HV), wide),
        "DL": ((tokens, HK), low),
        "DP": ((tokens, ext), low),
        "H2T": ((width, tokens), low),
        "CTT": ((width, tokens), low),
        "GF": ((steps, tiles, 2, ROWS, 3 * TILE), low),
        "GFC": ((steps, tiles, ROWS, 3 * TILE), low),
        "GFZ": ((steps, 3, tiles, 32, 3 * TILE), low),
        "GFL": ((steps, tiles, 32, 3 * TILE), low),
        "GFS": ((steps, tiles, 32, 3 * TILE), low),
        "GFR": ((CHIPS, steps, 32, 3 * TILE), low),
        "GA": ((2, tiles // 2, 2, ROWS, ext), low),
        "GAC": ((2, tiles // 2, ROWS, ext), low),
        "GAZ": ((2, 3, tiles // 2, 32, ext), low),
        "GAL": ((2, tiles // 2, 32, ext), low),
        "GAS": ((tiles, 32, ext), low),
        "GAR": ((CHIPS, 32, ext), low),
        "GO": ((2, ROWS, width), low),
        "GOC": ((ROWS, width), low),
        "GOZ": ((3, 32, width), low),
        "GOL": ((32, width), low),
        "GP": ((8, width), wide),
        "GPC": ((8, width), wide),
        "GPX": ((3, 8, width), wide),
        "GPZ": ((3, 8, width), wide),
        "GPS": ((8, width), wide),
        "UB": ((24, HK), wide),
        "UBC": ((24, HK), wide),
        "UBZ": ((3, 24, HK), wide),
    }


COPIES = 320
LOCALS = 24


def plane_kernel(names, *refs):
    (factor_ref, up_in_ref, gain_one_ref, gain_two_ref, head_gain_ref, bias_ref) = refs[:6]
    (x_ref, cot_ref, q_hbm, k_hbm, v_hbm, g_hbm, o_hbm, fg_hbm, fu_hbm, fd_hbm) = refs[6:16]
    (out_ref, in_ref, go_ref, gf_ref, ga_ref, gains_ref, ub_ref) = refs[16:23]
    b = dict(zip(names, refs[23 : 23 + len(names)]))
    send_sems, recv_sems, local_sems = refs[23 + len(names) :]
    SM, WA, WO, WG, WU, WD, DN, UP = (b[n] for n in ("SM", "WA", "WO", "WG", "WU", "WD", "DN", "UP"))
    H1, CT, H2, DR, PJ, LG, LR, RU, SC = (
        b[n] for n in ("H1", "CT", "H2", "DR", "PJ", "LG", "LR", "RU", "SC")
    )
    ADD, PUL, TOT, SS, DS, ATT, GS, GR, RES = (
        b[n] for n in ("ADD", "PUL", "TOT", "SS", "DS", "ATT", "GS", "GR", "RES")
    )
    MX, DGU, SB, RB, DGS, DGR, DO, DQ, DK, DV, DL, DP = (
        b[n] for n in ("MX", "DGU", "SB", "RB", "DGS", "DGR", "DO", "DQ", "DK", "DV", "DL", "DP")
    )
    GP, GPC, GPX, GPZ, GPS, UB, UBC, UBZ = (
        b[n] for n in ("GP", "GPC", "GPX", "GPZ", "GPS", "UB", "UBC", "UBZ")
    )
    GO, GOC, GOZ, GOL = (b[n] for n in ("GO", "GOC", "GOZ", "GOL"))
    H2T, CTT, RL = b["H2T"], b["CTT"], b["RL"]
    GF, GFC, GFZ, GFL, GFS, GFR = (b[n] for n in ("GF", "GFC", "GFZ", "GFL", "GFS", "GFR"))
    GA, GAC, GAZ, GAL, GAS, GAR = (b[n] for n in ("GA", "GAC", "GAZ", "GAL", "GAS", "GAR"))
    width = x_ref.shape[1]
    tokens = H1.shape[0]
    tiles = width // TILE
    ffw = WG.shape[1]
    steps = ffw // TILE
    last_ff = fg_hbm.shape[1] - (CHIPS - 1) * ffw
    rest_ff = ffw - last_ff
    ext = DP.shape[1]
    cols = 2 * HK + 2 * HV
    own = width // 4
    half = own // 2
    scale = HK ** (-0.5)

    s = lax.axis_index("seq")
    f = lax.axis_index("fsdp")
    p = s // 2
    c = s % 2
    chip = (None, p + 1 - 2 * (p % 2), (p + 2) % 4, 3 - p)
    plane = (None, f + 1 - 2 * (f % 2), (f + 2) % 4, 3 - f)
    near = (s + 1 - 2 * c, f)
    full = p < CHIPS - 1
    inner = (f > 0) & (f < 3)
    outer = jnp.logical_not(inner)

    used = [0, 0]
    pending = []

    def take(count=1):
        first = used[0]
        used[0] += count
        return first

    def remote(src, dst, dev, index, landed=None):
        return pltpu.make_async_remote_copy(
            src_ref=src,
            dst_ref=dst,
            send_sem=send_sems.at[index],
            recv_sem=recv_sems.at[index if landed is None else landed],
            device_id=dev,
            device_id_type=MESH,
        )

    def chip_dev(j):
        return (2 * chip[j] + c, f)

    def plane_dev(j):
        return (s, plane[j])

    def push(src, dst, dev):
        copy = remote(src, dst, dev, take())
        copy.start()
        pending.append(copy)
        return copy

    def local(src, dst):
        copy = pltpu.make_async_copy(src, dst, local_sems.at[used[1]])
        used[1] += 1
        copy.start()
        return copy

    def got(copies):
        for copy in copies:
            copy.wait_recv()

    ends = []

    def when(conds, action):
        conds = [cond for cond in conds if cond is not None]

        def run():
            action()

        if not conds:
            run()
            return
        both = conds[0]
        for cond in conds[1:]:
            both = both & cond
        pl.when(both)(run)

    class Gather:
        def __init__(self, parts, cond=None):
            self.parts, self.cond, self.count = parts, cond, len(parts)
            self.first, self.passed = take(3 * len(parts)), take(len(parts))
            ends.append(self.end)

        def copies(self, j, source=None):
            made = []
            for i, (src, view) in enumerate(self.parts):
                index = self.first + (j - 1) * self.count + i
                if source is None:
                    made.append(remote(src, view(f), plane_dev(j), index))
                else:
                    made.append(remote(view(source), view(source), plane_dev(j), index))
            return made

        def handed(self):
            return [
                remote(
                    view(plane[2]),
                    view(plane[2]),
                    plane_dev(1),
                    self.passed + i,
                    self.first + 2 * self.count + i,
                )
                for i, (_, view) in enumerate(self.parts)
            ]

        def start(self):
            when([self.cond], lambda: [copy.start() for j in (2, 1) for copy in self.copies(j)])
            when([self.cond, inner], lambda: [copy.start() for copy in self.copies(3)])

        def landed(self, j):
            for copy in self.copies(j, plane[j]):
                copy.wait_recv()

        def forward(self):
            def action():
                self.landed(2)
                for copy in self.handed():
                    copy.start()

            when([self.cond, inner], action)

        def arrived(self):
            when([self.cond], lambda: self.landed(1))
            when([self.cond, outer], lambda: self.landed(2))
            when([self.cond], lambda: self.landed(3))

        def end(self):
            when([self.cond], lambda: [copy.wait_send() for j in (1, 2) for copy in self.copies(j)])
            when(
                [self.cond, inner],
                lambda: [copy.wait_send() for copy in self.copies(3) + self.handed()],
            )

    class Scatter:
        def __init__(self, block, landing, relay):
            self.block, self.landing, self.relay = block, landing, relay
            self.first, self.extra = take(3), take(1)
            ends.append(self.end)

        def copy(self, j):
            return remote(self.block(plane[j]), self.landing.at[j - 1], plane_dev(j), self.first + j - 1)

        def aside(self):
            return remote(self.block(plane[3]), self.relay, plane_dev(1), self.extra)

        def start(self):
            when([outer], lambda: [self.aside().start(), self.copy(2).start()])
            self.copy(1).start()
            when([inner], lambda: self.copy(3).start())

        def forward(self):
            def action():
                self.aside().wait_recv()
                mine_too = self.block(plane[2])
                mine_too[...] = (mine_too[...].astype(wide) + self.relay[...].astype(wide)).astype(low)
                self.copy(2).start()

            when([inner], action)

        def arrived(self):
            self.copy(1).wait_recv()
            self.copy(2).wait_recv()
            when([inner], lambda: self.copy(3).wait_recv())

        def total(self):
            kept = self.block(f)[...].astype(wide)
            return kept + (
                self.landing[0].astype(wide) + self.landing[1].astype(wide) + self.landing[2].astype(wide)
            )

        def end(self):
            self.copy(1).wait_send()
            self.copy(2).wait_send()
            when([inner], lambda: self.copy(3).wait_send())
            when([outer], lambda: self.aside().wait_send())

    def token_rows(chip_at, part=None):
        if part is None:
            return at(chip_at * ROWS, ROWS, ROWS)
        return at(chip_at * ROWS + part * (ROWS // 2), ROWS // 2, ROWS // 2)

    class Spread:
        def __init__(self, buf):
            self.buf, self.first = buf, take(4)
            ends.append(self.end)

        def sent(self, j, chip_at, part=None, index=0):
            here = self.buf.at[token_rows(chip_at, part), :]
            return remote(here, here, chip_dev(j), self.first + index)

        def start(self):
            self.sent(1, p, None, 0).start()
            self.sent(2, p, None, 1).start()

        def forward(self):
            self.sent(1, chip[1], None, 0).wait_recv()
            self.sent(2, chip[1], 0, 2).start()
            self.sent(2, chip[2], None, 1).wait_recv()
            self.sent(1, chip[2], 1, 3).start()

        def arrived(self):
            self.sent(2, chip[3], 0, 2).wait_recv()
            self.sent(1, chip[3], 1, 3).wait_recv()

        def end(self):
            self.sent(1, p, None, 0).wait_send()
            self.sent(2, p, None, 1).wait_send()
            self.sent(2, chip[1], 0, 2).wait_send()
            self.sent(1, chip[2], 1, 3).wait_send()

    own_rows = at(f * own, own, own)
    at_qk = at(p * HK, HK, HK)
    at_v = at(p * HV, HV, HV)
    at_ff = at(p * ffw, last_ff, TILE)
    at_ff_rest = at(p * ffw + last_ff, rest_ff, TILE)
    @pl.when(jnp.logical_not(full))
    def _():
        WG[:, last_ff:ffw] = jnp.zeros((width, rest_ff), low)
        WU[:, last_ff:ffw] = jnp.zeros((width, rest_ff), low)
        WD[last_ff:ffw, :] = jnp.zeros((rest_ff, width), low)

    SM[f, 0:16, :] = factor_ref[...]
    SM[f, 16:32, 0:HK] = up_in_ref[...]

    def as_row(ref, count):
        row = ref[...].astype(wide).reshape(1, count)
        return row if count == TILE else jnp.concatenate([row, jnp.zeros((1, TILE - count), wide)], axis=1)

    SM[f, 32:48, :] = jnp.concatenate(
        [
            as_row(gain_one_ref, TILE),
            as_row(gain_two_ref, TILE),
            as_row(head_gain_ref, HV // CHIPS),
            as_row(bias_ref, HK),
            jnp.zeros((12, TILE), wide),
        ],
        axis=0,
    ).astype(low)

    barrier = pltpu.get_barrier_semaphore()
    peers = [near] + [chip_dev(j) for j in (1, 2, 3)] + [plane_dev(j) for j in (1, 2, 3)]
    for dev in peers:
        pl.semaphore_signal(barrier, inc=1, device_id=dev, device_id_type=MESH)
    pl.semaphore_wait(barrier, len(peers))

    smalls = [push(SM.at[f], SM.at[f], plane_dev(j)) for j in (1, 2, 3)]
    half_rows = at(c * half, half, half)

    def half_at(fi):
        return at(fi * own + c * half, half, half)

    def columns(ref, first, count, start=0):
        return lambda fi: ref.at[half_at(fi), start : start + count]

    weights_a = Gather(
        [
            (q_hbm.at[half_rows, at_qk], columns(WA, 0, HK)),
            (k_hbm.at[half_rows, at_qk], columns(WA, 0, HK, HK)),
            (v_hbm.at[half_rows, at_v], columns(WA, 0, HV, 2 * HK)),
        ]
    )
    weights_g = Gather([(g_hbm.at[half_rows, at_v], columns(WA, 0, HV, 2 * HK + HV))])
    o_rows = at(64 * p + 32 * c, 32, 32)
    weights_o = Gather([(o_hbm.at[o_rows, :], lambda fi: WO.at[4 * fi + p, c])])
    weights_f = []
    for n in range(steps):
        here = at(p * ffw + n * TILE, TILE, TILE)
        down_here = at(p * ffw + n * TILE + c * ROWS, ROWS, ROWS)
        down_there = at(n * TILE + c * ROWS, ROWS, ROWS)
        weights_f.append(
            Gather(
                [
                    (fg_hbm.at[half_rows, here], columns(WG, 0, TILE, n * TILE)),
                    (fu_hbm.at[half_rows, here], columns(WU, 0, TILE, n * TILE)),
                    (
                        fd_hbm.at[down_here, :],
                        lambda fi, down_there=down_there: WD.at[down_there, at(fi * own, own, own)],
                    ),
                ],
                None if n * TILE < last_ff else full,
            )
        )

    def swap_f(n):
        made = []
        for j in (1, 2, 3):
            for _, view in weights_f[n].parts:
                made.append(push(view(plane[j]), view(plane[j]), near))
        return made

    weights_a.start()
    weights_o.start()

    loads_a = [
        local(q_hbm.at[:, at_qk], WA.at[own_rows, 0:HK]),
        local(k_hbm.at[:, at_qk], WA.at[own_rows, HK : 2 * HK]),
        local(v_hbm.at[:, at_v], WA.at[own_rows, 2 * HK : 2 * HK + HV]),
        local(g_hbm.at[:, at_v], WA.at[own_rows, 2 * HK + HV : cols]),
    ]
    loads_o = [
        local(
            o_hbm.at[pl.ds(pl.multiple_of(64 * i + 32 * h, 32), 32), :],
            WO.at[4 * f + i, h],
        )
        for i in range(CHIPS)
        for h in range(2)
    ]
    loads_f = [
        local(fg_hbm.at[:, at_ff], WG.at[own_rows, 0:last_ff]),
        local(fu_hbm.at[:, at_ff], WU.at[own_rows, 0:last_ff]),
        local(fd_hbm.at[at_ff, :], WD.at[0:last_ff, own_rows]),
    ]
    rest_at = used[1]
    used[1] += 3

    def loads_rest():
        pairs = (
            (fg_hbm.at[:, at_ff_rest], WG.at[own_rows, last_ff:ffw]),
            (fu_hbm.at[:, at_ff_rest], WU.at[own_rows, last_ff:ffw]),
            (fd_hbm.at[at_ff_rest, :], WD.at[last_ff:ffw, own_rows]),
        )
        return [
            pltpu.make_async_copy(src, dst, local_sems.at[rest_at + i])
            for i, (src, dst) in enumerate(pairs)
        ]

    @pl.when(full)
    def _():
        for copy in loads_rest():
            copy.start()

    @pl.when(outer)
    def _():
        GFZ[:, 2] = jnp.zeros((steps, tiles, 32, 3 * TILE), low)
        GAZ[:, 2] = jnp.zeros((2, tiles // 2, 32, ext), low)
        GOZ[2] = jnp.zeros((32, width), low)

    DN[...] = jnp.zeros(DN.shape, low)
    UP[...] = jnp.zeros(UP.shape, low)
    GP[...] = jnp.zeros(GP.shape, wide)
    UB[...] = jnp.zeros(UB.shape, wide)

    x = x_ref[...]
    inv_one = lax.rsqrt(jnp.mean(x * x, axis=1, keepdims=True) + norm_eps)
    got(smalls)

    def full_row(row):
        return jnp.concatenate([SM[i, 32:48, :].astype(wide)[row : row + 1] for i in range(CHIPS)], axis=1)

    gain_one = full_row(0)
    gain_two = full_row(1)
    head_gain = jnp.concatenate(
        [SM[i, 32:48, :].astype(wide)[2:3, 0 : HV // CHIPS] for i in range(CHIPS)], axis=1
    )
    bias = SM[p, 32:48, 0:HK][3:4].astype(wide)
    for i in range(CHIPS):
        DN[0:16, i * TILE : (i + 1) * TILE] = SM[i, 0:16, :]
    UP[0:16, :] = SM[p, 16:32, 0:HK]

    mine = at(p * ROWS, ROWS, ROWS)
    H1[mine, :] = (x * inv_one * gain_one).astype(low)
    CT[mine, :] = cot_ref[...].astype(low)
    spread_h1, spread_ct, spread_h2, spread_dr = (Spread(buf) for buf in (H1, CT, H2, DR))
    spread_h1.start()
    spread_h1.forward()
    spread_ct.start()
    weights_a.forward()
    weights_g.start()
    weights_o.forward()
    weights_f[0].start()

    def swap_cols(first, last):
        made = []
        for j in (1, 2, 3):
            here = WA.at[half_at(plane[j]), first:last]
            made.append(push(here, here, near))
        return made

    weights_a.arrived()
    swaps_a = swap_cols(0, 2 * HK + HV)
    for copy in loads_a:
        copy.wait()
    spread_ct.forward()
    spread_h1.arrived()
    weights_g.forward()
    weights_f[1].start()
    got(swaps_a)

    def project(n, carry):
        PJ[n] = nn(H1[...], WA[:, at(n * TILE, TILE, TILE)])
        return carry

    lax.fori_loop(0, (2 * HK + HV) // TILE, project, 0)
    LR[...] = nt(H1[...], DN[...]).astype(low)
    LG[...] = nn(LR[...], UP[...]) + bias

    share_o = []
    weights_o.arrived()
    for j in (1, 2, 3):
        share_o += [
            push(WO.at[4 * plane[j] + p, c], WO.at[4 * plane[j] + p, c], chip_dev(t)) for t in (1, 2, 3)
        ]

    place_t = lax.broadcasted_iota(jnp.int32, (ROWS, ROWS), 0)
    place_s = lax.broadcasted_iota(jnp.int32, (ROWS, ROWS), 1)
    lower = place_t >= place_s
    ones_lower = lower.astype(wide).astype(low)
    ones_upper = (place_t <= place_s).astype(wide).astype(low)

    def block_rows(j):
        return at(j * ROWS, ROWS, ROWS)

    def block_q(rows):
        return PJ[0, rows, 0:HK].astype(low).astype(wide)

    def block_k(rows):
        return PJ[0, rows, HK : 2 * HK].astype(low).astype(wide)

    def block_v(rows):
        return PJ[1, rows, :].astype(low)

    mid = ROWS // 2

    def states(j, carry):
        rows = block_rows(j)
        running = summed_by(ones_lower, jax.nn.log_sigmoid(LG[rows, :]) / logit_norm)
        RU[rows, :] = running
        total = running[ROWS - 1 : ROWS]
        TOT[c, j] = jnp.broadcast_to(total, (8, HK))
        ADD[c, j] = fine_right(tn, block_v(rows), block_k(rows) * jnp.exp(total - running))
        return carry

    lax.fori_loop(0, CHIPS, states, 0)
    sends_state = [push(ADD.at[c], ADD.at[c], near), push(TOT.at[c], TOT.at[c], near)]

    def inside(j, carry):
        rows = block_rows(j)
        running = RU[rows, :]
        middle = running[mid - 1 : mid]
        qd = block_q(rows) * jnp.exp(running - middle)
        kd = block_k(rows) * jnp.exp(middle - running)
        scores = jnp.where(lower, fine_both(nt, qd, kd), 0.0)
        SC[rows, :] = scores
        ATT[rows, :] = fine_left(nn, scores, block_v(rows))
        return carry

    lax.fori_loop(0, CHIPS, inside, 0)

    weights_g.arrived()
    swaps_g = swap_cols(2 * HK + HV, cols)
    got(sends_state)
    state = jnp.zeros((HV, HK), wide)
    for blk in range(2 * CHIPS):
        SS[blk] = state
        state = jnp.exp(TOT[blk % 2, blk // 2, 0:1, :]) * state + ADD[blk % 2, blk // 2]
    SS[2 * CHIPS] = state

    got(swaps_g)
    lax.fori_loop((2 * HK + HV) // TILE, cols // TILE, project, 0)

    def attend(j, carry):
        rows = block_rows(j)
        qs = block_q(rows) * jnp.exp(RU[rows, :])
        att = scale * (ATT[rows, :] + fine_both(nt, qs, SS[2 * j + c]))
        ATT[rows, :] = att
        inv = lax.rsqrt(jnp.mean(att * att, axis=1, keepdims=True) + norm_eps)
        GS[rows, :] = (att * inv * head_gain * jax.nn.silu(PJ[2, rows, :])).astype(low)
        return carry

    lax.fori_loop(0, CHIPS, attend, 0)
    at_head = at(p * HV, HV, HV)
    sends_gated = [
        push(GS.at[at(chip[j] * ROWS, ROWS, ROWS), :], GR.at[:, at_head], chip_dev(j)) for j in (1, 2, 3)
    ]
    GR[:, at_head] = GS[mine, :]

    weights_f[0].forward()
    weights_f[2].start()

    got(share_o)
    swaps_o = []
    for j in (1, 2, 3):
        part = pl.ds(pl.multiple_of(4 * plane[j], 4), 4)
        swaps_o.append(push(WO.at[part, c], WO.at[part, c], near))

    got(sends_gated)
    for copy in loads_o:
        copy.wait()
    got(swaps_o)

    def out_tile(n, carry):
        here = at(n * TILE, TILE, TILE)
        RES[:, here] = x_ref[:, here] + nn(GR[...], WO[:, :, :, here].reshape(width, TILE))
        return carry

    lax.fori_loop(0, tiles, out_tile, 0)
    residual = RES[...]
    inv_two = lax.rsqrt(jnp.mean(residual * residual, axis=1, keepdims=True) + norm_eps)
    H2[mine, :] = (residual * inv_two * gain_two).astype(low)
    spread_h2.start()

    def turn(src, dst):
        def tile(n, carry):
            here = at(n * TILE, TILE, TILE)
            dst[here, :] = src[:, here].T
            return carry

        lax.fori_loop(0, tiles, tile, 0)

    spread_ct.arrived()
    turn(CT, CTT)
    weights_f[0].arrived()
    swaps_f = [swap_f(0)]
    for copy in loads_f:
        copy.wait()

    @pl.when(full)
    def _():
        for copy in loads_rest():
            copy.wait()

    spread_h2.forward()
    spread_h2.arrived()

    def feed(n):
        here = slice(n * TILE, (n + 1) * TILE)
        rows_h2 = H2[...]
        pre_g = nn(rows_h2, WG[:, here])
        pre_u = nn(rows_h2, WU[:, here])
        d_mixed = nt(CT[...], WD[here, :])
        sig = jax.nn.sigmoid(pre_g)
        act = pre_g * sig
        MX[:, here] = (act * pre_u).astype(low)
        DGU[:, here] = (d_mixed * pre_u * (sig * (1.0 + pre_g * (1.0 - sig)))).astype(low)
        DGU[:, ffw + n * TILE : ffw + (n + 1) * TILE] = (d_mixed * act).astype(low)

    def ffn_grads(n):
        here = slice(n * TILE, (n + 1) * TILE)
        there = slice(ffw + n * TILE, ffw + (n + 1) * TILE)

        def tile(m, carry):
            rows = at(m * TILE, TILE, TILE)
            left = H2T[rows, :]
            GF[n, m, :, :, 0:TILE] = nn(left, DGU[:, here]).reshape(2, ROWS, TILE).astype(low)
            GF[n, m, :, :, TILE : 2 * TILE] = nn(left, DGU[:, there]).reshape(2, ROWS, TILE).astype(low)
            GF[n, m, :, :, 2 * TILE :] = nn(CTT[rows, :], MX[:, here]).reshape(2, ROWS, TILE).astype(low)
            return carry

        lax.fori_loop(0, tiles, tile, 0)
        return push(GF.at[n, :, 1 - c], GFC.at[n], near)

    z_ffn = [
        Scatter(
            lambda fi, n=n: GF.at[n, :, c, at(fi * 32, 32, 32), :],
            GFZ.at[n],
            GFL.at[n],
        )
        for n in range(steps)
    ]

    def ffn_out(n, swap):
        swap.wait_recv()

        def tile(m, carry):
            GF[n, m, c] = (GF[n, m, c].astype(wide) + GFC[n, m].astype(wide)).astype(low)
            return carry

        lax.fori_loop(0, tiles, tile, 0)
        z_ffn[n].start()

    weights_f[1].forward()
    got(swaps_f[0])
    feed(0)
    turn(H2, H2T)
    weights_f[1].arrived()
    swaps_f.append(swap_f(1))
    swap_g = [ffn_grads(0)]
    for n in range(1, steps):
        if n + 1 < steps:
            weights_f[n + 1].forward()
        got(swaps_f[n])
        feed(n)
        ffn_out(n - 1, swap_g[n - 1])
        if n + 1 < steps:
            swap_g.append(ffn_grads(n))
            weights_f[n + 1].arrived()
            swaps_f.append(swap_f(n + 1))

    sums_at = [take(6 * tiles) for _ in range(3)]
    low_half, high_half = pl.ds(0, ROWS // 2), pl.ds(ROWS // 2, ROWS // 2)

    def part_copies(kind, n):
        index = sums_at[kind] + 6 * n

        def made(chip_at, part, dst, j, i):
            return remote(SB.at[kind, n, token_rows(chip_at, part), :], dst, chip_dev(j), index + i)

        return [
            made(chip[3], 0, RL.at[kind, 0, n], 1, 0),
            made(chip[3], 1, RL.at[kind, 1, n], 2, 1),
            made(chip[1], 0, RB.at[kind, 0, n, low_half], 1, 2),
            made(chip[2], 1, RB.at[kind, 1, n, high_half], 2, 3),
            made(chip[1], 1, RB.at[kind, 0, n, high_half], 1, 4),
            made(chip[2], 0, RB.at[kind, 1, n, low_half], 2, 5),
        ]

    def send_parts(kind, n):
        for copy in part_copies(kind, n)[:4]:
            copy.start()

    def pass_parts(kind):
        def tile(n, carry):
            copies = part_copies(kind, n)
            for side, rows in ((0, token_rows(chip[2], 0)), (1, token_rows(chip[1], 1))):
                copies[side].wait_recv()
                SB[kind, n, rows, :] = (
                    SB[kind, n, rows, :].astype(wide) + RL[kind, side, n].astype(wide)
                ).astype(low)
                copies[5 - side].start()
            return carry

        lax.fori_loop(0, tiles, tile, 0)

    def part_sum(kind, n):
        for copy in part_copies(kind, n)[2:]:
            copy.wait_recv()
        return (
            SB[kind, n, mine, :].astype(wide)
            + RB[kind, 0, n].astype(wide)
            + RB[kind, 1, n].astype(wide)
        )

    def d_hidden_tile(n, carry):
        rows = at(n * TILE, TILE, TILE)
        SB[0, n] = (nt(DGU[:, 0:ffw], WG[rows, :]) + nt(DGU[:, ffw : 2 * ffw], WU[rows, :])).astype(low)
        send_parts(0, n)
        return carry

    lax.fori_loop(0, tiles, d_hidden_tile, 0)

    swap_g.append(ffn_grads(steps - 1))
    pass_parts(0)

    def y_tile(n, carry):
        SB[1, n] = nn(MX[...], WD[:, at(n * TILE, TILE, TILE)]).astype(low)
        return carry

    lax.fori_loop(0, tiles, y_tile, 0)

    z_ffn[0].forward()
    ffn_out(steps - 1, swap_g[steps - 1])

    d_h2 = jnp.concatenate([part_sum(0, n) for n in range(tiles)], axis=1)
    residual = RES[...]
    inv_two = lax.rsqrt(jnp.mean(residual * residual, axis=1, keepdims=True) + norm_eps)
    unit = residual * inv_two
    pulled = d_h2 * gain_two
    GP[1:2, :] = jnp.sum(d_h2 * unit, axis=0, keepdims=True)
    d_res = cot_ref[...] + inv_two * (pulled - unit * jnp.mean(pulled * unit, axis=1, keepdims=True))
    in_ref[...] = d_res
    d_res_low = d_res.astype(low)
    DR[mine, :] = d_res_low

    def d_gated_tile(n, carry):
        w = WO[pl.ds(pl.multiple_of(4 * n, 4), 4)].reshape(own, width)
        DGS[n] = nt(DR[mine, :], w).astype(low)
        return carry

    lax.fori_loop(0, CHIPS, d_gated_tile, 0)
    sends_dg = [push(DGS.at[chip[j]], DGR.at[mine, :], chip_dev(j)) for j in (1, 2, 3)]
    DGR[mine, :] = DGS[p]

    got(sends_dg)
    z_ffn[1].forward()
    spread_dr.start()

    def through_gate(j, head_sum):
        rows = block_rows(j)
        att = ATT[rows, :]
        inv = lax.rsqrt(jnp.mean(att * att, axis=1, keepdims=True) + norm_eps)
        unit_att = att * inv
        pre = PJ[2, rows, :]
        sig = jax.nn.sigmoid(pre)
        act = pre * sig
        d_gated = DGR[rows, :].astype(wide)
        through = d_gated * unit_att
        DP[rows, 2 * HK + HV : cols] = (through * head_gain * (sig * (1.0 + pre * (1.0 - sig)))).astype(low)
        d_unit = d_gated * head_gain * act
        d_out = scale * inv * (d_unit - unit_att * jnp.mean(d_unit * unit_att, axis=1, keepdims=True))
        DO[rows, :] = d_out
        PUL[c, j] = fine_both(tn, d_out, block_q(rows) * jnp.exp(RU[rows, :]))
        return head_sum + jnp.sum(through * act, axis=0, keepdims=True)

    head_sum = lax.fori_loop(0, CHIPS, through_gate, jnp.zeros((1, HV), wide))
    GP[2:3, 0:HV] = head_sum
    send_pull = push(PUL.at[c], PUL.at[c], near)

    def inside_back(j, carry):
        rows = block_rows(j)
        running = RU[rows, :]
        middle = running[mid - 1 : mid]
        up = jnp.exp(running - middle)
        down = jnp.exp(middle - running)
        qd = block_q(rows) * up
        kd = block_k(rows) * down
        d_out = DO[rows, :]
        d_scores = jnp.where(lower, fine_left(nt, d_out, block_v(rows)), 0.0)
        DQ[rows, :] = up * fine_both(nn, d_scores, kd) + jnp.exp(running) * fine_both(nn, d_out, SS[2 * j + c])
        DK[rows, :] = down * fine_both(tn, d_scores, qd)
        DV[rows, :] = fine_both(tn, SC[rows, :], d_out)
        return carry

    lax.fori_loop(0, CHIPS, inside_back, 0)
    spread_dr.forward()
    send_pull.wait_recv()
    d_state = jnp.zeros((HV, HK), wide)
    for blk in range(2 * CHIPS - 1, -1, -1):
        DS[blk] = d_state
        d_state = jnp.exp(TOT[blk % 2, blk // 2, 0:1, :]) * d_state + PUL[blk % 2, blk // 2]

    def across_back(j, bias_sum):
        rows = block_rows(j)
        running = RU[rows, :]
        to_end = jnp.exp(running[ROWS - 1 : ROWS] - running)
        d_after = DS[2 * j + c]
        k_rows = block_k(rows)
        d_k = DK[rows, :] + to_end * fine_right(nn, block_v(rows), d_after)
        d_v = DV[rows, :] + fine_both(nt, k_rows * to_end, d_after)
        d_q = DQ[rows, :]
        tail = jnp.sum(d_after * SS[2 * j + c + 1], axis=0, keepdims=True)
        d_decay = summed_by(ones_upper, block_q(rows) * d_q - k_rows * d_k) + tail
        d_logits = d_decay * jax.nn.sigmoid(-LG[rows, :]) / logit_norm
        d_logits_low = d_logits.astype(low)
        DL[rows, :] = d_logits_low
        DP[rows, 0:HK] = d_q.astype(low)
        DP[rows, HK : 2 * HK] = d_k.astype(low)
        DP[rows, 2 * HK : 2 * HK + HV] = d_v.astype(low)
        DP[rows, cols:ext] = nt(d_logits_low, UP[...]).astype(low)
        return bias_sum + jnp.sum(d_logits, axis=0, keepdims=True)

    bias_sum = lax.fori_loop(0, CHIPS, across_back, jnp.zeros((1, HK), wide))
    UB[0:16, :] = tn(LR[...], DL[...])[0:16]
    UB[16:17, :] = bias_sum
    send_ub = push(UB, UBC, near)

    z_attn = [
        Scatter(
            lambda fi, i=i: GA.at[i, :, c, at(fi * 32, 32, 32), :],
            GAZ.at[i],
            GAL.at[i],
        )
        for i in range(2)
    ]

    def attn_grads(i):
        for m in range(tiles // 2):
            col = (i * (tiles // 2) + m) * TILE
            GA[i, m] = nn(H1[:, col : col + TILE].T, DP[...]).reshape(2, ROWS, ext).astype(low)
        return push(GA.at[i, :, 1 - c], GAC.at[i], near)

    def attn_out(i, swap):
        swap.wait_recv()
        for m in range(tiles // 2):
            GA[i, m, c] = (GA[i, m, c].astype(wide) + GAC[i, m].astype(wide)).astype(low)
        z_attn[i].start()

    swap_a = [attn_grads(0), attn_grads(1)]
    z_ffn[2].forward()
    attn_out(0, swap_a[0])
    attn_out(1, swap_a[1])

    spread_dr.arrived()

    def out_grad(n, carry):
        here = at(n * TILE, TILE, TILE)
        GO[:, :, here] = tn(GS[...], DR[:, here]).reshape(2, ROWS, TILE).astype(low)
        return carry

    lax.fori_loop(0, tiles, out_grad, 0)
    swap_out = push(GO.at[1 - c], GOC, near)

    def d_input_tile(n, carry):
        rows = at(n * TILE, TILE, TILE)
        SB[2, n] = (nt(DP[:, 0:cols], WA[rows, :]) + nn(DP[:, cols:ext], DN[:, rows])).astype(low)
        send_parts(2, n)
        return carry

    lax.fori_loop(0, tiles, d_input_tile, 0)

    swap_out.wait_recv()
    GO[c] = (GO[c].astype(wide) + GOC[...].astype(wide)).astype(low)
    z_out = Scatter(lambda fi: GO.at[c, at(fi * 32, 32, 32), :], GOZ, GOL)
    z_out.start()
    z_attn[0].forward()
    send_ub.wait_recv()
    UBC[...] = UB[...] + UBC[...]
    z_ub = [push(UBC, UBZ.at[j - 1], plane_dev(j)) for j in (1, 2, 3)]

    pass_parts(2)

    for n in range(tiles):
        send_parts(1, n)

    d_h1 = jnp.concatenate([part_sum(2, n) for n in range(tiles)], axis=1)
    x = x_ref[...]
    inv_one = lax.rsqrt(jnp.mean(x * x, axis=1, keepdims=True) + norm_eps)
    unit_one = x * inv_one
    pulled_one = d_h1 * gain_one
    GP[0:1, :] = jnp.sum(d_h1 * unit_one, axis=0, keepdims=True)
    send_gp = push(GP, GPC, near)
    in_ref[...] += inv_one * (
        pulled_one - unit_one * jnp.mean(pulled_one * unit_one, axis=1, keepdims=True)
    )
    send_gp.wait_recv()
    GPC[...] = GP[...] + GPC[...]
    x_gp = [push(GPC, GPX.at[j - 1], chip_dev(j)) for j in (1, 2, 3)]

    z_attn[1].forward()
    z_out.forward()

    def ffn_done(n):
        z_ffn[n].arrived()
        GFS[n] = z_ffn[n].total().astype(low)
        GFR[p, n] = GFS[n, p]
        return [push(GFS.at[n, chip[j]], GFR.at[p, n], chip_dev(j)) for j in (1, 2, 3)]

    a_ffn = [ffn_done(0)]
    pass_parts(1)
    a_ffn += [ffn_done(n) for n in range(1, steps)]
    got(x_gp)
    GPS[...] = GPC[...] + GPX[0] + GPX[1] + GPX[2]
    z_gp = [push(GPS, GPZ.at[j - 1], plane_dev(j)) for j in (1, 2, 3)]

    for n in range(tiles):
        here = slice(n * TILE, (n + 1) * TILE)
        out_ref[:, here] = RES[:, here] + part_sum(1, n)

    a_attn = []
    for i in range(2):
        z_attn[i].arrived()
        GAS[i * (tiles // 2) : (i + 1) * (tiles // 2)] = z_attn[i].total().astype(low)
    for j in (1, 2, 3):
        a_attn.append(push(GAS.at[chip[j]], GAR.at[p], chip_dev(j)))
    GAR[p] = GAS[p]
    for copies in a_ffn:
        got(copies)
    gf_ref[...] = GFR[...]
    z_out.arrived()
    go_ref[...] = z_out.total()
    got(z_ub)
    ub_ref[...] = UBC[...] + UBZ[0] + UBZ[1] + UBZ[2]
    got(z_gp)
    gains_ref[...] = GPS[...] + GPZ[0] + GPZ[1] + GPZ[2]
    got(a_attn)
    ga_ref[...] = GAR[...]

    for copy in pending:
        copy.wait_send()
    for end in ends:
        end()
    for kind in range(3):
        for n in range(tiles):
            for copy in part_copies(kind, n):
                copy.wait_send()


def finish_kernel(out_in, in_in, go_in, gf, ga, gains, ub, *refs):
    (
        out_ref,
        in_ref,
        attn_gain_ref,
        gq_ref,
        gk_ref,
        gv_ref,
        gg_ref,
        down_ref,
        up_ref,
        bias_ref,
        head_ref,
        go_ref,
        ffn_gain_ref,
        gfg_ref,
        gfu_ref,
        gfd_ref,
    ) = refs
    out_ref[...] = out_in[...]
    in_ref[...] = in_in[...]
    go_ref[...] = go_in[...]
    device = lax.axis_index("seq") * CHIPS + lax.axis_index("fsdp")
    steps = gf.shape[1]
    cols = 2 * HK + 2 * HV
    down_total = jnp.zeros((32, ga.shape[2] - cols), wide)
    for i in range(CHIPS):
        piece = ga[i].astype(wide)
        gq_ref[:, i * HK : (i + 1) * HK] = piece[:, 0:HK]
        gk_ref[:, i * HK : (i + 1) * HK] = piece[:, HK : 2 * HK]
        gv_ref[:, i * HV : (i + 1) * HV] = piece[:, 2 * HK : 2 * HK + HV]
        gg_ref[:, i * HV : (i + 1) * HV] = piece[:, 2 * HK + HV : cols]
        down_total = down_total + piece[:, cols:]
        for n in range(steps):
            first = (i * steps + n) * TILE
            if first < gfg_ref.shape[1]:
                piece_f = gf[i, n].astype(wide)
                gfg_ref[:, first : first + TILE] = piece_f[:, 0:TILE]
                gfu_ref[:, first : first + TILE] = piece_f[:, TILE : 2 * TILE]
                gfd_ref[:, first : first + TILE] = piece_f[:, 2 * TILE :]
    down_ref[...] = down_total.T[0 : down_ref.shape[0], :]

    def lanes(ref, first, count):
        around = ref[:, pl.ds(pl.multiple_of(first // 128 * 128, 128), 128)]
        return pltpu.roll(around, (128 - first % 128) % 128, 1)[:, 0:count]

    gain_part = lanes(gains, device * attn_gain_ref.shape[1], attn_gain_ref.shape[1])
    attn_gain_ref[...] = gain_part[0:1]
    ffn_gain_ref[...] = gain_part[1:2]
    head_ref[...] = lanes(gains, device * head_ref.shape[1], head_ref.shape[1])[2:3]
    up_part = lanes(ub, (device % 8) * up_ref.shape[1], up_ref.shape[1])
    up_ref[...] = up_part[0:16]
    bias_ref[...] = up_part[16:17]


def in_plane(
    block_input,
    attn_gain,
    query_weight,
    key_weight,
    value_weight,
    gate_weight,
    decay_down,
    decay_up,
    decay_bias,
    head_gain,
    out_weight,
    ffn_gain,
    ffn_gate,
    ffn_up,
    ffn_down,
    cotangent,
):
    width = block_input.shape[2]
    ff_full = ffn_gate.shape[1]
    ffw = -(-ff_full // (CHIPS * TILE)) * TILE
    rank = decay_down.shape[1]

    scratch = scratch_of(width, ffw, 128)
    f32 = jax.ShapeDtypeStruct
    outs = pl.pallas_call(
        functools.partial(plane_kernel, tuple(scratch)),
        out_shape=[
            f32((ROWS, width), wide),
            f32((ROWS, width), wide),
            f32((32, width), wide),
            f32(*scratch["GFR"]),
            f32(*scratch["GAR"]),
            f32((8, width), wide),
            f32((24, HK), wide),
        ],
        in_specs=[pl.BlockSpec(memory_space=pltpu.VMEM)] * 8 + [pl.BlockSpec(memory_space=pl.ANY)] * 8,
        out_specs=[pl.BlockSpec(memory_space=pltpu.VMEM)] * 7,
        scratch_shapes=[pltpu.VMEM(shape, kind) for shape, kind in scratch.values()]
        + [
            pltpu.SemaphoreType.DMA((COPIES,)),
            pltpu.SemaphoreType.DMA((COPIES,)),
            pltpu.SemaphoreType.DMA((LOCALS,)),
        ],
        compiler_params=pltpu.CompilerParams(
            collective_id=0, has_side_effects=True, vmem_limit_bytes=62 * 1024 * 1024
        ),
        name="layer_step",
    )(
        decay_down.T,
        decay_up,
        attn_gain,
        ffn_gain,
        head_gain,
        decay_bias,
        block_input[0],
        cotangent[0],
        query_weight,
        key_weight,
        value_weight,
        gate_weight,
        out_weight,
        ffn_gate,
        ffn_up,
        ffn_down,
    )
    each = width // 32
    done = pl.pallas_call(
        finish_kernel,
        out_shape=[
            f32((ROWS, width), wide),
            f32((ROWS, width), wide),
            f32((1, each), wide),
            f32((32, CHIPS * HK), wide),
            f32((32, CHIPS * HK), wide),
            f32((32, CHIPS * HV), wide),
            f32((32, CHIPS * HV), wide),
            f32((rank, 32), wide),
            f32((rank, CHIPS * HK // 32), wide),
            f32((1, CHIPS * HK // 32), wide),
            f32((1, HV // 32), wide),
            f32((32, width), wide),
            f32((1, each), wide),
            f32((32, ff_full), wide),
            f32((32, ff_full), wide),
            f32((32, ff_full), wide),
        ],
        in_specs=[pl.BlockSpec(memory_space=pltpu.VMEM)] * 7,
        out_specs=[pl.BlockSpec(memory_space=pltpu.VMEM)] * 16,
        compiler_params=pltpu.CompilerParams(vmem_limit_bytes=62 * 1024 * 1024),
        name="results",
    )(*outs)
    shapes = {0: (1, ROWS, width), 1: (1, ROWS, width), 2: (-1,), 9: (-1,), 10: (-1,), 12: (-1,)}
    done = [v.reshape(shapes[i]) if i in shapes else v for i, v in enumerate(done)]
    done[7], done[15] = done[7].T, done[15].T
    return tuple(done)


def solution(mesh):
    one_plane = mesh.shape["seq"] == 2 * CHIPS and mesh.shape["fsdp"] == CHIPS
    return jax.shard_map(
        in_plane if one_plane else spread,
        mesh=mesh,
        in_specs=(
            P("fsdp", "seq", None),
            P("fsdp"),
            P("fsdp", None),
            P("fsdp", None),
            P("fsdp", None),
            P("fsdp", None),
            P("fsdp", None),
            P(None, "fsdp"),
            P("fsdp"),
            P("fsdp"),
            P("fsdp", None),
            P("fsdp"),
            P("fsdp", None),
            P("fsdp", None),
            P(None, "fsdp"),
            P("fsdp", "seq", None),
        ),
        out_specs=(
            P("fsdp", "seq", None),
            P("fsdp", "seq", None),
            P(("seq", "fsdp")),
            P(("seq", "fsdp"), None),
            P(("seq", "fsdp"), None),
            P(("seq", "fsdp"), None),
            P(("seq", "fsdp"), None),
            P(("seq", "fsdp"), None),
            P(None, ("seq", "fsdp")),
            P(("seq", "fsdp")),
            P(("seq", "fsdp")),
            P(("seq", "fsdp"), None),
            P(("seq", "fsdp")),
            P(("seq", "fsdp"), None),
            P(("seq", "fsdp"), None),
            P(None, ("seq", "fsdp")),
        ),
        check_vma=False,
    )
```

```python
import functools

import jax
import jax.numpy as jnp
from jax import lax
from jax.experimental import pallas as pl
from jax.experimental.pallas import tpu as pltpu
from jax.sharding import PartitionSpec as P

HK = 128
HV = 256
BLOCK = 64


norm_eps = 1e-06
logit_norm = 16.0
exact = lax.Precision.HIGHEST
fine = lax.Precision.HIGH
low = jnp.bfloat16
wide = jnp.float32


def product(left, right):
    return jnp.dot(left, right, preferred_element_type=wide)


def transposed(left, right):
    return lax.dot_general(left, right, (((0,), (0,)), ((), ())), preferred_element_type=wide)


def against(left, right):
    return lax.dot_general(left, right, (((1,), (1,)), ((), ())), preferred_element_type=wide)


def fine_dot(spec, left, right):
    return jnp.einsum(spec, left, right, precision=fine, preferred_element_type=wide)


def rms_gain(token_rows, gain_row):
    return (
        token_rows
        * lax.rsqrt(jnp.mean(token_rows * token_rows, axis=-1, keepdims=True) + norm_eps)
        * gain_row
    )


def gated_norm(attended, gate_pre, head_gain):
    return rms_gain(attended, head_gain) * jax.nn.silu(gate_pre)


def swiglu(gate_part, up_part):
    return jax.nn.silu(gate_part) * up_part


def exchange(pieces):
    return lax.all_to_all(pieces, "fsdp", 0, 0)


def gather_rows(rows):
    return lax.all_gather(rows, "fsdp", axis=0, tiled=True)


def scatter_rows(rows):
    return lax.psum_scatter(rows.astype(low), "fsdp", scatter_dimension=0, tiled=True).astype(wide)


def summed_rows(grads):
    return lax.psum_scatter(grads.astype(low), "seq", scatter_dimension=0, tiled=True)


def owned_columns(section, parts):
    return exchange(section.reshape(parts, section.shape[0] // parts, -1))


def across(pieces):
    rows = pieces.shape[1]
    return pieces.transpose(1, 0, 2).reshape(rows, -1).astype(wide)


def spread(
    block_input,
    attn_gain,
    query_weight,
    key_weight,
    value_weight,
    gate_weight,
    decay_down,
    decay_up,
    decay_bias,
    head_gain,
    out_weight,
    ffn_gain,
    ffn_gate,
    ffn_up,
    ffn_down,
    cotangent,
):
    shards, parts = lax.axis_size("seq"), lax.axis_size("fsdp")
    si = lax.axis_index("seq")
    x = block_input[0]
    cot_rows = cotangent[0]
    length, width = x.shape
    blocks = length // BLOCK
    scale = HK ** (-0.5)

    small = jnp.concatenate([attn_gain, ffn_gain, head_gain, decay_down.reshape(-1)])
    small = exchange(jnp.broadcast_to(small[None], (parts, small.shape[0])))
    own = attn_gain.shape[0]
    own_head = head_gain.shape[0]
    gain_one = small[:, :own].reshape(-1).astype(wide)
    gain_two = small[:, own : 2 * own].reshape(-1).astype(wide)
    gain_head = small[:, 2 * own : 2 * own + own_head].reshape(-1).astype(wide)
    down_full = small[:, 2 * own + own_head :].reshape(width, -1)
    rank = down_full.shape[1]

    normed_one, norm_one_back = jax.vjp(rms_gain, x, gain_one)
    both = gather_rows(jnp.concatenate([normed_one.astype(low), cot_rows.astype(low)], axis=1))
    hidden_one = both[:, :width]
    cot_low = both[:, width:]
    ff = ffn_gate.shape[1] // parts
    rows = own // shards
    down_rows = ff // shards
    cuts = [
        lax.dynamic_slice_in_dim(w, si * rows, rows, 0).reshape(rows, parts, -1).transpose(1, 0, 2)
        for w in (query_weight, key_weight, value_weight, gate_weight, ffn_gate, ffn_up)
    ]
    cuts.append(
        lax.dynamic_slice_in_dim(
            ffn_down.reshape(parts, ff, own), si * down_rows, down_rows, 1
        ).reshape(parts, rows, -1)
    )
    got = lax.all_gather(exchange(jnp.concatenate(cuts, axis=2)), "seq")
    attn_columns = 2 * HK + 2 * HV
    attn_w = got[..., :attn_columns].transpose(1, 0, 2, 3).reshape(width, -1)
    ffn_w = (
        got[..., attn_columns : attn_columns + 2 * ff].transpose(1, 0, 2, 3).reshape(width, -1)
    )
    down_w = (
        got[..., attn_columns + 2 * ff :]
        .reshape(shards, parts, down_rows, own)
        .transpose(0, 2, 1, 3)
        .reshape(ff, width)
    )

    projected = product(hidden_one, attn_w)
    rounded = projected[:, : 2 * HK + HV].astype(low)
    gate_pre = projected[:, 2 * HK + HV :]
    low_rank = product(hidden_one, down_full).astype(low)
    logits = product(low_rank, decay_up) + decay_bias.astype(wide)
    log_decay = jax.nn.log_sigmoid(logits) / logit_norm

    def chunked(rows):
        return rows.reshape(parts * blocks, BLOCK, -1)

    q = chunked(rounded[:, :HK].astype(wide))
    k = chunked(rounded[:, HK : 2 * HK].astype(wide))
    v = chunked(rounded[:, 2 * HK :].astype(wide))
    place = jnp.arange(BLOCK)
    lower = place[:, None] >= place[None, :]
    ones_lower = lower.astype(wide)
    running = jnp.einsum("ts,bsk->btk", ones_lower, chunked(log_decay), precision=exact)
    total = running[:, -1]
    grown = jnp.exp(running)
    shrunk = jnp.exp(-running)
    to_end = jnp.exp(total[:, None] - running)
    qd = q * grown
    kd = k * shrunk
    kf = k * to_end
    scores = jnp.where(lower[None], fine_dot("btk,bsk->bts", qd, kd), 0.0)
    intra = fine_dot("bts,bsv->btv", scores, v)
    added = fine_dot("bsk,bsv->bkv", kf, v)
    added_c = added.reshape(parts, blocks, HK, HV)
    total_c = total.reshape(parts, blocks, HK)
    factor_c = jnp.exp(total_c)[..., None]
    local_state = added_c[:, 0]
    for c in range(1, blocks):
        local_state = factor_c[:, c] * local_state + added_c[:, c]
    totals = lax.all_gather(jnp.sum(total_c, axis=1), "seq")
    states = lax.all_gather(local_state.astype(low), "seq")
    index = jnp.arange(shards)
    upto = jnp.cumsum(totals, axis=0)
    mine_upto = lax.dynamic_index_in_dim(upto, si, 0, False)
    mine_total = lax.dynamic_index_in_dim(totals, si, 0, False)
    before = (index < si)[:, None, None]
    after = (index > si)[:, None, None]
    early = jnp.where(before, jnp.exp(jnp.where(before, mine_upto - mine_total - upto, 0.0)), 0.0)
    late = jnp.where(
        after, jnp.exp(jnp.where(after, upto - totals - mine_upto, 0.0)), 0.0
    )
    incoming = jnp.sum(early[..., None] * states.astype(wide), axis=0)
    entering = [incoming]
    for c in range(blocks):
        entering.append(factor_c[:, c] * entering[-1] + added_c[:, c])
    state_in = jnp.stack(entering[:-1], axis=1).reshape(parts * blocks, HK, HV)
    state_out = jnp.stack(entering[1:], axis=1).reshape(parts * blocks, HK, HV)
    attended = scale * (intra + fine_dot("btk,bkv->btv", qd, state_in))
    attended = attended.reshape(parts * length, HV)

    gated, gated_back = jax.vjp(gated_norm, attended, gate_pre, gain_head)
    gated_low = gated.astype(low)
    residual = x + scatter_rows(product(gated_low, out_weight))
    normed_two, norm_two_back = jax.vjp(rms_gain, residual, gain_two)
    hidden_two = gather_rows(normed_two.astype(low))
    pre = product(hidden_two, ffn_w)
    mixed, mixed_back = jax.vjp(swiglu, pre[:, :ff], pre[:, ff:])
    mixed_low = mixed.astype(low)
    d_gate_part, d_up_part = mixed_back(against(cot_low, down_w))
    d_pre = jnp.concatenate([d_gate_part.astype(low), d_up_part.astype(low)], axis=1)
    both = scatter_rows(
        jnp.concatenate(
            [against(d_pre, ffn_w).astype(low), product(mixed_low, down_w).astype(low)], axis=1
        )
    )
    d_residual_norm, grad_ffn_gain = norm_two_back(both[:, :width])
    d_residual = cot_rows + d_residual_norm
    d_res_low = gather_rows(d_residual.astype(low))
    block_output = residual + both[:, width:]
    ffn_section = summed_rows(
        jnp.concatenate(
            [transposed(hidden_two, d_pre).astype(low), transposed(cot_low, mixed_low).astype(low)],
            axis=1,
        )
    )
    ffn_owned = owned_columns(ffn_section, parts)

    d_attended, d_gate_pre, grad_head_gain = gated_back(against(d_res_low, out_weight))
    d_out = chunked(scale * d_attended)
    pulled = fine_dot("btk,btv->bkv", qd, d_out)
    pulled_c = pulled.reshape(parts, blocks, HK, HV)
    local_pull = pulled_c[:, blocks - 1]
    for c in range(blocks - 2, -1, -1):
        local_pull = factor_c[:, c] * local_pull + pulled_c[:, c]
    pulls = lax.all_gather(local_pull.astype(low), "seq")
    later = jnp.sum(late[..., None] * pulls.astype(wide), axis=0)
    leaving = [later]
    for c in range(blocks - 1, 0, -1):
        leaving.insert(0, factor_c[:, c] * leaving[0] + pulled_c[:, c])
    d_state = jnp.stack(leaving, axis=1).reshape(parts * blocks, HK, HV)
    d_scores = jnp.where(lower[None], fine_dot("btv,bsv->bts", d_out, v), 0.0)
    d_q = grown * (
        fine_dot("bts,bsk->btk", d_scores, kd) + fine_dot("btv,bkv->btk", d_out, state_in)
    )
    d_k = shrunk * fine_dot("bts,btk->bsk", d_scores, qd) + to_end * fine_dot(
        "bsv,bkv->bsk", v, d_state
    )
    d_v = fine_dot("bts,btv->bsv", scores, d_out) + fine_dot("bsk,bkv->bsv", kf, d_state)
    tail_term = jnp.sum(d_state * state_out, axis=2)
    d_log_decay = (
        jnp.einsum("st,bsk->btk", ones_lower, q * d_q - k * d_k, precision=exact)
        + tail_term[:, None]
    )
    d_logits = d_log_decay.reshape(parts * length, HK) * jax.nn.sigmoid(-logits) / logit_norm
    grad_decay_bias = jnp.sum(d_logits, axis=0)
    d_logits_low = d_logits.astype(low)
    grad_decay_up = transposed(low_rank, d_logits_low)
    d_low_rank = against(d_logits_low, decay_up).astype(low)
    grad_decay_down = transposed(hidden_one, d_low_rank)
    d_projected = jnp.concatenate(
        [
            d_q.reshape(parts * length, HK).astype(low),
            d_k.reshape(parts * length, HK).astype(low),
            d_v.reshape(parts * length, HV).astype(low),
            d_gate_pre.astype(low),
        ],
        axis=1,
    )
    d_hidden_one = scatter_rows(against(d_projected, attn_w) + against(d_low_rank, down_full))
    d_input_norm, grad_attn_gain = norm_one_back(d_hidden_one)
    input_grad = d_residual + d_input_norm
    devices = shards * parts
    grad_out = transposed(gated_low, d_res_low).astype(low)
    attn_section = summed_rows(
        jnp.concatenate(
            [transposed(hidden_one, d_projected).astype(low), grad_out.reshape(width, HV)], axis=1
        )
    )
    attn_owned = owned_columns(attn_section[:, :attn_columns], parts)
    turned = [(s * parts + f, f * shards + s) for s in range(shards) for f in range(parts)]
    own_out = lax.ppermute(
        attn_section[:, attn_columns:].reshape(-1, width), ("seq", "fsdp"), turned
    ).astype(wide)
    head_part = jnp.concatenate(
        [
            grad_decay_up.reshape(rank, shards, -1).transpose(1, 0, 2).reshape(shards, -1),
            grad_decay_bias.reshape(shards, -1),
        ],
        axis=1,
    )
    mine = jnp.arange(parts)[:, None, None] == lax.axis_index("fsdp")
    head_part = jnp.where(mine, head_part[None], 0.0).reshape(devices, -1)
    own_bias_size = HK // shards
    summed = jnp.concatenate(
        [
            grad_attn_gain.reshape(devices, -1),
            grad_ffn_gain.reshape(devices, -1),
            grad_head_gain.reshape(devices, -1),
            grad_decay_down.reshape(devices, -1),
            head_part,
        ],
        axis=1,
    )
    summed = jnp.sum(lax.all_to_all(summed, ("seq", "fsdp"), 0, 0), axis=0)
    each = width // devices
    each_head = HV // devices
    own_attn_gain = summed[:each]
    own_ffn_gain = summed[each : 2 * each]
    own_head_gain = summed[2 * each : 2 * each + each_head]
    at_up = 2 * each + each_head + each * rank
    at_bias = at_up + rank * own_bias_size
    own_down = summed[2 * each + each_head : at_up].reshape(each, rank)
    own_up = summed[at_up:at_bias].reshape(rank, own_bias_size)
    own_bias = summed[at_bias:]
    return (
        block_output[None],
        input_grad[None],
        own_attn_gain,
        across(attn_owned[:, :, :HK]),
        across(attn_owned[:, :, HK : 2 * HK]),
        across(attn_owned[:, :, 2 * HK : 2 * HK + HV]),
        across(attn_owned[:, :, 2 * HK + HV :]),
        own_down,
        own_up,
        own_bias,
        own_head_gain,
        own_out,
        own_ffn_gain,
        across(ffn_owned[:, :, :ff]),
        across(ffn_owned[:, :, ff : 2 * ff]),
        across(ffn_owned[:, :, 2 * ff :]).T,
    )


MESH = pl.DeviceIdType.MESH
CHIPS = 4
ROWS = 128
TILE = 256


def nn(left, right):
    return lax.dot_general(left, right, (((1,), (0,)), ((), ())), preferred_element_type=wide)


def nt(left, right):
    return lax.dot_general(left, right, (((1,), (1,)), ((), ())), preferred_element_type=wide)


def tn(left, right):
    return lax.dot_general(left, right, (((0,), (0,)), ((), ())), preferred_element_type=wide)


def halves(values):
    top = values.astype(low)
    return top, (values - top.astype(wide)).astype(low)


def fine_both(op, left, right):
    lh, ll = halves(left)
    rh, rl = halves(right)
    return op(lh, rh) + (op(lh, rl) + op(ll, rh))


def fine_left(op, left, right):
    lh, ll = halves(left)
    return op(lh, right) + op(ll, right)


def fine_right(op, left, right):
    rh, rl = halves(right)
    return op(left, rh) + op(left, rl)


def summed_by(ones, values):
    top, rest = halves(values)
    mid = (values - top.astype(wide)).astype(low)
    last = (values - top.astype(wide) - mid.astype(wide)).astype(low)
    return nn(ones, top) + (nn(ones, mid) + nn(ones, last))


def at(start, size, unit):
    return pl.ds(pl.multiple_of(start, unit), size)


def scratch_of(width, ffw, rank_pad):
    tokens = CHIPS * ROWS
    attn_cols = 2 * HK + 2 * HV
    ext = attn_cols + rank_pad
    tiles = width // TILE
    steps = ffw // TILE
    return {
        "SM": ((CHIPS, 48, TILE), low),
        "WA": ((width, attn_cols), low),
        "WO": ((4 * CHIPS, 2, 32, width), low),
        "WG": ((width, ffw), low),
        "WU": ((width, ffw), low),
        "WD": ((ffw, width), low),
        "DN": ((rank_pad, width), low),
        "UP": ((rank_pad, HK), low),
        "H1": ((tokens, width), low),
        "CT": ((tokens, width), low),
        "H2": ((tokens, width), low),
        "DR": ((tokens, width), low),
        "PJ": ((3, tokens, TILE), wide),
        "LG": ((tokens, HK), wide),
        "LR": ((tokens, rank_pad), low),
        "RU": ((tokens, HK), wide),
        "SC": ((tokens, ROWS), wide),
        "ADD": ((2, CHIPS, HV, HK), wide),
        "PUL": ((2, CHIPS, HV, HK), wide),
        "TOT": ((2, CHIPS, 8, HK), wide),
        "SS": ((2 * CHIPS + 1, HV, HK), wide),
        "DS": ((2 * CHIPS, HV, HK), wide),
        "ATT": ((tokens, HV), wide),
        "GS": ((tokens, HV), low),
        "GR": ((ROWS, width), low),
        "RES": ((ROWS, width), wide),
        "MX": ((tokens, ffw), low),
        "DGU": ((tokens, 2 * ffw), low),
        "SB": ((3, tiles, tokens, TILE), low),
        "RB": ((3, 2, tiles, ROWS, TILE), low),
        "RL": ((3, 2, tiles, ROWS // 2, TILE), low),
        "DGS": ((CHIPS, ROWS, HV), low),
        "DGR": ((tokens, HV), low),
        "DO": ((tokens, HV), wide),
        "DQ": ((tokens, HK), wide),
        "DK": ((tokens, HK), wide),
        "DV": ((tokens, HV), wide),
        "DL": ((tokens, HK), low),
        "DP": ((tokens, ext), low),
        "H2T": ((width, tokens), low),
        "CTT": ((width, tokens), low),
        "GF": ((steps, tiles, 2, ROWS, 3 * TILE), low),
        "GFC": ((steps, tiles, ROWS, 3 * TILE), low),
        "GFZ": ((steps, 3, tiles, 32, 3 * TILE), low),
        "GFL": ((steps, tiles, 32, 3 * TILE), low),
        "GFS": ((steps, tiles, 32, 3 * TILE), low),
        "GFR": ((CHIPS, steps, 32, 3 * TILE), low),
        "GA": ((2, tiles // 2, 2, ROWS, ext), low),
        "GAC": ((2, tiles // 2, ROWS, ext), low),
        "GAZ": ((2, 3, tiles // 2, 32, ext), low),
        "GAL": ((2, tiles // 2, 32, ext), low),
        "GAS": ((tiles, 32, ext), low),
        "GAR": ((CHIPS, 32, ext), low),
        "GO": ((2, ROWS, width), low),
        "GOC": ((ROWS, width), low),
        "GOZ": ((3, 32, width), low),
        "GOL": ((32, width), low),
        "GP": ((8, width), wide),
        "GPC": ((8, width), wide),
        "GPX": ((3, 8, width), wide),
        "GPZ": ((3, 8, width), wide),
        "GPS": ((8, width), wide),
        "UB": ((24, HK), wide),
        "UBC": ((24, HK), wide),
        "UBZ": ((3, 24, HK), wide),
    }


COPIES = 320
LOCALS = 24


def plane_kernel(names, *refs):
    (factor_ref, up_in_ref, gain_one_ref, gain_two_ref, head_gain_ref, bias_ref) = refs[:6]
    (x_ref, cot_ref, q_hbm, k_hbm, v_hbm, g_hbm, o_hbm, fg_hbm, fu_hbm, fd_hbm) = refs[6:16]
    (out_ref, in_ref, go_ref, gf_ref, ga_ref, gains_ref, ub_ref) = refs[16:23]
    b = dict(zip(names, refs[23 : 23 + len(names)]))
    send_sems, recv_sems, local_sems = refs[23 + len(names) :]
    SM, WA, WO, WG, WU, WD, DN, UP = (b[n] for n in ("SM", "WA", "WO", "WG", "WU", "WD", "DN", "UP"))
    H1, CT, H2, DR, PJ, LG, LR, RU, SC = (
        b[n] for n in ("H1", "CT", "H2", "DR", "PJ", "LG", "LR", "RU", "SC")
    )
    ADD, PUL, TOT, SS, DS, ATT, GS, GR, RES = (
        b[n] for n in ("ADD", "PUL", "TOT", "SS", "DS", "ATT", "GS", "GR", "RES")
    )
    MX, DGU, SB, RB, DGS, DGR, DO, DQ, DK, DV, DL, DP = (
        b[n] for n in ("MX", "DGU", "SB", "RB", "DGS", "DGR", "DO", "DQ", "DK", "DV", "DL", "DP")
    )
    GP, GPC, GPX, GPZ, GPS, UB, UBC, UBZ = (
        b[n] for n in ("GP", "GPC", "GPX", "GPZ", "GPS", "UB", "UBC", "UBZ")
    )
    GO, GOC, GOZ, GOL = (b[n] for n in ("GO", "GOC", "GOZ", "GOL"))
    H2T, CTT, RL = b["H2T"], b["CTT"], b["RL"]
    GF, GFC, GFZ, GFL, GFS, GFR = (b[n] for n in ("GF", "GFC", "GFZ", "GFL", "GFS", "GFR"))
    GA, GAC, GAZ, GAL, GAS, GAR = (b[n] for n in ("GA", "GAC", "GAZ", "GAL", "GAS", "GAR"))
    width = x_ref.shape[1]
    tokens = H1.shape[0]
    tiles = width // TILE
    ffw = WG.shape[1]
    steps = ffw // TILE
    last_ff = fg_hbm.shape[1] - (CHIPS - 1) * ffw
    rest_ff = ffw - last_ff
    ext = DP.shape[1]
    cols = 2 * HK + 2 * HV
    own = width // 4
    half = own // 2
    scale = HK ** (-0.5)

    s = lax.axis_index("seq")
    f = lax.axis_index("fsdp")
    p = s // 2
    c = s % 2
    chip = (None, p + 1 - 2 * (p % 2), (p + 2) % 4, 3 - p)
    plane = (None, f + 1 - 2 * (f % 2), (f + 2) % 4, 3 - f)
    near = (s + 1 - 2 * c, f)
    full = p < CHIPS - 1
    inner = (f > 0) & (f < 3)
    outer = jnp.logical_not(inner)

    used = [0, 0]
    pending = []

    def take(count=1):
        first = used[0]
        used[0] += count
        return first

    def remote(src, dst, dev, index, landed=None):
        return pltpu.make_async_remote_copy(
            src_ref=src,
            dst_ref=dst,
            send_sem=send_sems.at[index],
            recv_sem=recv_sems.at[index if landed is None else landed],
            device_id=dev,
            device_id_type=MESH,
        )

    def chip_dev(j):
        return (2 * chip[j] + c, f)

    def plane_dev(j):
        return (s, plane[j])

    def push(src, dst, dev):
        copy = remote(src, dst, dev, take())
        copy.start()
        pending.append(copy)
        return copy

    def local(src, dst):
        copy = pltpu.make_async_copy(src, dst, local_sems.at[used[1]])
        used[1] += 1
        copy.start()
        return copy

    def got(copies):
        for copy in copies:
            copy.wait_recv()

    ends = []

    def when(conds, action):
        conds = [cond for cond in conds if cond is not None]

        def run():
            action()

        if not conds:
            run()
            return
        both = conds[0]
        for cond in conds[1:]:
            both = both & cond
        pl.when(both)(run)

    class Gather:
        def __init__(self, parts, cond=None):
            self.parts, self.cond, self.count = parts, cond, len(parts)
            self.first, self.passed = take(3 * len(parts)), take(len(parts))
            ends.append(self.end)

        def copies(self, j, source=None):
            made = []
            for i, (src, view) in enumerate(self.parts):
                index = self.first + (j - 1) * self.count + i
                if source is None:
                    made.append(remote(src, view(f), plane_dev(j), index))
                else:
                    made.append(remote(view(source), view(source), plane_dev(j), index))
            return made

        def handed(self):
            return [
                remote(
                    view(plane[2]),
                    view(plane[2]),
                    plane_dev(1),
                    self.passed + i,
                    self.first + 2 * self.count + i,
                )
                for i, (_, view) in enumerate(self.parts)
            ]

        def start(self):
            when([self.cond], lambda: [copy.start() for j in (2, 1) for copy in self.copies(j)])
            when([self.cond, inner], lambda: [copy.start() for copy in self.copies(3)])

        def landed(self, j):
            for copy in self.copies(j, plane[j]):
                copy.wait_recv()

        def forward(self):
            def action():
                self.landed(2)
                for copy in self.handed():
                    copy.start()

            when([self.cond, inner], action)

        def arrived(self):
            when([self.cond], lambda: self.landed(1))
            when([self.cond, outer], lambda: self.landed(2))
            when([self.cond], lambda: self.landed(3))

        def end(self):
            when([self.cond], lambda: [copy.wait_send() for j in (1, 2) for copy in self.copies(j)])
            when(
                [self.cond, inner],
                lambda: [copy.wait_send() for copy in self.copies(3) + self.handed()],
            )

    class Scatter:
        def __init__(self, block, landing, relay):
            self.block, self.landing, self.relay = block, landing, relay
            self.first, self.extra = take(3), take(1)
            ends.append(self.end)

        def copy(self, j):
            return remote(self.block(plane[j]), self.landing.at[j - 1], plane_dev(j), self.first + j - 1)

        def aside(self):
            return remote(self.block(plane[3]), self.relay, plane_dev(1), self.extra)

        def start(self):
            when([outer], lambda: [self.aside().start(), self.copy(2).start()])
            self.copy(1).start()
            when([inner], lambda: self.copy(3).start())

        def forward(self):
            def action():
                self.aside().wait_recv()
                mine_too = self.block(plane[2])
                mine_too[...] = (mine_too[...].astype(wide) + self.relay[...].astype(wide)).astype(low)
                self.copy(2).start()

            when([inner], action)

        def arrived(self):
            self.copy(1).wait_recv()
            self.copy(2).wait_recv()
            when([inner], lambda: self.copy(3).wait_recv())

        def total(self):
            kept = self.block(f)[...].astype(wide)
            return kept + (
                self.landing[0].astype(wide) + self.landing[1].astype(wide) + self.landing[2].astype(wide)
            )

        def end(self):
            self.copy(1).wait_send()
            self.copy(2).wait_send()
            when([inner], lambda: self.copy(3).wait_send())
            when([outer], lambda: self.aside().wait_send())

    def token_rows(chip_at, part=None):
        if part is None:
            return at(chip_at * ROWS, ROWS, ROWS)
        return at(chip_at * ROWS + part * (ROWS // 2), ROWS // 2, ROWS // 2)

    class Spread:
        def __init__(self, buf):
            self.buf, self.first = buf, take(4)
            ends.append(self.end)

        def sent(self, j, chip_at, part=None, index=0):
            here = self.buf.at[token_rows(chip_at, part), :]
            return remote(here, here, chip_dev(j), self.first + index)

        def start(self):
            self.sent(1, p, None, 0).start()
            self.sent(2, p, None, 1).start()

        def forward(self):
            self.sent(1, chip[1], None, 0).wait_recv()
            self.sent(2, chip[1], 0, 2).start()
            self.sent(2, chip[2], None, 1).wait_recv()
            self.sent(1, chip[2], 1, 3).start()

        def arrived(self):
            self.sent(2, chip[3], 0, 2).wait_recv()
            self.sent(1, chip[3], 1, 3).wait_recv()

        def end(self):
            self.sent(1, p, None, 0).wait_send()
            self.sent(2, p, None, 1).wait_send()
            self.sent(2, chip[1], 0, 2).wait_send()
            self.sent(1, chip[2], 1, 3).wait_send()

    own_rows = at(f * own, own, own)
    at_qk = at(p * HK, HK, HK)
    at_v = at(p * HV, HV, HV)
    at_ff = at(p * ffw, last_ff, TILE)
    at_ff_rest = at(p * ffw + last_ff, rest_ff, TILE)
    @pl.when(jnp.logical_not(full))
    def _():
        WG[:, last_ff:ffw] = jnp.zeros((width, rest_ff), low)
        WU[:, last_ff:ffw] = jnp.zeros((width, rest_ff), low)
        WD[last_ff:ffw, :] = jnp.zeros((rest_ff, width), low)

    SM[f, 0:16, :] = factor_ref[...]
    SM[f, 16:32, 0:HK] = up_in_ref[...]

    def as_row(ref, count):
        row = ref[...].astype(wide).reshape(1, count)
        return row if count == TILE else jnp.concatenate([row, jnp.zeros((1, TILE - count), wide)], axis=1)

    SM[f, 32:48, :] = jnp.concatenate(
        [
            as_row(gain_one_ref, TILE),
            as_row(gain_two_ref, TILE),
            as_row(head_gain_ref, HV // CHIPS),
            as_row(bias_ref, HK),
            jnp.zeros((12, TILE), wide),
        ],
        axis=0,
    ).astype(low)

    barrier = pltpu.get_barrier_semaphore()
    peers = [near] + [chip_dev(j) for j in (1, 2, 3)] + [plane_dev(j) for j in (1, 2, 3)]
    for dev in peers:
        pl.semaphore_signal(barrier, inc=1, device_id=dev, device_id_type=MESH)
    pl.semaphore_wait(barrier, len(peers))

    smalls = [push(SM.at[f], SM.at[f], plane_dev(j)) for j in (1, 2, 3)]
    half_rows = at(c * half, half, half)

    def half_at(fi):
        return at(fi * own + c * half, half, half)

    def columns(ref, first, count, start=0):
        return lambda fi: ref.at[half_at(fi), start : start + count]

    weights_a = Gather(
        [
            (q_hbm.at[half_rows, at_qk], columns(WA, 0, HK)),
            (k_hbm.at[half_rows, at_qk], columns(WA, 0, HK, HK)),
            (v_hbm.at[half_rows, at_v], columns(WA, 0, HV, 2 * HK)),
        ]
    )
    weights_g = Gather([(g_hbm.at[half_rows, at_v], columns(WA, 0, HV, 2 * HK + HV))])
    o_rows = at(64 * p + 32 * c, 32, 32)
    weights_o = Gather([(o_hbm.at[o_rows, :], lambda fi: WO.at[4 * fi + p, c])])
    weights_f = []
    for n in range(steps):
        here = at(p * ffw + n * TILE, TILE, TILE)
        down_here = at(p * ffw + n * TILE + c * ROWS, ROWS, ROWS)
        down_there = at(n * TILE + c * ROWS, ROWS, ROWS)
        weights_f.append(
            Gather(
                [
                    (fg_hbm.at[half_rows, here], columns(WG, 0, TILE, n * TILE)),
                    (fu_hbm.at[half_rows, here], columns(WU, 0, TILE, n * TILE)),
                    (
                        fd_hbm.at[down_here, :],
                        lambda fi, down_there=down_there: WD.at[down_there, at(fi * own, own, own)],
                    ),
                ],
                None if n * TILE < last_ff else full,
            )
        )

    def swap_f(n):
        made = []
        for j in (1, 2, 3):
            for _, view in weights_f[n].parts:
                made.append(push(view(plane[j]), view(plane[j]), near))
        return made

    weights_a.start()
    weights_o.start()

    loads_a = [
        local(q_hbm.at[:, at_qk], WA.at[own_rows, 0:HK]),
        local(k_hbm.at[:, at_qk], WA.at[own_rows, HK : 2 * HK]),
        local(v_hbm.at[:, at_v], WA.at[own_rows, 2 * HK : 2 * HK + HV]),
        local(g_hbm.at[:, at_v], WA.at[own_rows, 2 * HK + HV : cols]),
    ]
    loads_o = [
        local(
            o_hbm.at[pl.ds(pl.multiple_of(64 * i + 32 * h, 32), 32), :],
            WO.at[4 * f + i, h],
        )
        for i in range(CHIPS)
        for h in range(2)
    ]
    loads_f = [
        local(fg_hbm.at[:, at_ff], WG.at[own_rows, 0:last_ff]),
        local(fu_hbm.at[:, at_ff], WU.at[own_rows, 0:last_ff]),
        local(fd_hbm.at[at_ff, :], WD.at[0:last_ff, own_rows]),
    ]
    rest_at = used[1]
    used[1] += 3

    def loads_rest():
        pairs = (
            (fg_hbm.at[:, at_ff_rest], WG.at[own_rows, last_ff:ffw]),
            (fu_hbm.at[:, at_ff_rest], WU.at[own_rows, last_ff:ffw]),
            (fd_hbm.at[at_ff_rest, :], WD.at[last_ff:ffw, own_rows]),
        )
        return [
            pltpu.make_async_copy(src, dst, local_sems.at[rest_at + i])
            for i, (src, dst) in enumerate(pairs)
        ]

    @pl.when(full)
    def _():
        for copy in loads_rest():
            copy.start()

    @pl.when(outer)
    def _():
        GFZ[:, 2] = jnp.zeros((steps, tiles, 32, 3 * TILE), low)
        GAZ[:, 2] = jnp.zeros((2, tiles // 2, 32, ext), low)
        GOZ[2] = jnp.zeros((32, width), low)

    DN[...] = jnp.zeros(DN.shape, low)
    UP[...] = jnp.zeros(UP.shape, low)
    GP[...] = jnp.zeros(GP.shape, wide)
    UB[...] = jnp.zeros(UB.shape, wide)

    x = x_ref[...]
    inv_one = lax.rsqrt(jnp.mean(x * x, axis=1, keepdims=True) + norm_eps)
    got(smalls)

    def full_row(row):
        return jnp.concatenate([SM[i, 32:48, :].astype(wide)[row : row + 1] for i in range(CHIPS)], axis=1)

    gain_one = full_row(0)
    gain_two = full_row(1)
    head_gain = jnp.concatenate(
        [SM[i, 32:48, :].astype(wide)[2:3, 0 : HV // CHIPS] for i in range(CHIPS)], axis=1
    )
    bias = SM[p, 32:48, 0:HK][3:4].astype(wide)
    for i in range(CHIPS):
        DN[0:16, i * TILE : (i + 1) * TILE] = SM[i, 0:16, :]
    UP[0:16, :] = SM[p, 16:32, 0:HK]

    mine = at(p * ROWS, ROWS, ROWS)
    H1[mine, :] = (x * inv_one * gain_one).astype(low)
    CT[mine, :] = cot_ref[...].astype(low)
    spread_h1, spread_ct, spread_h2, spread_dr = (Spread(buf) for buf in (H1, CT, H2, DR))
    spread_h1.start()
    spread_h1.forward()
    spread_ct.start()
    weights_a.forward()
    weights_g.start()
    weights_o.forward()
    weights_f[0].start()

    def swap_cols(first, last):
        made = []
        for j in (1, 2, 3):
            here = WA.at[half_at(plane[j]), first:last]
            made.append(push(here, here, near))
        return made

    weights_a.arrived()
    swaps_a = swap_cols(0, 2 * HK + HV)
    for copy in loads_a:
        copy.wait()
    spread_ct.forward()
    spread_h1.arrived()
    weights_g.forward()
    weights_f[1].start()
    got(swaps_a)

    def project(n, carry):
        PJ[n] = nn(H1[...], WA[:, at(n * TILE, TILE, TILE)])
        return carry

    lax.fori_loop(0, (2 * HK + HV) // TILE, project, 0)
    LR[...] = nt(H1[...], DN[...]).astype(low)
    LG[...] = nn(LR[...], UP[...]) + bias

    share_o = []
    weights_o.arrived()
    for j in (1, 2, 3):
        share_o += [
            push(WO.at[4 * plane[j] + p, c], WO.at[4 * plane[j] + p, c], chip_dev(t)) for t in (1, 2, 3)
        ]

    place_t = lax.broadcasted_iota(jnp.int32, (ROWS, ROWS), 0)
    place_s = lax.broadcasted_iota(jnp.int32, (ROWS, ROWS), 1)
    lower = place_t >= place_s
    ones_lower = lower.astype(wide).astype(low)
    ones_upper = (place_t <= place_s).astype(wide).astype(low)

    def block_rows(j):
        return at(j * ROWS, ROWS, ROWS)

    def block_q(rows):
        return PJ[0, rows, 0:HK].astype(low).astype(wide)

    def block_k(rows):
        return PJ[0, rows, HK : 2 * HK].astype(low).astype(wide)

    def block_v(rows):
        return PJ[1, rows, :].astype(low)

    mid = ROWS // 2

    def states(j, carry):
        rows = block_rows(j)
        running = summed_by(ones_lower, jax.nn.log_sigmoid(LG[rows, :]) / logit_norm)
        RU[rows, :] = running
        total = running[ROWS - 1 : ROWS]
        TOT[c, j] = jnp.broadcast_to(total, (8, HK))
        ADD[c, j] = fine_right(tn, block_v(rows), block_k(rows) * jnp.exp(total - running))
        return carry

    lax.fori_loop(0, CHIPS, states, 0)
    sends_state = [push(ADD.at[c], ADD.at[c], near), push(TOT.at[c], TOT.at[c], near)]

    def inside(j, carry):
        rows = block_rows(j)
        running = RU[rows, :]
        middle = running[mid - 1 : mid]
        qd = block_q(rows) * jnp.exp(running - middle)
        kd = block_k(rows) * jnp.exp(middle - running)
        scores = jnp.where(lower, fine_both(nt, qd, kd), 0.0)
        SC[rows, :] = scores
        ATT[rows, :] = fine_left(nn, scores, block_v(rows))
        return carry

    lax.fori_loop(0, CHIPS, inside, 0)

    weights_g.arrived()
    swaps_g = swap_cols(2 * HK + HV, cols)
    got(sends_state)
    state = jnp.zeros((HV, HK), wide)
    for blk in range(2 * CHIPS):
        SS[blk] = state
        state = jnp.exp(TOT[blk % 2, blk // 2, 0:1, :]) * state + ADD[blk % 2, blk // 2]
    SS[2 * CHIPS] = state

    got(swaps_g)
    lax.fori_loop((2 * HK + HV) // TILE, cols // TILE, project, 0)

    def attend(j, carry):
        rows = block_rows(j)
        qs = block_q(rows) * jnp.exp(RU[rows, :])
        att = scale * (ATT[rows, :] + fine_both(nt, qs, SS[2 * j + c]))
        ATT[rows, :] = att
        inv = lax.rsqrt(jnp.mean(att * att, axis=1, keepdims=True) + norm_eps)
        GS[rows, :] = (att * inv * head_gain * jax.nn.silu(PJ[2, rows, :])).astype(low)
        return carry

    lax.fori_loop(0, CHIPS, attend, 0)
    at_head = at(p * HV, HV, HV)
    sends_gated = [
        push(GS.at[at(chip[j] * ROWS, ROWS, ROWS), :], GR.at[:, at_head], chip_dev(j)) for j in (1, 2, 3)
    ]
    GR[:, at_head] = GS[mine, :]

    weights_f[0].forward()
    weights_f[2].start()

    got(share_o)
    swaps_o = []
    for j in (1, 2, 3):
        part = pl.ds(pl.multiple_of(4 * plane[j], 4), 4)
        swaps_o.append(push(WO.at[part, c], WO.at[part, c], near))

    got(sends_gated)
    for copy in loads_o:
        copy.wait()
    got(swaps_o)

    def out_tile(n, carry):
        here = at(n * TILE, TILE, TILE)
        RES[:, here] = x_ref[:, here] + nn(GR[...], WO[:, :, :, here].reshape(width, TILE))
        return carry

    lax.fori_loop(0, tiles, out_tile, 0)
    residual = RES[...]
    inv_two = lax.rsqrt(jnp.mean(residual * residual, axis=1, keepdims=True) + norm_eps)
    H2[mine, :] = (residual * inv_two * gain_two).astype(low)
    spread_h2.start()

    def turn(src, dst):
        def tile(n, carry):
            here = at(n * TILE, TILE, TILE)
            dst[here, :] = src[:, here].T
            return carry

        lax.fori_loop(0, tiles, tile, 0)

    spread_ct.arrived()
    turn(CT, CTT)
    weights_f[0].arrived()
    swaps_f = [swap_f(0)]
    for copy in loads_f:
        copy.wait()

    @pl.when(full)
    def _():
        for copy in loads_rest():
            copy.wait()

    spread_h2.forward()
    spread_h2.arrived()

    def feed(n):
        here = slice(n * TILE, (n + 1) * TILE)
        rows_h2 = H2[...]
        pre_g = nn(rows_h2, WG[:, here])
        pre_u = nn(rows_h2, WU[:, here])
        d_mixed = nt(CT[...], WD[here, :])
        sig = jax.nn.sigmoid(pre_g)
        act = pre_g * sig
        MX[:, here] = (act * pre_u).astype(low)
        DGU[:, here] = (d_mixed * pre_u * (sig * (1.0 + pre_g * (1.0 - sig)))).astype(low)
        DGU[:, ffw + n * TILE : ffw + (n + 1) * TILE] = (d_mixed * act).astype(low)

    def ffn_grads(n):
        here = slice(n * TILE, (n + 1) * TILE)
        there = slice(ffw + n * TILE, ffw + (n + 1) * TILE)

        def tile(m, carry):
            rows = at(m * TILE, TILE, TILE)
            left = H2T[rows, :]
            GF[n, m, :, :, 0:TILE] = nn(left, DGU[:, here]).reshape(2, ROWS, TILE).astype(low)
            GF[n, m, :, :, TILE : 2 * TILE] = nn(left, DGU[:, there]).reshape(2, ROWS, TILE).astype(low)
            GF[n, m, :, :, 2 * TILE :] = nn(CTT[rows, :], MX[:, here]).reshape(2, ROWS, TILE).astype(low)
            return carry

        lax.fori_loop(0, tiles, tile, 0)
        return push(GF.at[n, :, 1 - c], GFC.at[n], near)

    z_ffn = [
        Scatter(
            lambda fi, n=n: GF.at[n, :, c, at(fi * 32, 32, 32), :],
            GFZ.at[n],
            GFL.at[n],
        )
        for n in range(steps)
    ]

    def ffn_out(n, swap):
        swap.wait_recv()

        def tile(m, carry):
            GF[n, m, c] = (GF[n, m, c].astype(wide) + GFC[n, m].astype(wide)).astype(low)
            return carry

        lax.fori_loop(0, tiles, tile, 0)
        z_ffn[n].start()

    weights_f[1].forward()
    got(swaps_f[0])
    feed(0)
    turn(H2, H2T)
    weights_f[1].arrived()
    swaps_f.append(swap_f(1))
    swap_g = [ffn_grads(0)]
    for n in range(1, steps):
        if n + 1 < steps:
            weights_f[n + 1].forward()
        got(swaps_f[n])
        feed(n)
        ffn_out(n - 1, swap_g[n - 1])
        if n + 1 < steps:
            swap_g.append(ffn_grads(n))
            weights_f[n + 1].arrived()
            swaps_f.append(swap_f(n + 1))

    sums_at = [take(6 * tiles) for _ in range(3)]
    low_half, high_half = pl.ds(0, ROWS // 2), pl.ds(ROWS // 2, ROWS // 2)

    def part_copies(kind, n):
        index = sums_at[kind] + 6 * n

        def made(chip_at, part, dst, j, i):
            return remote(SB.at[kind, n, token_rows(chip_at, part), :], dst, chip_dev(j), index + i)

        return [
            made(chip[3], 0, RL.at[kind, 0, n], 1, 0),
            made(chip[3], 1, RL.at[kind, 1, n], 2, 1),
            made(chip[1], 0, RB.at[kind, 0, n, low_half], 1, 2),
            made(chip[2], 1, RB.at[kind, 1, n, high_half], 2, 3),
            made(chip[1], 1, RB.at[kind, 0, n, high_half], 1, 4),
            made(chip[2], 0, RB.at[kind, 1, n, low_half], 2, 5),
        ]

    def send_parts(kind, n):
        for copy in part_copies(kind, n)[:4]:
            copy.start()

    def pass_parts(kind):
        def tile(n, carry):
            copies = part_copies(kind, n)
            for side, rows in ((0, token_rows(chip[2], 0)), (1, token_rows(chip[1], 1))):
                copies[side].wait_recv()
                SB[kind, n, rows, :] = (
                    SB[kind, n, rows, :].astype(wide) + RL[kind, side, n].astype(wide)
                ).astype(low)
                copies[5 - side].start()
            return carry

        lax.fori_loop(0, tiles, tile, 0)

    def part_sum(kind, n):
        for copy in part_copies(kind, n)[2:]:
            copy.wait_recv()
        return (
            SB[kind, n, mine, :].astype(wide)
            + RB[kind, 0, n].astype(wide)
            + RB[kind, 1, n].astype(wide)
        )

    def d_hidden_tile(n, carry):
        rows = at(n * TILE, TILE, TILE)
        SB[0, n] = (nt(DGU[:, 0:ffw], WG[rows, :]) + nt(DGU[:, ffw : 2 * ffw], WU[rows, :])).astype(low)
        send_parts(0, n)
        return carry

    lax.fori_loop(0, tiles, d_hidden_tile, 0)

    swap_g.append(ffn_grads(steps - 1))
    pass_parts(0)

    def y_tile(n, carry):
        SB[1, n] = nn(MX[...], WD[:, at(n * TILE, TILE, TILE)]).astype(low)
        return carry

    lax.fori_loop(0, tiles, y_tile, 0)

    z_ffn[0].forward()
    ffn_out(steps - 1, swap_g[steps - 1])

    d_h2 = jnp.concatenate([part_sum(0, n) for n in range(tiles)], axis=1)
    residual = RES[...]
    inv_two = lax.rsqrt(jnp.mean(residual * residual, axis=1, keepdims=True) + norm_eps)
    unit = residual * inv_two
    pulled = d_h2 * gain_two
    GP[1:2, :] = jnp.sum(d_h2 * unit, axis=0, keepdims=True)
    d_res = cot_ref[...] + inv_two * (pulled - unit * jnp.mean(pulled * unit, axis=1, keepdims=True))
    in_ref[...] = d_res
    d_res_low = d_res.astype(low)
    DR[mine, :] = d_res_low

    def d_gated_tile(n, carry):
        w = WO[pl.ds(pl.multiple_of(4 * n, 4), 4)].reshape(own, width)
        DGS[n] = nt(DR[mine, :], w).astype(low)
        return carry

    lax.fori_loop(0, CHIPS, d_gated_tile, 0)
    sends_dg = [push(DGS.at[chip[j]], DGR.at[mine, :], chip_dev(j)) for j in (1, 2, 3)]
    DGR[mine, :] = DGS[p]

    got(sends_dg)
    z_ffn[1].forward()
    spread_dr.start()

    def through_gate(j, head_sum):
        rows = block_rows(j)
        att = ATT[rows, :]
        inv = lax.rsqrt(jnp.mean(att * att, axis=1, keepdims=True) + norm_eps)
        unit_att = att * inv
        pre = PJ[2, rows, :]
        sig = jax.nn.sigmoid(pre)
        act = pre * sig
        d_gated = DGR[rows, :].astype(wide)
        through = d_gated * unit_att
        DP[rows, 2 * HK + HV : cols] = (through * head_gain * (sig * (1.0 + pre * (1.0 - sig)))).astype(low)
        d_unit = d_gated * head_gain * act
        d_out = scale * inv * (d_unit - unit_att * jnp.mean(d_unit * unit_att, axis=1, keepdims=True))
        DO[rows, :] = d_out
        PUL[c, j] = fine_both(tn, d_out, block_q(rows) * jnp.exp(RU[rows, :]))
        return head_sum + jnp.sum(through * act, axis=0, keepdims=True)

    head_sum = lax.fori_loop(0, CHIPS, through_gate, jnp.zeros((1, HV), wide))
    GP[2:3, 0:HV] = head_sum
    send_pull = push(PUL.at[c], PUL.at[c], near)

    def inside_back(j, carry):
        rows = block_rows(j)
        running = RU[rows, :]
        middle = running[mid - 1 : mid]
        up = jnp.exp(running - middle)
        down = jnp.exp(middle - running)
        qd = block_q(rows) * up
        kd = block_k(rows) * down
        d_out = DO[rows, :]
        d_scores = jnp.where(lower, fine_left(nt, d_out, block_v(rows)), 0.0)
        DQ[rows, :] = up * fine_both(nn, d_scores, kd) + jnp.exp(running) * fine_both(nn, d_out, SS[2 * j + c])
        DK[rows, :] = down * fine_both(tn, d_scores, qd)
        DV[rows, :] = fine_both(tn, SC[rows, :], d_out)
        return carry

    lax.fori_loop(0, CHIPS, inside_back, 0)
    spread_dr.forward()
    send_pull.wait_recv()
    d_state = jnp.zeros((HV, HK), wide)
    for blk in range(2 * CHIPS - 1, -1, -1):
        DS[blk] = d_state
        d_state = jnp.exp(TOT[blk % 2, blk // 2, 0:1, :]) * d_state + PUL[blk % 2, blk // 2]

    def across_back(j, bias_sum):
        rows = block_rows(j)
        running = RU[rows, :]
        to_end = jnp.exp(running[ROWS - 1 : ROWS] - running)
        d_after = DS[2 * j + c]
        k_rows = block_k(rows)
        d_k = DK[rows, :] + to_end * fine_right(nn, block_v(rows), d_after)
        d_v = DV[rows, :] + fine_both(nt, k_rows * to_end, d_after)
        d_q = DQ[rows, :]
        tail = jnp.sum(d_after * SS[2 * j + c + 1], axis=0, keepdims=True)
        d_decay = summed_by(ones_upper, block_q(rows) * d_q - k_rows * d_k) + tail
        d_logits = d_decay * jax.nn.sigmoid(-LG[rows, :]) / logit_norm
        d_logits_low = d_logits.astype(low)
        DL[rows, :] = d_logits_low
        DP[rows, 0:HK] = d_q.astype(low)
        DP[rows, HK : 2 * HK] = d_k.astype(low)
        DP[rows, 2 * HK : 2 * HK + HV] = d_v.astype(low)
        DP[rows, cols:ext] = nt(d_logits_low, UP[...]).astype(low)
        return bias_sum + jnp.sum(d_logits, axis=0, keepdims=True)

    bias_sum = lax.fori_loop(0, CHIPS, across_back, jnp.zeros((1, HK), wide))
    UB[0:16, :] = tn(LR[...], DL[...])[0:16]
    UB[16:17, :] = bias_sum
    send_ub = push(UB, UBC, near)

    z_attn = [
        Scatter(
            lambda fi, i=i: GA.at[i, :, c, at(fi * 32, 32, 32), :],
            GAZ.at[i],
            GAL.at[i],
        )
        for i in range(2)
    ]

    def attn_grads(i):
        for m in range(tiles // 2):
            col = (i * (tiles // 2) + m) * TILE
            GA[i, m] = nn(H1[:, col : col + TILE].T, DP[...]).reshape(2, ROWS, ext).astype(low)
        return push(GA.at[i, :, 1 - c], GAC.at[i], near)

    def attn_out(i, swap):
        swap.wait_recv()
        for m in range(tiles // 2):
            GA[i, m, c] = (GA[i, m, c].astype(wide) + GAC[i, m].astype(wide)).astype(low)
        z_attn[i].start()

    swap_a = [attn_grads(0), attn_grads(1)]
    z_ffn[2].forward()
    attn_out(0, swap_a[0])
    attn_out(1, swap_a[1])

    spread_dr.arrived()

    def out_grad(n, carry):
        here = at(n * TILE, TILE, TILE)
        GO[:, :, here] = tn(GS[...], DR[:, here]).reshape(2, ROWS, TILE).astype(low)
        return carry

    lax.fori_loop(0, tiles, out_grad, 0)
    swap_out = push(GO.at[1 - c], GOC, near)

    def d_input_tile(n, carry):
        rows = at(n * TILE, TILE, TILE)
        SB[2, n] = (nt(DP[:, 0:cols], WA[rows, :]) + nn(DP[:, cols:ext], DN[:, rows])).astype(low)
        send_parts(2, n)
        return carry

    lax.fori_loop(0, tiles, d_input_tile, 0)

    swap_out.wait_recv()
    GO[c] = (GO[c].astype(wide) + GOC[...].astype(wide)).astype(low)
    z_out = Scatter(lambda fi: GO.at[c, at(fi * 32, 32, 32), :], GOZ, GOL)
    z_out.start()
    z_attn[0].forward()
    send_ub.wait_recv()
    UBC[...] = UB[...] + UBC[...]
    z_ub = [push(UBC, UBZ.at[j - 1], plane_dev(j)) for j in (1, 2, 3)]

    pass_parts(2)

    for n in range(tiles):
        send_parts(1, n)

    d_h1 = jnp.concatenate([part_sum(2, n) for n in range(tiles)], axis=1)
    x = x_ref[...]
    inv_one = lax.rsqrt(jnp.mean(x * x, axis=1, keepdims=True) + norm_eps)
    unit_one = x * inv_one
    pulled_one = d_h1 * gain_one
    GP[0:1, :] = jnp.sum(d_h1 * unit_one, axis=0, keepdims=True)
    send_gp = push(GP, GPC, near)
    in_ref[...] += inv_one * (
        pulled_one - unit_one * jnp.mean(pulled_one * unit_one, axis=1, keepdims=True)
    )
    send_gp.wait_recv()
    GPC[...] = GP[...] + GPC[...]
    x_gp = [push(GPC, GPX.at[j - 1], chip_dev(j)) for j in (1, 2, 3)]

    def ffn_done(n):
        z_ffn[n].arrived()
        GFS[n] = z_ffn[n].total().astype(low)
        GFR[p, n] = GFS[n, p]
        return [push(GFS.at[n, chip[j]], GFR.at[p, n], chip_dev(j)) for j in (1, 2, 3)]

    a_ffn = [ffn_done(0)]
    pass_parts(1)
    a_ffn += [ffn_done(n) for n in range(1, steps)]
    z_attn[1].forward()
    z_out.forward()
    got(x_gp)
    GPS[...] = GPC[...] + GPX[0] + GPX[1] + GPX[2]
    z_gp = [push(GPS, GPZ.at[j - 1], plane_dev(j)) for j in (1, 2, 3)]

    for n in range(tiles):
        here = slice(n * TILE, (n + 1) * TILE)
        out_ref[:, here] = RES[:, here] + part_sum(1, n)

    a_attn = []
    for i in range(2):
        z_attn[i].arrived()
        GAS[i * (tiles // 2) : (i + 1) * (tiles // 2)] = z_attn[i].total().astype(low)
    for j in (1, 2, 3):
        a_attn.append(push(GAS.at[chip[j]], GAR.at[p], chip_dev(j)))
    GAR[p] = GAS[p]
    for copies in a_ffn:
        got(copies)
    gf_ref[...] = GFR[...]
    z_out.arrived()
    go_ref[...] = z_out.total()
    got(z_ub)
    ub_ref[...] = UBC[...] + UBZ[0] + UBZ[1] + UBZ[2]
    got(z_gp)
    gains_ref[...] = GPS[...] + GPZ[0] + GPZ[1] + GPZ[2]
    got(a_attn)
    ga_ref[...] = GAR[...]

    for copy in pending:
        copy.wait_send()
    for end in ends:
        end()
    for kind in range(3):
        for n in range(tiles):
            for copy in part_copies(kind, n):
                copy.wait_send()


def finish_kernel(out_in, in_in, go_in, gf, ga, gains, ub, *refs):
    (
        out_ref,
        in_ref,
        attn_gain_ref,
        gq_ref,
        gk_ref,
        gv_ref,
        gg_ref,
        down_ref,
        up_ref,
        bias_ref,
        head_ref,
        go_ref,
        ffn_gain_ref,
        gfg_ref,
        gfu_ref,
        gfd_ref,
    ) = refs
    out_ref[...] = out_in[...]
    in_ref[...] = in_in[...]
    go_ref[...] = go_in[...]
    device = lax.axis_index("seq") * CHIPS + lax.axis_index("fsdp")
    steps = gf.shape[1]
    cols = 2 * HK + 2 * HV
    down_total = jnp.zeros((32, ga.shape[2] - cols), wide)
    for i in range(CHIPS):
        piece = ga[i].astype(wide)
        gq_ref[:, i * HK : (i + 1) * HK] = piece[:, 0:HK]
        gk_ref[:, i * HK : (i + 1) * HK] = piece[:, HK : 2 * HK]
        gv_ref[:, i * HV : (i + 1) * HV] = piece[:, 2 * HK : 2 * HK + HV]
        gg_ref[:, i * HV : (i + 1) * HV] = piece[:, 2 * HK + HV : cols]
        down_total = down_total + piece[:, cols:]
        for n in range(steps):
            first = (i * steps + n) * TILE
            if first < gfg_ref.shape[1]:
                piece_f = gf[i, n].astype(wide)
                gfg_ref[:, first : first + TILE] = piece_f[:, 0:TILE]
                gfu_ref[:, first : first + TILE] = piece_f[:, TILE : 2 * TILE]
                gfd_ref[:, first : first + TILE] = piece_f[:, 2 * TILE :]
    down_ref[...] = down_total.T[0 : down_ref.shape[0], :]

    def lanes(ref, first, count):
        around = ref[:, pl.ds(pl.multiple_of(first // 128 * 128, 128), 128)]
        return pltpu.roll(around, (128 - first % 128) % 128, 1)[:, 0:count]

    gain_part = lanes(gains, device * attn_gain_ref.shape[1], attn_gain_ref.shape[1])
    attn_gain_ref[...] = gain_part[0:1]
    ffn_gain_ref[...] = gain_part[1:2]
    head_ref[...] = lanes(gains, device * head_ref.shape[1], head_ref.shape[1])[2:3]
    up_part = lanes(ub, (device % 8) * up_ref.shape[1], up_ref.shape[1])
    up_ref[...] = up_part[0:16]
    bias_ref[...] = up_part[16:17]


def in_plane(
    block_input,
    attn_gain,
    query_weight,
    key_weight,
    value_weight,
    gate_weight,
    decay_down,
    decay_up,
    decay_bias,
    head_gain,
    out_weight,
    ffn_gain,
    ffn_gate,
    ffn_up,
    ffn_down,
    cotangent,
):
    width = block_input.shape[2]
    ff_full = ffn_gate.shape[1]
    ffw = -(-ff_full // (CHIPS * TILE)) * TILE
    rank = decay_down.shape[1]

    scratch = scratch_of(width, ffw, 128)
    f32 = jax.ShapeDtypeStruct
    outs = pl.pallas_call(
        functools.partial(plane_kernel, tuple(scratch)),
        out_shape=[
            f32((ROWS, width), wide),
            f32((ROWS, width), wide),
            f32((32, width), wide),
            f32(*scratch["GFR"]),
            f32(*scratch["GAR"]),
            f32((8, width), wide),
            f32((24, HK), wide),
        ],
        in_specs=[pl.BlockSpec(memory_space=pltpu.VMEM)] * 8 + [pl.BlockSpec(memory_space=pl.ANY)] * 8,
        out_specs=[pl.BlockSpec(memory_space=pltpu.VMEM)] * 7,
        scratch_shapes=[pltpu.VMEM(shape, kind) for shape, kind in scratch.values()]
        + [
            pltpu.SemaphoreType.DMA((COPIES,)),
            pltpu.SemaphoreType.DMA((COPIES,)),
            pltpu.SemaphoreType.DMA((LOCALS,)),
        ],
        compiler_params=pltpu.CompilerParams(
            collective_id=0, has_side_effects=True, vmem_limit_bytes=62 * 1024 * 1024
        ),
        name="layer_step",
    )(
        decay_down.T,
        decay_up,
        attn_gain,
        ffn_gain,
        head_gain,
        decay_bias,
        block_input[0],
        cotangent[0],
        query_weight,
        key_weight,
        value_weight,
        gate_weight,
        out_weight,
        ffn_gate,
        ffn_up,
        ffn_down,
    )
    each = width // 32
    done = pl.pallas_call(
        finish_kernel,
        out_shape=[
            f32((ROWS, width), wide),
            f32((ROWS, width), wide),
            f32((1, each), wide),
            f32((32, CHIPS * HK), wide),
            f32((32, CHIPS * HK), wide),
            f32((32, CHIPS * HV), wide),
            f32((32, CHIPS * HV), wide),
            f32((rank, 32), wide),
            f32((rank, CHIPS * HK // 32), wide),
            f32((1, CHIPS * HK // 32), wide),
            f32((1, HV // 32), wide),
            f32((32, width), wide),
            f32((1, each), wide),
            f32((32, ff_full), wide),
            f32((32, ff_full), wide),
            f32((32, ff_full), wide),
        ],
        in_specs=[pl.BlockSpec(memory_space=pltpu.VMEM)] * 7,
        out_specs=[pl.BlockSpec(memory_space=pltpu.VMEM)] * 16,
        compiler_params=pltpu.CompilerParams(vmem_limit_bytes=62 * 1024 * 1024),
        name="results",
    )(*outs)
    shapes = {0: (1, ROWS, width), 1: (1, ROWS, width), 2: (-1,), 9: (-1,), 10: (-1,), 12: (-1,)}
    done = [v.reshape(shapes[i]) if i in shapes else v for i, v in enumerate(done)]
    done[7], done[15] = done[7].T, done[15].T
    return tuple(done)


def solution(mesh):
    one_plane = mesh.shape["seq"] == 2 * CHIPS and mesh.shape["fsdp"] == CHIPS
    return jax.shard_map(
        in_plane if one_plane else spread,
        mesh=mesh,
        in_specs=(
            P("fsdp", "seq", None),
            P("fsdp"),
            P("fsdp", None),
            P("fsdp", None),
            P("fsdp", None),
            P("fsdp", None),
            P("fsdp", None),
            P(None, "fsdp"),
            P("fsdp"),
            P("fsdp"),
            P("fsdp", None),
            P("fsdp"),
            P("fsdp", None),
            P("fsdp", None),
            P(None, "fsdp"),
            P("fsdp", "seq", None),
        ),
        out_specs=(
            P("fsdp", "seq", None),
            P("fsdp", "seq", None),
            P(("seq", "fsdp")),
            P(("seq", "fsdp"), None),
            P(("seq", "fsdp"), None),
            P(("seq", "fsdp"), None),
            P(("seq", "fsdp"), None),
            P(("seq", "fsdp"), None),
            P(None, ("seq", "fsdp")),
            P(("seq", "fsdp")),
            P(("seq", "fsdp")),
            P(("seq", "fsdp"), None),
            P(("seq", "fsdp")),
            P(("seq", "fsdp"), None),
            P(("seq", "fsdp"), None),
            P(None, ("seq", "fsdp")),
        ),
        check_vma=False,
    )
```
